128 devices in a mesh: shard: 64 (over z, x, y), rep: 2 (over core).
Axes of the slice: x: 4, y: 4, z: 4, core: 2. Of those that a mesh axis runs over, the one named last changes fastest.
Arguments:
- touched_ids: int32 [16384, 32], P(('shard', 'rep')), may hold values from 0 to 131071, as said below
- bag_lengths: int32 [16384, 4], P(('shard', 'rep')), may hold values from 1 to 24, 32 in all within a row
- train_map: int32 [131072], replicated, may hold values from 0 to 131071, as said below
- serve_map: int32 [131072], P('shard'), may hold values from 0 to 131071, as said below
- slot_grads: bfloat16 [16384, 32, 128], P(('shard', 'rep')), may hold values from -6 to 6
- table: float32 [131072, 128], P('shard'), may hold values from -6 to 6
- moment: float32 [131072, 128], P('shard'), may hold values from -4 to 4
- row_var: float32 [131072], P('shard'), may hold values from 0.01 to 1
- serving_old: bfloat16 [131072, 128], P('shard'), may hold values from -6 to 6
- w_first: bfloat16 [512, 1024], replicated, may hold values from -0.25 to 0.25
- w_second: bfloat16 [1024, 1024], replicated, may hold values from -0.1875 to 0.1875
- w_score: bfloat16 [1024], replicated, may hold values from -0.1875 to 0.1875
Outputs:
- new_table: float32 [131072, 128], P('shard')
- new_moment: float32 [131072, 128], P('shard')
- new_var: float32 [131072], P('shard')
- serving_table: bfloat16 [131072, 128], P('shard')
- scores: float32 [16384], P(('shard', 'rep'))
The draws below stay inside these ranges and needn't reach their ends.
Inputs may be any that keep to these rules, and one draw needn't show every extreme that they name: `touched_ids`: of the 4096 ids of one device's samples at most 256 have their training position in one owner's range of 2048 positions; 4 owners receive exactly 256 from every device. `train_map`: A permutation of the row ids; the owner of a row is its position // 2048. `serve_map`: A permutation; the row at training position j * 2048 + s has its serving position in the range of serving owner s % 64.
All inputs are finite; a program needn't handle non-finite values.
Results may differ from the reference program's by a relative error of at most 0.008.
Values may be sent and summed in bfloat16 or wider, within the bound.
No kernel may reach another device: no remote copies, remote signals or barrier semaphores. Data moves between devices by JAX's collectives and lax.ppermute only.
A program may use at most 256 MiB of HBM per device.

```python
import math
import jax
import jax.numpy as jnp
import numpy as np
from jax import lax

E = 128
HID = 1024
FIELDS = 4
BAG = 32
HOT = 4
B_DEV = 128
TAB_DEV = 2048
MOST = 24
OWNERS = 64
ROWS = 131072
BATCH = 16384
SLOTS = 4096
CAP = 256
BLK = 32
IN = 512


def shared_positions(key):
    return jax.random.permutation(jax.random.fold_in(key, 11), ROWS).astype(jnp.int32)


def draw_train_map(key, part):
    return shared_positions(key)


def draw_touched_ids(key, part):
    positions = shared_positions(key)
    inverse = jnp.zeros((ROWS,), jnp.int32).at[positions].set(jnp.arange(ROWS, dtype=jnp.int32))
    devices = BATCH // B_DEV
    hot_owners = jax.random.permutation(jax.random.fold_in(key, 12), OWNERS)[:HOT].astype(jnp.int32)
    hot_rank = jnp.full((OWNERS,), -1, jnp.int32).at[hot_owners].set(jnp.arange(HOT, dtype=jnp.int32))
    device_keys = jax.random.split(jax.random.fold_in(key, 13), devices)
    orders = jax.vmap(lambda one_key: jax.random.permutation(one_key, OWNERS))(device_keys).astype(jnp.int32)
    device_rows = jnp.arange(devices, dtype=jnp.int32)[:, None]
    places = jnp.zeros((devices, OWNERS), jnp.int32).at[device_rows, orders].set(jnp.arange(OWNERS, dtype=jnp.int32)[None, :])
    ranking = jnp.where(hot_rank[None, :] >= 0, hot_rank[None, :], HOT + places)
    by_rank = jnp.argsort(ranking, axis=1, stable=True).astype(jnp.int32)
    remain = SLOTS - HOT * CAP
    colder = OWNERS - HOT
    owner_ranks = jnp.arange(OWNERS, dtype=jnp.int32)
    counts = jnp.where(owner_ranks < HOT, CAP, remain // colder + (owner_ranks - HOT < remain % colder).astype(jnp.int32))
    count_ends = jnp.cumsum(counts)
    slot_rank = jnp.sum((jnp.arange(SLOTS, dtype=jnp.int32)[:, None] >= count_ends[None, :]).astype(jnp.int32), axis=1)
    sorted_owner = by_rank[:, slot_rank]
    shuffle_keys = jax.random.split(jax.random.fold_in(key, 14), devices)
    shuffles = jax.vmap(lambda one_key: jax.random.permutation(one_key, SLOTS))(shuffle_keys).astype(jnp.int32)
    owner_of = jnp.take_along_axis(sorted_owner, shuffles, axis=1)
    limits = jax.random.randint(jax.random.fold_in(key, 15), (devices, SLOTS), 1, TAB_DEV + 1)
    row_in_owner = jax.random.randint(jax.random.fold_in(key, 16), (devices, SLOTS), 0, limits)
    picked = inverse[owner_of * TAB_DEV + row_in_owner]
    return picked.reshape(BATCH, BAG).astype(jnp.int32)


def draw_serve_map(key, part):
    owner_keys = jax.random.split(jax.random.fold_in(key, 21), OWNERS)
    shuffles = jax.vmap(lambda one_key: jax.random.permutation(one_key, TAB_DEV))(owner_keys).astype(jnp.int32)
    spots = jnp.arange(ROWS, dtype=jnp.int32)
    holder = spots // TAB_DEV
    within = spots % TAB_DEV
    server = within % OWNERS
    stride = within // OWNERS
    return (server * TAB_DEV + shuffles[server, holder * BLK + stride]).astype(jnp.int32)


def block_levels(key, extent, shards, least, top_value):
    factor_of, own = 1.0, jax.random.fold_in(key, 6)
    for dim, blocks in shards:
        steps = jnp.exp(jax.random.uniform(jax.random.fold_in(own, dim), (blocks,), jnp.float32, least / len(shards), top_value / len(shards)))
        factor_of = factor_of * jnp.repeat(steps, extent[dim] // blocks).reshape([-1 if axis == dim else 1 for axis in range(len(extent))])
    return factor_of


def split_up(count, total, bound, slope):
    loads = [(1 << 20) // math.isqrt(grade ** slope) + 1 for grade in range(2, count + 1)]
    rest, given = total - bound - (count - 1), [1] * (count - 1)
    while rest > 0:
        free = [i for i in range(count - 1) if given[i] < bound]
        pool, remaining = sum([loads[i] for i in free]), rest
        for i in free:
            extra = min(bound - given[i], max(1, remaining * loads[i] // pool), rest)
            given[i] = given[i] + extra
            rest = rest - extra
    return np.array([bound] + given)


def uneven(stream_key, count, total, most, slope):
    if count == 2:
        one = jax.random.randint(stream_key, (), max(1, total - most), min(most, total - 1) + 1)
        return jnp.stack([one, total - one])
    tallies = jnp.asarray(split_up(count, total, most, slope), jnp.int32)
    twos = (count - 1) // 2
    giver, sink = tallies[1:1 + 2 * twos:2], tallies[2:2 + 2 * twos:2]
    room = jnp.minimum(giver - 1, most - sink)
    shifted = jax.random.randint(jax.random.fold_in(stream_key, 1), (twos,), 0, 1 << 20) % (room + 1)
    tallies = tallies.at[1:1 + 2 * twos:2].set(giver - shifted).at[2:2 + 2 * twos:2].set(sink + shifted)
    return tallies[jax.random.permutation(jax.random.fold_in(stream_key, 2), count)]


def normal_values(rng, extent, scale, reach, pieces=(), held_as=jnp.bfloat16):
    result = jax.random.normal(rng, extent, jnp.float32) * scale
    if len(pieces) > 0:
        result = block_levels(rng, extent, pieces, -0.22, 0.18) * result
    return jnp.clip(result, min=-reach, max=reach).astype(held_as)


def setup_inputs(seed: int = 0) -> dict:
    streams_of = jax.random.split(jax.random.key(seed), 13)
    touched_ids = draw_touched_ids(jax.random.fold_in(streams_of[12], 71), 0)
    bag_lengths = jax.vmap(lambda own: uneven(own, FIELDS, BAG, MOST, 2))(jax.random.split(streams_of[1], BATCH)).reshape((BATCH, FIELDS)).astype(jnp.int32)
    train_map = draw_train_map(jax.random.fold_in(streams_of[12], 71), 0)
    serve_map = draw_serve_map(jax.random.fold_in(streams_of[12], 71), 0)
    slot_grads = normal_values(streams_of[4], (BATCH, BAG, E), 1.0, 6.0, ((0, 128),))
    table = normal_values(streams_of[5], (ROWS, E), 1.0, 6.0, ((0, 64),), jnp.float32)
    moment = normal_values(streams_of[6], (ROWS, E), 0.3, 4.0, ((0, 64),), jnp.float32)
    row_var = jnp.clip(jnp.exp(math.log(1.0) - 4.6051702 * jax.random.uniform(streams_of[7], (ROWS,), jnp.float32) ** block_levels(streams_of[7], (ROWS,), ((0, 64),), -0.2, 0.2)), 0.01, 1.0)
    serving_old = normal_values(streams_of[8], (ROWS, E), 1.0, 6.0, ((0, 64),))
    w_first = normal_values(streams_of[9], (IN, HID), IN ** -0.5, 0.25)
    w_second = normal_values(streams_of[10], (HID, HID), HID ** -0.5, 0.1875)
    w_score = normal_values(streams_of[11], (HID,), HID ** -0.5, 0.1875)
    return {"touched_ids": touched_ids, "bag_lengths": bag_lengths, "train_map": train_map, "serve_map": serve_map, "slot_grads": slot_grads, "table": table, "moment": moment, "row_var": row_var, "serving_old": serving_old, "w_first": w_first, "w_second": w_second, "w_score": w_score}


beta_one = 0.9
beta_two = 0.999
learn_rate = 0.1
epsilon = 1e-06

def reference(touched_ids, bag_lengths, train_map, serve_map, slot_grads, table, moment, row_var, serving_old, w_first, w_second, w_score):
    position = train_map[touched_ids]
    flat_pos = position.reshape(-1)
    grads = slot_grads.reshape(-1, E).astype(jnp.float32)
    grad_sum = jnp.zeros((ROWS, E), jnp.float32).at[flat_pos].add(grads)
    touches = jnp.zeros((ROWS,), jnp.float32).at[flat_pos].add(jnp.ones(flat_pos.shape, jnp.float32))
    touched = touches > 0.0
    new_moment = jnp.where(touched[:, None], beta_one * moment + (1.0 - beta_one) * grad_sum, moment)
    new_var = jnp.where(touched, beta_two * row_var + (1.0 - beta_two) * lax.optimization_barrier(jnp.mean(grad_sum * grad_sum, axis=1)), row_var)
    new_table = jnp.where(touched[:, None], table - learn_rate * new_moment / (jnp.sqrt(new_var)[:, None] + epsilon), table)
    rounded = new_table.astype(jnp.bfloat16)
    targets = jnp.where(touched, serve_map, ROWS).astype(jnp.int32)
    serving_table = serving_old.at[targets].set(rounded, mode='drop')
    looked = rounded[position].astype(jnp.float32)
    ends = jnp.cumsum(bag_lengths, axis=1)
    starts = ends - bag_lengths
    slot_pos = jnp.arange(BAG, dtype=jnp.int32)
    member = ((slot_pos[None, None, :] >= starts[:, :, None]) & (slot_pos[None, None, :] < ends[:, :, None])).astype(jnp.float32)
    pooled = jnp.einsum('bft,bte->bfe', member, looked, precision=lax.Precision.HIGHEST)
    features = pooled.reshape(BATCH, FIELDS * E).astype(jnp.bfloat16)
    hidden_one = jax.nn.relu(jnp.dot(features, w_first, preferred_element_type=jnp.float32)).astype(jnp.bfloat16)
    hidden_two = jax.nn.relu(jnp.dot(hidden_one, w_second, preferred_element_type=jnp.float32)).astype(jnp.bfloat16)
    scores = jnp.dot(hidden_two, w_score, preferred_element_type=jnp.float32)
    return (new_table, new_moment, new_var, serving_table, scores)
```

```python
import functools

import jax
import jax.numpy as jnp
from jax import lax
from jax.experimental import pallas as pl
from jax.experimental.pallas import tpu as pltpu
from jax.sharding import PartitionSpec as P

beta_one = 0.9
beta_two = 0.999
learn_rate = 0.1
epsilon = 1e-06

ROUND = 64
DEVS = 128
LANES = 128
UNTOUCHED = 1e30
F32 = jnp.float32
BF16 = jnp.bfloat16
I32 = jnp.int32
ALL = ("shard", "rep")


def iota(shape, dim):
    return lax.broadcasted_iota(I32, shape, dim)


def one_hot(mask):
    return jnp.where(mask, 1.0, 0.0).astype(BF16)


def route_kernel(round_ref, ids_ref, map_ref, extra_ref, slots_ref, keys_ref, row_ref):
    bag, samples = ids_ref.shape[0] - 4, ids_ref.shape[1]
    step = 4
    wide = step * samples
    first = round_ref[0] * ROUND
    table = map_ref[...]
    high = (table >> 9).astype(F32).T
    low = ((table & 511) - 256).astype(F32).T
    parts = jnp.concatenate([high, low], axis=0).astype(BF16)
    upto = one_hot(iota((wide, wide), 0) <= iota((wide, wide), 1))
    ends = []
    total = jnp.zeros((1, samples), I32)
    for f in range(3):
        total = total + ids_ref[bag + f : bag + f + 1, :]
        ends.append(total)
    sample = iota((1, samples), 1)
    seen = jnp.zeros((DEVS, 1), F32)
    layout = jnp.zeros((DEVS, 4 * ROUND), F32)
    for t in range(0, bag, step):
        ids = jnp.concatenate([ids_ref[t + u : t + u + 1, :] for u in range(step)], axis=1)
        keys = []
        for u in range(step):
            field = sum((jnp.where(e <= t + u, 1, 0) for e in ends), jnp.zeros((1, samples), I32))
            keys.append(field * samples + sample)
        key = jnp.concatenate(keys, axis=1) + 1
        hit = one_hot(iota((table.shape[0], wide), 0) == (ids >> 7))
        both = jnp.dot(parts, hit, preferred_element_type=F32)
        value = both[:LANES] * 512.0 + both[LANES:] + 256.0
        value = jnp.where(iota((LANES, wide), 0) == (ids & 127), value, 0.0)
        position = jnp.sum(value, axis=0, keepdims=True).astype(I32)
        owner = position >> 11
        stride = (position >> 6) & 31
        dest = (position & 63) * 2 + ((stride + owner) & 1)
        local = owner * 16 + (stride >> 1) + 1
        mine = iota((DEVS, wide), 0) == dest
        hot = one_hot(mine)
        running = jnp.dot(hot, upto, preferred_element_type=F32)
        rank = jnp.sum(jnp.where(mine, running + seen, 0.0), axis=0, keepdims=True)
        seen = seen + running[:, wide - 1 : wide]
        rank = rank.astype(I32) - 1 - first
        here = iota((ROUND, wide), 0) == rank
        columns = jnp.concatenate(
            [
                jnp.where(here, v.astype(F32), 0.0)
                for v in (local >> 5, key >> 5, local & 31, key & 31)
            ],
            axis=0,
        ).astype(BF16)
        layout = layout + lax.dot_general(
            hot, columns, (((1,), (1,)), ((), ())), preferred_element_type=F32
        )
        fits = (rank >= 0) & (rank < ROUND)
        slot = jnp.where(fits, dest * ROUND + rank, DEVS * ROUND)
        for u in range(step):
            slots_ref[t + u : t + u + 1, :] = slot[:, u * samples : (u + 1) * samples]
    layout = layout[:, :LANES] * 32.0 + layout[:, LANES:] - 1.0
    keys_ref[...] = layout
    most = jnp.max(seen, axis=0, keepdims=True)
    line = jnp.where(iota((DEVS, LANES), 1) < ROUND, layout, extra_ref[...])
    row_ref[:, 0:1, :] = line.reshape(DEVS, 1, LANES)
    row_ref[:, 1:8, :] = jnp.broadcast_to(most.reshape(1, 1, 1), (DEVS, 7, LANES))


def route(round_index, ids, train_map, extra):
    bag = ids.shape[0] - 4
    return pl.pallas_call(
        route_kernel,
        in_specs=[pl.BlockSpec(memory_space=pltpu.SMEM)]
        + [pl.BlockSpec(memory_space=pltpu.VMEM)] * 3,
        out_specs=[pl.BlockSpec(memory_space=pltpu.VMEM)] * 3,
        out_shape=(
            jax.ShapeDtypeStruct((bag, ids.shape[1]), I32),
            jax.ShapeDtypeStruct((DEVS, LANES), F32),
            jax.ShapeDtypeStruct((DEVS, 8, LANES), F32),
        ),
        name="route",
    )(round_index, ids, train_map, extra)


def pack_kernel(slots_ref, grads_ref, out_ref, from_ref, to_ref):
    bag, samples = slots_ref.shape
    block = 512

    def widen(i, carry):
        at = pl.multiple_of(i * block, block)
        from_ref[pl.ds(at, block), :] = grads_ref[pl.ds(at, block), :].astype(F32)
        return carry

    def clear(i, carry):
        at = pl.multiple_of(i * block, block)
        to_ref[pl.ds(at, block), :] = jnp.zeros((block, LANES), F32)
        return carry

    def move(b, carry):
        for t in range(bag):
            to_ref[pl.ds(slots_ref[t, b], 1), :] = from_ref[pl.ds(b * bag + t, 1), :]
        return carry

    def narrow(i, carry):
        at = pl.multiple_of(i * block, block)
        out_ref[pl.ds(at, block), :] = to_ref[pl.ds(at, block), :].astype(BF16)
        return carry

    lax.fori_loop(0, bag * samples // block, widen, 0)
    lax.fori_loop(0, DEVS * ROUND // block, clear, 0)
    lax.fori_loop(0, samples, move, 0)
    lax.fori_loop(0, DEVS * ROUND // block, narrow, 0)


def pack(slots, grads):
    return pl.pallas_call(
        pack_kernel,
        in_specs=[
            pl.BlockSpec(memory_space=pltpu.SMEM),
            pl.BlockSpec(memory_space=pltpu.VMEM),
        ],
        out_specs=pl.BlockSpec(memory_space=pltpu.VMEM),
        out_shape=jax.ShapeDtypeStruct((DEVS * ROUND, LANES), BF16),
        scratch_shapes=[
            pltpu.VMEM(grads.shape, F32),
            pltpu.VMEM((DEVS * ROUND + 8, LANES), F32),
        ],
        name="pack",
    )(slots, grads)


def pair_up(line, low):
    other = pltpu.roll(line, ROUND, 1)
    half = DEVS // 2
    left = (line if low else other)[:half]
    right = (other if low else line)[half:]
    return jnp.where(iota((half, LANES), 1) < ROUND, left, right)


def pair_rows(ref, i):
    half = DEVS // 2
    left = ref[pl.ds(i * 8, 8)]
    right = ref[pl.ds(half + i * 8, 8)]
    pieces = []
    for u in range(8):
        pieces += [left[u], right[u]]
    return jnp.concatenate(pieces, axis=0)


def lanes_of(index_ref, i):
    rows = index_ref[pl.ds(pl.multiple_of(i * 8, 8), 8), :]
    return jnp.concatenate([rows[u : u + 1] for u in range(8)], axis=1)


def add_rows(index_ref, rows_ref, acc_ref, with_count):
    width = 8 * LANES

    def add(i, carry):
        hit = one_hot(iota((acc_ref.shape[0], width), 0) == lanes_of(index_ref, i))
        rows = pair_rows(rows_ref, i)
        if with_count:
            rows = jnp.concatenate([rows, jnp.ones_like(rows)], axis=1)
        acc_ref[...] = acc_ref[...] + jnp.dot(hit, rows, preferred_element_type=F32)
        return carry

    lax.fori_loop(0, DEVS * ROUND // width, add, 0)


def sum_kernel(line_ref, rows_ref, start_ref, out_ref, index_ref, *, low, with_count):
    index_ref[...] = pair_up(line_ref[...], low).astype(I32)
    out_ref[...] = start_ref[...]
    add_rows(index_ref, rows_ref, out_ref, with_count)


def sum_rows(line, rows, start, low, with_count):
    return pl.pallas_call(
        functools.partial(sum_kernel, low=low, with_count=with_count),
        in_specs=[pl.BlockSpec(memory_space=pltpu.VMEM)] * 3,
        out_specs=pl.BlockSpec(memory_space=pltpu.VMEM),
        out_shape=jax.ShapeDtypeStruct(start.shape, F32),
        scratch_shapes=[pltpu.VMEM((DEVS // 2, LANES), I32)],
        name="sum_rows",
    )(line, rows, start)


def update_kernel(
    core_ref, state_ref, rows_ref, start_ref, new_ref, sums_ref, spots_ref, index_ref, acc_ref
):
    index_ref[...] = pair_up(state_ref[:, 16:17, :].reshape(DEVS, LANES), True).astype(I32)
    acc_ref[...] = start_ref[...]
    add_rows(index_ref, rows_ref, acc_ref, True)
    core = core_ref[0]

    def step(i, carry):
        at = pl.multiple_of(i * LANES, LANES)
        part = pl.ds(i * 16, 16)
        total = acc_ref[pl.ds(at, LANES), :]
        grad = total[:, :LANES].reshape(16, 8, LANES)
        touched = (total[:, LANES:] > 0.5).reshape(16, 8, LANES)
        shape = (16, 8, LANES)
        source = iota(shape, 0)
        within = iota(shape, 1)
        lane = iota(shape, 2)
        parity = (core + i * 8 + (source >> 1)) & 1
        own = (source & 1) * 16 + within * 2 + parity
        extra = jnp.broadcast_to(state_ref[part, 16:17, :], shape)
        var = jnp.sum(jnp.where(lane == ROUND + own, extra, 0.0), axis=2, keepdims=True)
        spot = jnp.sum(jnp.where(lane == ROUND + 32 + own, extra, 0.0), axis=2, keepdims=True)
        table = state_ref[part, 0:8, :]
        moment = state_ref[part, 8:16, :]
        mean = jnp.sum(grad * grad, axis=2, keepdims=True) * (1.0 / LANES)
        new_var = beta_two * var + (1.0 - beta_two) * mean
        new_moment = beta_one * moment + (1.0 - beta_one) * grad
        new_table = table - learn_rate * new_moment / (jnp.sqrt(new_var) + epsilon)
        new_table = jnp.where(touched, new_table, table)
        new_ref[pl.ds(at, LANES), :] = new_table.reshape(LANES, LANES).astype(BF16)
        sums_ref[part] = jnp.where(touched, grad, UNTOUCHED)
        spot = jnp.where(touched & (lane == within), spot, 0.0)
        away = jnp.where(touched | (lane != within), 0.0, 4096.0)
        spots_ref[pl.ds(pl.multiple_of(i * 16, 16), 16), :] = jnp.sum(spot + away, axis=1)
        return carry

    lax.fori_loop(0, 8, step, 0)


def update(core, state, rows, start):
    return pl.pallas_call(
        update_kernel,
        in_specs=[pl.BlockSpec(memory_space=pltpu.SMEM)]
        + [pl.BlockSpec(memory_space=pltpu.VMEM)] * 3,
        out_specs=[pl.BlockSpec(memory_space=pltpu.VMEM)] * 3,
        out_shape=(
            jax.ShapeDtypeStruct((start.shape[0], LANES), BF16),
            jax.ShapeDtypeStruct((DEVS, 8, LANES), F32),
            jax.ShapeDtypeStruct((DEVS, LANES), F32),
        ),
        scratch_shapes=[
            pltpu.VMEM((DEVS // 2, LANES), I32),
            pltpu.VMEM(start.shape, F32),
        ],
        name="update",
    )(core, state, rows, start)


def reply_kernel(line_ref, new_ref, out_ref, turned_ref):
    turned_ref[...] = line_ref[...].T
    rows = new_ref.shape[0]

    def look(i, carry):
        turned = pltpu.roll(turned_ref[0:ROUND, :], LANES - i * 8, 1).astype(I32)
        hit = jnp.concatenate(
            [one_hot(iota((ROUND, rows), 1) == turned[:, u : u + 1]) for u in range(8)], axis=0
        )
        found = jnp.dot(hit, new_ref[...], preferred_element_type=F32)
        at = pl.multiple_of(i * 8 * ROUND, 8 * ROUND)
        out_ref[pl.ds(at, 8 * ROUND), :] = found.astype(BF16)
        return carry

    lax.fori_loop(0, DEVS // 8, look, 0)


def reply(line, new_rows):
    return pl.pallas_call(
        reply_kernel,
        in_specs=[pl.BlockSpec(memory_space=pltpu.VMEM)] * 2,
        out_specs=pl.BlockSpec(memory_space=pltpu.VMEM),
        out_shape=jax.ShapeDtypeStruct((DEVS * ROUND, LANES), BF16),
        scratch_shapes=[pltpu.VMEM((DEVS, LANES), F32)],
        name="reply",
    )(line, new_rows)


def score_kernel(
    keys_ref, rows_ref, start_ref, first_ref, second_ref, score_ref, out_ref, index_ref, acc_ref
):
    index_ref[...] = pair_up(keys_ref[...], False).astype(I32)
    acc_ref[...] = start_ref[...]
    add_rows(index_ref, rows_ref, acc_ref, False)
    samples = out_ref.shape[1]
    pooled = jnp.concatenate(
        [acc_ref[f * samples : (f + 1) * samples, :] for f in range(4)], axis=1
    ).astype(BF16)
    hidden = jnp.dot(pooled, first_ref[...], preferred_element_type=F32)
    hidden = jnp.maximum(hidden, 0.0).astype(BF16)
    hidden = jnp.dot(hidden, second_ref[...], preferred_element_type=F32)
    hidden = jnp.maximum(hidden, 0.0).astype(BF16)
    weights = jnp.broadcast_to(score_ref[...], (16, score_ref.shape[1]))
    scores = lax.dot_general(
        weights, hidden, (((1,), (1,)), ((), ())), preferred_element_type=F32
    )
    out_ref[...] = scores[0:1, :]


def score(keys, rows, start, w_first, w_second, w_score):
    return pl.pallas_call(
        score_kernel,
        in_specs=[pl.BlockSpec(memory_space=pltpu.VMEM)] * 6,
        out_specs=pl.BlockSpec(memory_space=pltpu.VMEM),
        out_shape=jax.ShapeDtypeStruct((1, start.shape[0] // 4), F32),
        scratch_shapes=[
            pltpu.VMEM((DEVS // 2, LANES), I32),
            pltpu.VMEM(start.shape, F32),
        ],
        name="score",
    )(keys, rows, start, w_first, w_second, w_score)


def exchange(value, width):
    out = lax.all_to_all(value.reshape(DEVS, -1, width), ALL, 0, 0, tiled=True)
    return out


def place_rows(serving_old, slot_index, rows_in):
    tab_rows, row_width = serving_old.shape
    block = 512
    old_blocks = serving_old.reshape(tab_rows // block, block, row_width)
    firsts = jnp.arange(tab_rows // block, dtype=jnp.int32) * block

    def place_block(pieces):
        old_piece, first = pieces
        wanted = first + jnp.arange(block, dtype=jnp.int32)
        hit = (wanted[:, None] == slot_index[None, :]).astype(jnp.bfloat16)
        fresh = jnp.dot(hit, rows_in, preferred_element_type=jnp.float32)
        found = jnp.sum(hit.astype(jnp.float32), axis=1) > 0.5
        return jnp.where(found[:, None], fresh.astype(jnp.bfloat16), old_piece)

    return lax.map(place_block, (old_blocks, firsts)).reshape(tab_rows, row_width)


def per_device(
    touched_ids,
    bag_lengths,
    train_map,
    serve_map,
    slot_grads,
    table,
    moment,
    row_var,
    serving_old,
    w_first,
    w_second,
    w_score,
):
    owners = lax.axis_size("shard")
    owner = lax.axis_index("shard")
    rep = lax.axis_index("rep")
    tab_rows, row_width = table.shape
    samples, bag = touched_ids.shape
    swap = [(0, 1), (1, 0)]
    odd = owner % 2 == 1
    rows_here = tab_rows // 2

    ids = jnp.concatenate([touched_ids, bag_lengths], axis=1).T
    map_rows = train_map.reshape(-1, LANES)
    grads = slot_grads.reshape(samples * bag, row_width)

    def outgoing(value):
        half = lax.dynamic_slice_in_dim(value, rep * rows_here, rows_here, 0)
        half = half.reshape(8, 2, owners, row_width)
        half = jnp.where(odd, half[:, ::-1], half)
        return half.transpose(2, 1, 0, 3).reshape(DEVS, 8, row_width)

    spots = (serve_map % tab_rows).astype(F32).reshape(tab_rows // owners, owners).T
    spread = jnp.concatenate([row_var.reshape(tab_rows // owners, owners).T, spots], axis=1)
    spread = jnp.broadcast_to(spread[:, None, :], (owners, 2, 2 * tab_rows // owners))
    extra = jnp.concatenate([jnp.zeros((DEVS, ROUND), F32), spread.reshape(DEVS, -1)], axis=1)

    slots, keys, head = route(jnp.zeros((1,), I32), ids, map_rows, extra)
    state = jnp.concatenate([outgoing(table), outgoing(moment), head], axis=1)
    state = exchange(state, row_width)
    received = exchange(pack(slots, grads), row_width)
    state, received = lax.optimization_barrier((state, received))
    rounds = (jnp.max(state[:, 17, 0]).astype(I32) + ROUND - 1) // ROUND

    def more_sums(carry):
        k, acc = carry
        slots, _, head = route(k.reshape(1), ids, map_rows, extra)
        line = exchange(head, row_width)[:, 0, :]
        got = exchange(pack(slots, grads), row_width)
        return (k + 1, sum_rows(line, got, acc, True, True))

    one = jnp.ones((), I32)
    _, start = lax.while_loop(
        lambda c: c[0] < rounds,
        more_sums,
        (one, jnp.zeros((rows_here, 2 * row_width), F32)),
    )
    new_rows, sums, places = update(rep.reshape(1).astype(I32), state, received, start)

    back = exchange(sums, row_width)
    answer = exchange(reply(state[:, 16, :], new_rows), row_width)

    other_rows = lax.ppermute(new_rows, "rep", swap)
    places = places[:, :8].reshape(-1).astype(I32)
    other_places = lax.ppermute(places, "rep", swap)
    serving_table = place_rows(
        serving_old,
        jnp.concatenate([places, other_places]),
        jnp.concatenate([new_rows, other_rows]),
    )

    back = back.reshape(owners, 2, 8, row_width)
    back = jnp.where(odd, back[:, ::-1], back)
    half = back.transpose(2, 1, 0, 3).reshape(rows_here, row_width)
    other = lax.ppermute(half, "rep", swap)
    grad_sum = jnp.where(
        rep == 0, jnp.concatenate([half, other]), jnp.concatenate([other, half])
    )
    touched = grad_sum[:, :1] < 0.5 * UNTOUCHED
    new_moment = jnp.where(touched, beta_one * moment + (1.0 - beta_one) * grad_sum, moment)
    mean = jnp.mean(jnp.where(touched, grad_sum * grad_sum, 0.0), axis=1)
    new_var = jnp.where(touched[:, 0], beta_two * row_var + (1.0 - beta_two) * mean, row_var)
    new_table = jnp.where(
        touched, table - learn_rate * new_moment / (jnp.sqrt(new_var)[:, None] + epsilon), table
    )

    def more_pooled(carry):
        k, acc = carry
        _, keys, head = route(k.reshape(1), ids, map_rows, extra)
        line = exchange(head, row_width)[:, 0, :]
        got = exchange(reply(line, new_rows), row_width)
        return (k + 1, sum_rows(keys, got, acc, False, False))

    answer, rounds = lax.optimization_barrier((answer, rounds))
    _, pooled = lax.while_loop(
        lambda c: c[0] < rounds,
        more_pooled,
        (one, jnp.zeros((4 * samples, row_width), F32)),
    )
    scores = score(keys, answer, pooled, w_first, w_second, w_score.reshape(1, -1))
    return (new_table, new_moment, new_var, serving_table, scores.reshape(samples))


def solution(mesh):
    in_specs = (
        P(("shard", "rep"), None),
        P(("shard", "rep"), None),
        P(),
        P("shard"),
        P(("shard", "rep"), None, None),
        P("shard", None),
        P("shard", None),
        P("shard"),
        P("shard", None),
        P(),
        P(),
        P(),
    )
    out_specs = (
        P("shard", None),
        P("shard", None),
        P("shard"),
        P("shard", None),
        P(("shard", "rep")),
    )
    return jax.shard_map(
        per_device, mesh=mesh, in_specs=in_specs, out_specs=out_specs, check_vma=False
    )
```

```python
import functools

import jax
import jax.numpy as jnp
from jax import lax
from jax.experimental import pallas as pl
from jax.experimental.pallas import tpu as pltpu
from jax.sharding import PartitionSpec as P

beta_one = 0.9
beta_two = 0.999
learn_rate = 0.1
epsilon = 1e-06

ROUND = 64
DEVS = 128
LANES = 128
UNTOUCHED = 1e30
F32 = jnp.float32
BF16 = jnp.bfloat16
I32 = jnp.int32
ALL = ("shard", "rep")
SENT = ROUND + 32


def iota(shape, dim):
    return lax.broadcasted_iota(I32, shape, dim)


def one_hot(mask):
    return jnp.where(mask, 1.0, 0.0).astype(BF16)


def route_kernel(round_ref, ids_ref, map_ref, extra_ref, slots_ref, keys_ref, row_ref):
    bag, samples = ids_ref.shape[0] - 4, ids_ref.shape[1]
    step = 4
    wide = step * samples
    first = round_ref[0] * ROUND
    table = map_ref[...]
    high = (table >> 9).astype(F32).T
    low = ((table & 511) - 256).astype(F32).T
    parts = jnp.concatenate([high, low], axis=0).astype(BF16)
    upto = one_hot(iota((wide, wide), 0) <= iota((wide, wide), 1))
    ends = []
    total = jnp.zeros((1, samples), I32)
    for f in range(3):
        total = total + ids_ref[bag + f : bag + f + 1, :]
        ends.append(total)
    sample = iota((1, samples), 1)
    seen = jnp.zeros((DEVS, 1), F32)
    layout = jnp.zeros((DEVS, 4 * ROUND), F32)
    for t in range(0, bag, step):
        ids = jnp.concatenate([ids_ref[t + u : t + u + 1, :] for u in range(step)], axis=1)
        keys = []
        for u in range(step):
            field = sum((jnp.where(e <= t + u, 1, 0) for e in ends), jnp.zeros((1, samples), I32))
            keys.append(field * samples + sample)
        key = jnp.concatenate(keys, axis=1) + 1
        hit = one_hot(iota((table.shape[0], wide), 0) == (ids >> 7))
        both = jnp.dot(parts, hit, preferred_element_type=F32)
        value = both[:LANES] * 512.0 + both[LANES:] + 256.0
        value = jnp.where(iota((LANES, wide), 0) == (ids & 127), value, 0.0)
        position = jnp.sum(value, axis=0, keepdims=True).astype(I32)
        owner = position >> 11
        stride = (position >> 6) & 31
        dest = (position & 63) * 2 + ((stride + owner) & 1)
        local = owner * 16 + (stride >> 1) + 1
        mine = iota((DEVS, wide), 0) == dest
        hot = one_hot(mine)
        running = jnp.dot(hot, upto, preferred_element_type=F32)
        rank = jnp.sum(jnp.where(mine, running + seen, 0.0), axis=0, keepdims=True)
        seen = seen + running[:, wide - 1 : wide]
        rank = rank.astype(I32) - 1 - first
        here = iota((ROUND, wide), 0) == rank
        columns = jnp.concatenate(
            [
                jnp.where(here, v.astype(F32), 0.0)
                for v in (local >> 5, key >> 5, local & 31, key & 31)
            ],
            axis=0,
        ).astype(BF16)
        layout = layout + lax.dot_general(
            hot, columns, (((1,), (1,)), ((), ())), preferred_element_type=F32
        )
        fits = (rank >= 0) & (rank < ROUND)
        slot = jnp.where(fits, dest * ROUND + rank, DEVS * ROUND)
        for u in range(step):
            slots_ref[t + u : t + u + 1, :] = slot[:, u * samples : (u + 1) * samples]
    keys_ref[...] = layout[:, :LANES] * 32.0 + layout[:, LANES:] - 1.0
    most = jnp.max(seen, axis=0, keepdims=True).astype(I32)
    rounds = ((most + ROUND - 1) // ROUND).astype(F32)
    extra = extra_ref[...]
    coarse = extra.astype(BF16).astype(F32)
    index = iota((DEVS, LANES), 1) < ROUND
    high = jnp.where(index, layout[:, :LANES], coarse)
    low = jnp.where(index, layout[:, LANES:], extra - coarse)
    row_ref[:, 0:1, :] = high.reshape(DEVS, 1, LANES)
    row_ref[:, 1:2, :] = low.reshape(DEVS, 1, LANES)
    row_ref[:, 2:8, :] = jnp.broadcast_to(rounds.reshape(1, 1, 1), (DEVS, 6, LANES))


def route(round_index, ids, train_map, extra):
    bag = ids.shape[0] - 4
    return pl.pallas_call(
        route_kernel,
        in_specs=[pl.BlockSpec(memory_space=pltpu.SMEM)]
        + [pl.BlockSpec(memory_space=pltpu.VMEM)] * 3,
        out_specs=[pl.BlockSpec(memory_space=pltpu.VMEM)] * 3,
        out_shape=(
            jax.ShapeDtypeStruct((bag, ids.shape[1]), I32),
            jax.ShapeDtypeStruct((DEVS, LANES), F32),
            jax.ShapeDtypeStruct((DEVS, 8, LANES), F32),
        ),
        name="route",
    )(round_index, ids, train_map, extra)


def pack_kernel(slots_ref, grads_ref, table_ref, moment_ref, head_ref, out_ref, from_ref, to_ref):
    bag, samples = slots_ref.shape
    block = 512

    def widen(i, carry):
        at = pl.multiple_of(i * block, block)
        from_ref[pl.ds(at, block), :] = grads_ref[pl.ds(at, block), :].astype(F32)
        to_ref[pl.ds(at * 2, block), :] = jnp.zeros((block, LANES), F32)
        to_ref[pl.ds(at * 2 + block, block), :] = jnp.zeros((block, LANES), F32)
        return carry

    def move(b, carry):
        for t in range(bag):
            to_ref[pl.ds(slots_ref[t, b], 1), :] = from_ref[pl.ds(b * bag + t, 1), :]
        return carry

    def narrow(i, carry):
        at = pl.multiple_of(i * 8, 8)
        rows = to_ref[pl.ds(pl.multiple_of(i * block, block), block), :].astype(BF16)
        table = table_ref[pl.ds(at, 8)]
        coarse = table.astype(BF16).astype(F32)
        state = jnp.concatenate([coarse, table - coarse], axis=1).astype(BF16)
        more = jnp.concatenate([moment_ref[pl.ds(at, 8)], head_ref[pl.ds(at, 8)]], axis=1)
        out_ref[pl.ds(at, 8), 0:ROUND, :] = rows.reshape(8, ROUND, LANES)
        out_ref[pl.ds(at, 8), ROUND : ROUND + 16, :] = state
        out_ref[pl.ds(at, 8), ROUND + 16 : ROUND + 32, :] = more.astype(BF16)
        return carry

    lax.fori_loop(0, bag * samples // block, widen, 0)
    lax.fori_loop(0, samples, move, 0)
    lax.fori_loop(0, DEVS // 8, narrow, 0)


def pack(slots, grads, table, moment, head):
    return pl.pallas_call(
        pack_kernel,
        in_specs=[pl.BlockSpec(memory_space=pltpu.SMEM)]
        + [pl.BlockSpec(memory_space=pltpu.VMEM)] * 4,
        out_specs=pl.BlockSpec(memory_space=pltpu.VMEM),
        out_shape=jax.ShapeDtypeStruct((DEVS, SENT, LANES), BF16),
        scratch_shapes=[
            pltpu.VMEM(grads.shape, F32),
            pltpu.VMEM((DEVS * ROUND + 8, LANES), F32),
        ],
        name="pack",
    )(slots, grads, table, moment, head)


def pair_up(line, low):
    other = pltpu.roll(line, ROUND, 1)
    half = DEVS // 2
    left = (line if low else other)[:half]
    right = (other if low else line)[half:]
    return jnp.where(iota((half, LANES), 1) < ROUND, left, right).astype(I32)


def add_rows(index_ref, left_ref, right_ref, acc_ref, with_count):
    width = 8 * LANES
    step = pl.program_id(0)
    turns = left_ref.shape[0] // 8

    def add(i, carry):
        at = pl.ds(pl.multiple_of(i * 8, 8), 8)
        pieces = pl.ds(pl.multiple_of((step * turns + i) * 8, 8), 8)
        index = index_ref[pieces, :]
        index = jnp.concatenate([index[u : u + 1] for u in range(8)], axis=1)
        left, right = left_ref[at], right_ref[at]
        rows = jnp.concatenate([p[u] for u in range(8) for p in (left, right)], axis=0)
        if with_count:
            rows = jnp.concatenate([rows, jnp.ones_like(rows)], axis=1)
        hit = one_hot(iota((acc_ref.shape[0], width), 0) == index)
        acc_ref[...] = acc_ref[...] + jnp.dot(hit, rows, preferred_element_type=F32)
        return carry

    lax.fori_loop(0, turns, add, 0)


STEPS = 4


def half_spec(second):
    count = DEVS // 2 // STEPS
    return pl.BlockSpec((count, ROUND, LANES), lambda i: (i + second * STEPS, 0, 0))


def whole(shape, at=None):
    place = at if at is not None else (0,) * len(shape)
    return pl.BlockSpec(shape, lambda i: place)


STATE_SPEC = whole((DEVS, 32, LANES), (0, ROUND // 32, 0))


def line_of(state_ref):
    high = state_ref[:, 24:25, :].astype(F32).reshape(DEVS, LANES)
    low = state_ref[:, 25:26, :].astype(F32).reshape(DEVS, LANES)
    return high * 32.0 + low - 1.0


def adam(core, state_ref, acc_ref, new_ref, sums_ref, spots_ref):
    def step(i, carry):
        at = pl.multiple_of(i * LANES, LANES)
        part = pl.ds(i * 16, 16)
        total = acc_ref[pl.ds(at, LANES), :]
        shape = (16, 8, LANES)
        grad = total[:, :LANES].reshape(shape)
        touched = (total[:, LANES:] > 0.5).reshape(shape)
        state = state_ref[part].astype(F32)
        table = state[:, 0:8, :] + state[:, 8:16, :]
        moment = state[:, 16:24, :]
        source = iota(shape, 0)
        within = iota(shape, 1)
        lane = iota(shape, 2)
        parity = (core + i * 8 + (source >> 1)) & 1
        own = (source & 1) * 16 + within * 2 + parity
        high = jnp.broadcast_to(state[:, 24:25, :], shape)
        extra = high + jnp.broadcast_to(state[:, 25:26, :], shape)
        var = jnp.sum(jnp.where(lane == ROUND + own, extra, 0.0), axis=2, keepdims=True)
        spot = jnp.sum(jnp.where(lane == ROUND + 32 + own, extra, 0.0), axis=2, keepdims=True)
        mean = jnp.sum(grad * grad, axis=2, keepdims=True) * (1.0 / LANES)
        new_var = beta_two * var + (1.0 - beta_two) * mean
        new_moment = beta_one * moment + (1.0 - beta_one) * grad
        new_table = table - learn_rate * new_moment / (jnp.sqrt(new_var) + epsilon)
        new_table = jnp.where(touched, new_table, table)
        new_ref[pl.ds(at, LANES), :] = new_table.reshape(LANES, LANES).astype(BF16)
        sums_ref[part] = jnp.where(touched, grad, UNTOUCHED)
        spot = jnp.where(touched & (lane == within), spot, 0.0)
        away = jnp.where(touched | (lane != within), 0.0, 4096.0)
        spots_ref[pl.ds(pl.multiple_of(i * 16, 16), 16), :] = jnp.sum(spot + away, axis=1)
        return carry

    lax.fori_loop(0, 8, step, 0)


def update_kernel(
    core_ref,
    state_ref,
    left_ref,
    right_ref,
    new_ref,
    sums_ref,
    spots_ref,
    acc_ref,
    line_ref,
    rounds_ref,
    index_ref,
):
    @pl.when(pl.program_id(0) == 0)
    def _():
        line = line_of(state_ref)
        line_ref[...] = line
        index_ref[...] = pair_up(line, True)
        rounds = state_ref[:, 26:27, :].astype(F32).reshape(DEVS, LANES)
        rounds_ref[0] = jnp.max(rounds).astype(I32)
        acc_ref[...] = jnp.zeros(acc_ref.shape, F32)

    add_rows(index_ref, left_ref, right_ref, acc_ref, True)

    @pl.when(pl.program_id(0) == STEPS - 1)
    def _():
        adam(core_ref[0], state_ref, acc_ref, new_ref, sums_ref, spots_ref)


def updated_shapes(rows):
    return (
        jax.ShapeDtypeStruct((rows, LANES), BF16),
        jax.ShapeDtypeStruct((DEVS, 8, LANES), F32),
        jax.ShapeDtypeStruct((DEVS, LANES), F32),
    )


def updated_specs(rows):
    return [whole((rows, LANES)), whole((DEVS, 8, LANES)), whole((DEVS, LANES))]


def update(core, received, rows):
    return pl.pallas_call(
        update_kernel,
        grid=(STEPS,),
        in_specs=[
            pl.BlockSpec(memory_space=pltpu.SMEM),
            STATE_SPEC,
            half_spec(0),
            half_spec(1),
        ],
        out_specs=updated_specs(rows)
        + [
            whole((rows, 2 * LANES)),
            whole((DEVS, LANES)),
            pl.BlockSpec(memory_space=pltpu.SMEM),
        ],
        out_shape=updated_shapes(rows)
        + (
            jax.ShapeDtypeStruct((rows, 2 * LANES), F32),
            jax.ShapeDtypeStruct((DEVS, LANES), F32),
            jax.ShapeDtypeStruct((1,), I32),
        ),
        scratch_shapes=[pltpu.VMEM((DEVS // 2, LANES), I32)],
        name="update",
    )(core, received, received, received)


def adam_kernel(core_ref, state_ref, acc_ref, new_ref, sums_ref, spots_ref):
    adam(core_ref[0], state_ref, acc_ref, new_ref, sums_ref, spots_ref)


def adam_again(core, received, acc):
    rows = acc.shape[0]
    return pl.pallas_call(
        adam_kernel,
        grid=(1,),
        in_specs=[pl.BlockSpec(memory_space=pltpu.SMEM), STATE_SPEC, whole(acc.shape)],
        out_specs=updated_specs(rows),
        out_shape=updated_shapes(rows),
        name="adam",
    )(core, received, acc)


def more_kernel(line_ref, left_ref, right_ref, start_ref, out_ref, index_ref, *, low, with_count):
    @pl.when(pl.program_id(0) == 0)
    def _():
        index_ref[...] = pair_up(line_ref[...], low)
        out_ref[...] = start_ref[...]

    add_rows(index_ref, left_ref, right_ref, out_ref, with_count)


def more_rows(line, rows, start, low, with_count):
    return pl.pallas_call(
        functools.partial(more_kernel, low=low, with_count=with_count),
        grid=(STEPS,),
        in_specs=[whole(line.shape), half_spec(0), half_spec(1), whole(start.shape)],
        out_specs=whole(start.shape),
        out_shape=jax.ShapeDtypeStruct(start.shape, F32),
        scratch_shapes=[pltpu.VMEM((DEVS // 2, LANES), I32)],
        name="more_rows",
    )(line, rows, rows, start)


def reply_kernel(line_ref, new_ref, out_ref, turned_ref, table_ref):
    turned_ref[...] = line_ref[...].T
    half = new_ref.shape[0] // 2
    table_ref[...] = jnp.concatenate([new_ref[0:half, :], new_ref[half:, :]], axis=1)

    def look(i, carry):
        turned = pltpu.roll(turned_ref[0:ROUND, :], LANES - i * 8, 1).astype(I32)
        within = turned & (half - 1)
        hit = jnp.concatenate(
            [one_hot(iota((ROUND, half), 1) == within[:, u : u + 1]) for u in range(8)], axis=0
        )
        found = jnp.dot(hit, table_ref[...], preferred_element_type=F32)
        for u in range(8):
            piece = found[u * ROUND : (u + 1) * ROUND]
            piece = jnp.where(turned[:, u : u + 1] < half, piece[:, :LANES], piece[:, LANES:])
            out_ref[i * 8 + u] = piece.astype(BF16)
        return carry

    lax.fori_loop(0, DEVS // 8, look, 0)


def reply(line, new_rows):
    return pl.pallas_call(
        reply_kernel,
        in_specs=[pl.BlockSpec(memory_space=pltpu.VMEM)] * 2,
        out_specs=pl.BlockSpec(memory_space=pltpu.VMEM),
        out_shape=jax.ShapeDtypeStruct((DEVS, ROUND, LANES), BF16),
        scratch_shapes=[
            pltpu.VMEM((DEVS, LANES), F32),
            pltpu.VMEM((new_rows.shape[0] // 2, 2 * LANES), BF16),
        ],
        name="reply",
    )(line, new_rows)


def score_kernel(
    keys_ref,
    left_ref,
    right_ref,
    start_ref,
    first_ref,
    second_ref,
    score_ref,
    out_ref,
    index_ref,
    acc_ref,
):
    @pl.when(pl.program_id(0) == 0)
    def _():
        index_ref[...] = pair_up(keys_ref[...], False)
        acc_ref[...] = start_ref[...]

    add_rows(index_ref, left_ref, right_ref, acc_ref, False)

    @pl.when(pl.program_id(0) == STEPS - 1)
    def _():
        samples = out_ref.shape[1]
        pooled = jnp.concatenate(
            [acc_ref[f * samples : (f + 1) * samples, :] for f in range(4)], axis=1
        ).astype(BF16)
        hidden = jnp.dot(pooled, first_ref[...], preferred_element_type=F32)
        hidden = jnp.maximum(hidden, 0.0).astype(BF16)
        hidden = jnp.dot(hidden, second_ref[...], preferred_element_type=F32)
        hidden = jnp.maximum(hidden, 0.0).astype(BF16)
        weights = jnp.broadcast_to(score_ref[...], (16, score_ref.shape[1]))
        scores = lax.dot_general(
            weights, hidden, (((1,), (1,)), ((), ())), preferred_element_type=F32
        )
        out_ref[...] = scores[0:1, :]


def score(keys, rows, start, w_first, w_second, w_score):
    samples = start.shape[0] // 4
    return pl.pallas_call(
        score_kernel,
        grid=(STEPS,),
        in_specs=[whole(keys.shape), half_spec(0), half_spec(1), whole(start.shape)]
        + [whole(w.shape) for w in (w_first, w_second, w_score)],
        out_specs=whole((1, samples)),
        out_shape=jax.ShapeDtypeStruct((1, samples), F32),
        scratch_shapes=[
            pltpu.VMEM((DEVS // 2, LANES), I32),
            pltpu.VMEM(start.shape, F32),
        ],
        name="score",
    )(keys, rows, rows, start, w_first, w_second, w_score)


def exchange(value):
    return lax.all_to_all(value, ALL, 0, 0, tiled=True)


def place_rows(serving_old, slot_index, rows_in):
    tab_rows, row_width = serving_old.shape
    block = 512
    old_blocks = serving_old.reshape(tab_rows // block, block, row_width)
    firsts = jnp.arange(tab_rows // block, dtype=jnp.int32) * block

    def place_block(pieces):
        old_piece, first = pieces
        wanted = first + jnp.arange(block, dtype=jnp.int32)
        hit = (wanted[:, None] == slot_index[None, :]).astype(jnp.bfloat16)
        fresh = jnp.dot(hit, rows_in, preferred_element_type=jnp.float32)
        found = jnp.sum(hit.astype(jnp.float32), axis=1) > 0.5
        return jnp.where(found[:, None], fresh.astype(jnp.bfloat16), old_piece)

    return lax.map(place_block, (old_blocks, firsts)).reshape(tab_rows, row_width)


def per_device(
    touched_ids,
    bag_lengths,
    train_map,
    serve_map,
    slot_grads,
    table,
    moment,
    row_var,
    serving_old,
    w_first,
    w_second,
    w_score,
):
    owners = lax.axis_size("shard")
    owner = lax.axis_index("shard")
    rep = lax.axis_index("rep")
    tab_rows, row_width = table.shape
    samples, bag = touched_ids.shape
    swap = [(0, 1), (1, 0)]
    odd = owner % 2 == 1
    rows_here = tab_rows // 2

    ids = jnp.concatenate([touched_ids, bag_lengths], axis=1).T
    map_rows = train_map.reshape(-1, LANES)
    grads = slot_grads.reshape(samples * bag, row_width)

    def outgoing(value):
        half = lax.dynamic_slice_in_dim(value, rep * rows_here, rows_here, 0)
        half = half.reshape(8, 2, owners, row_width)
        half = jnp.where(odd, half[:, ::-1], half)
        return half.transpose(2, 1, 0, 3).reshape(DEVS, 8, row_width)

    spots = (serve_map % tab_rows).astype(F32).reshape(tab_rows // owners, owners).T
    spread = jnp.concatenate([row_var.reshape(tab_rows // owners, owners).T, spots], axis=1)
    spread = jnp.broadcast_to(spread[:, None, :], (owners, 2, 2 * tab_rows // owners))
    extra = jnp.concatenate([jnp.zeros((DEVS, ROUND), F32), spread.reshape(DEVS, -1)], axis=1)

    table_out, moment_out = outgoing(table), outgoing(moment)
    slots, keys, head = route(jnp.zeros((1,), I32), ids, map_rows, extra)
    received = exchange(pack(slots, grads, table_out, moment_out, head))
    core = rep.reshape(1).astype(I32)
    new_rows, sums, places, acc, line, rounds = update(core, received, rows_here)
    rounds = rounds[0]
    one = jnp.ones((), I32)

    def more_sums(carry):
        k, acc = carry[0], carry[1]
        slots, _, head = route(k.reshape(1), ids, map_rows, extra)
        got = exchange(pack(slots, grads, table_out, moment_out, head))
        line = got[:, ROUND + 24].astype(F32) * 32.0 + got[:, ROUND + 25].astype(F32) - 1.0
        acc = more_rows(line, got, acc, True, True)
        return (k + 1, acc) + tuple(adam_again(core, received, acc))

    _, _, new_rows, sums, places = lax.while_loop(
        lambda c: c[0] < rounds, more_sums, (one, acc, new_rows, sums, places)
    )

    back = exchange(sums)
    answer = exchange(reply(line, new_rows))

    other_rows = lax.ppermute(new_rows, "rep", swap)
    places = places[:, :8].reshape(-1).astype(I32)
    other_places = lax.ppermute(places, "rep", swap)
    serving_table = place_rows(
        serving_old,
        jnp.concatenate([places, other_places]),
        jnp.concatenate([new_rows, other_rows]),
    )

    back = back.reshape(owners, 2, 8, row_width)
    back = jnp.where(odd, back[:, ::-1], back)
    half = back.transpose(2, 1, 0, 3).reshape(rows_here, row_width)
    other = lax.ppermute(half, "rep", swap)
    grad_sum = jnp.where(
        rep == 0, jnp.concatenate([half, other]), jnp.concatenate([other, half])
    )
    touched = grad_sum[:, :1] < 0.5 * UNTOUCHED
    new_moment = jnp.where(touched, beta_one * moment + (1.0 - beta_one) * grad_sum, moment)
    mean = jnp.mean(jnp.where(touched, grad_sum * grad_sum, 0.0), axis=1)
    new_var = jnp.where(touched[:, 0], beta_two * row_var + (1.0 - beta_two) * mean, row_var)
    new_table = jnp.where(
        touched, table - learn_rate * new_moment / (jnp.sqrt(new_var)[:, None] + epsilon), table
    )

    def more_pooled(carry):
        k, acc = carry
        _, keys, head = route(k.reshape(1), ids, map_rows, extra)
        got = exchange(head)
        line = got[:, 0] * 32.0 + got[:, 1] - 1.0
        return (k + 1, more_rows(keys, exchange(reply(line, new_rows)), acc, False, False))

    answer, rounds = lax.optimization_barrier((answer, rounds))
    _, pooled = lax.while_loop(
        lambda c: c[0] < rounds,
        more_pooled,
        (one, jnp.zeros((4 * samples, row_width), F32)),
    )
    scores = score(keys, answer, pooled, w_first, w_second, w_score.reshape(1, -1))
    return (new_table, new_moment, new_var, serving_table, scores.reshape(samples))


def solution(mesh):
    in_specs = (
        P(("shard", "rep"), None),
        P(("shard", "rep"), None),
        P(),
        P("shard"),
        P(("shard", "rep"), None, None),
        P("shard", None),
        P("shard", None),
        P("shard"),
        P("shard", None),
        P(),
        P(),
        P(),
    )
    out_specs = (
        P("shard", None),
        P("shard", None),
        P("shard"),
        P("shard", None),
        P(("shard", "rep")),
    )
    return jax.shard_map(
        per_device, mesh=mesh, in_specs=in_specs, out_specs=out_specs, check_vma=False
    )
```

```python
import functools

import jax
import jax.numpy as jnp
from jax import lax
from jax.experimental import pallas as pl
from jax.experimental.pallas import tpu as pltpu
from jax.sharding import PartitionSpec as P

beta_one = 0.9
beta_two = 0.999
learn_rate = 0.1
epsilon = 1e-06

ROUND = 64
DEVS = 128
LANES = 128
UNTOUCHED = 1e30
F32 = jnp.float32
BF16 = jnp.bfloat16
I32 = jnp.int32
ALL = ("shard", "rep")
SENT = ROUND + 32


def iota(shape, dim):
    return lax.broadcasted_iota(I32, shape, dim)


def one_hot(mask):
    return jnp.where(mask, 1.0, 0.0).astype(BF16)


def hot_rows(count, index):
    index = index.astype(jnp.int16)
    place = iota((count, index.shape[1]), 0).astype(jnp.int16)
    return jnp.where(place == index, jnp.bfloat16(1), jnp.bfloat16(0))


def route_kernel(round_ref, ids_ref, map_ref, extra_ref, slots_ref, keys_ref, row_ref):
    bag, samples = ids_ref.shape[0] - 4, ids_ref.shape[1]
    step = 4
    wide = step * samples
    first = round_ref[0] * ROUND
    table = map_ref[...]
    high = (table >> 9).astype(F32).T
    low = ((table & 511) - 256).astype(F32).T
    parts = jnp.concatenate([high, low], axis=0).astype(BF16)
    upto = one_hot(iota((wide, wide), 0) <= iota((wide, wide), 1))
    ends = []
    total = jnp.zeros((1, samples), I32)
    for f in range(3):
        total = total + ids_ref[bag + f : bag + f + 1, :]
        ends.append(total)
    sample = iota((1, samples), 1)
    seen = jnp.zeros((DEVS, 1), F32)
    layout = jnp.zeros((DEVS, 4 * ROUND), F32)
    for t in range(0, bag, step):
        ids = jnp.concatenate([ids_ref[t + u : t + u + 1, :] for u in range(step)], axis=1)
        keys = []
        for u in range(step):
            field = sum((jnp.where(e <= t + u, 1, 0) for e in ends), jnp.zeros((1, samples), I32))
            keys.append(field * samples + sample)
        key = jnp.concatenate(keys, axis=1) + 1
        hit = hot_rows(table.shape[0], ids >> 7)
        both = jnp.dot(parts, hit, preferred_element_type=F32)
        value = both[:LANES] * 512.0 + both[LANES:] + 256.0
        value = jnp.where(iota((LANES, wide), 0) == (ids & 127), value, 0.0)
        position = jnp.sum(value, axis=0, keepdims=True).astype(I32)
        owner = position >> 11
        stride = (position >> 6) & 31
        dest = (position & 63) * 2 + ((stride + owner) & 1)
        local = owner * 16 + (stride >> 1) + 1
        mine = iota((DEVS, wide), 0) == dest
        hot = one_hot(mine)
        running = jnp.dot(hot, upto, preferred_element_type=F32)
        rank = jnp.sum(jnp.where(mine, running + seen, 0.0), axis=0, keepdims=True)
        seen = seen + running[:, wide - 1 : wide]
        rank = rank.astype(I32) - 1 - first
        here = iota((ROUND, wide), 0) == rank
        columns = jnp.concatenate(
            [
                jnp.where(here, v.astype(F32), 0.0)
                for v in (local >> 5, key >> 5, local & 31, key & 31)
            ],
            axis=0,
        ).astype(BF16)
        layout = layout + lax.dot_general(
            hot, columns, (((1,), (1,)), ((), ())), preferred_element_type=F32
        )
        fits = (rank >= 0) & (rank < ROUND)
        slot = jnp.where(fits, dest * ROUND + rank, DEVS * ROUND)
        for u in range(step):
            slots_ref[t + u : t + u + 1, :] = slot[:, u * samples : (u + 1) * samples]
    keys_ref[...] = layout[:, :LANES] * 32.0 + layout[:, LANES:] - 1.0
    most = jnp.max(seen, axis=0, keepdims=True).astype(I32)
    rounds = ((most + ROUND - 1) // ROUND).astype(F32)
    extra = extra_ref[...]
    coarse = extra.astype(BF16).astype(F32)
    index = iota((DEVS, LANES), 1) < ROUND
    high = jnp.where(index, layout[:, :LANES], coarse)
    low = jnp.where(index, layout[:, LANES:], extra - coarse)
    row_ref[:, 0:1, :] = high.reshape(DEVS, 1, LANES)
    row_ref[:, 1:2, :] = low.reshape(DEVS, 1, LANES)
    row_ref[:, 2:8, :] = jnp.broadcast_to(rounds.reshape(1, 1, 1), (DEVS, 6, LANES))


def route(round_index, ids, train_map, extra):
    bag = ids.shape[0] - 4
    return pl.pallas_call(
        route_kernel,
        in_specs=[pl.BlockSpec(memory_space=pltpu.SMEM)]
        + [pl.BlockSpec(memory_space=pltpu.VMEM)] * 3,
        out_specs=[pl.BlockSpec(memory_space=pltpu.VMEM)] * 3,
        out_shape=(
            jax.ShapeDtypeStruct((bag, ids.shape[1]), I32),
            jax.ShapeDtypeStruct((DEVS, LANES), F32),
            jax.ShapeDtypeStruct((DEVS, 8, LANES), F32),
        ),
        name="route",
    )(round_index, ids, train_map, extra)


def pack_kernel(slots_ref, grads_ref, table_ref, moment_ref, head_ref, out_ref, from_ref, to_ref):
    count = slots_ref.shape[0]
    bag = 32
    samples = count // bag
    block = 512

    def widen(i, carry):
        at = pl.multiple_of(i * block, block)
        from_ref[pl.ds(at, block), :] = grads_ref[pl.ds(at, block), :].astype(F32)
        to_ref[pl.ds(at * 2, block), :] = jnp.zeros((block, LANES), F32)
        to_ref[pl.ds(at * 2 + block, block), :] = jnp.zeros((block, LANES), F32)
        return carry

    def move(i, carry):
        first = (i & 3) * (bag * bag) + (i >> 2)
        for u in range(bag):
            slot = slots_ref[i * bag + u]
            to_ref[pl.ds(slot, 1), :] = from_ref[pl.ds(first + u * bag, 1), :]
        return carry

    def narrow(i, carry):
        at = pl.multiple_of(i * 8, 8)
        rows = to_ref[pl.ds(pl.multiple_of(i * block, block), block), :].astype(BF16)
        table = table_ref[pl.ds(at, 8)]
        coarse = table.astype(BF16).astype(F32)
        state = jnp.concatenate([coarse, table - coarse], axis=1).astype(BF16)
        more = jnp.concatenate([moment_ref[pl.ds(at, 8)], head_ref[pl.ds(at, 8)]], axis=1)
        out_ref[pl.ds(at, 8), 0:ROUND, :] = rows.reshape(8, ROUND, LANES)
        out_ref[pl.ds(at, 8), ROUND : ROUND + 16, :] = state
        out_ref[pl.ds(at, 8), ROUND + 16 : ROUND + 32, :] = more.astype(BF16)
        return carry

    lax.fori_loop(0, bag * samples // block, widen, 0)
    lax.fori_loop(0, count // bag, move, 0)
    lax.fori_loop(0, DEVS // 8, narrow, 0)


def pack(slots, grads, table, moment, head):
    return pl.pallas_call(
        pack_kernel,
        in_specs=[pl.BlockSpec(memory_space=pltpu.SMEM)]
        + [pl.BlockSpec(memory_space=pltpu.VMEM)] * 4,
        out_specs=pl.BlockSpec(memory_space=pltpu.VMEM),
        out_shape=jax.ShapeDtypeStruct((DEVS, SENT, LANES), BF16),
        scratch_shapes=[
            pltpu.VMEM(grads.shape, F32),
            pltpu.VMEM((DEVS * ROUND + 8, LANES), F32),
        ],
        name="pack",
    )(slots.reshape(-1), grads, table, moment, head)


def pair_up(line, low):
    other = pltpu.roll(line, ROUND, 1)
    half = DEVS // 2
    left = (line if low else other)[:half]
    right = (other if low else line)[half:]
    return jnp.where(iota((half, LANES), 1) < ROUND, left, right).astype(I32)


def add_rows(index_ref, left_ref, right_ref, acc_ref, with_count):
    width = 8 * LANES
    step = pl.program_id(0)
    turns = left_ref.shape[0] // 8

    def add(i, carry):
        at = pl.ds(pl.multiple_of(i * 8, 8), 8)
        pieces = pl.ds(pl.multiple_of((step * turns + i) * 8, 8), 8)
        index = index_ref[pieces, :]
        index = jnp.concatenate([index[u : u + 1] for u in range(8)], axis=1)
        left, right = left_ref[at], right_ref[at]
        rows = jnp.concatenate([p[u] for u in range(8) for p in (left, right)], axis=0)
        if with_count:
            rows = jnp.concatenate([rows, jnp.ones_like(rows)], axis=1)
        hit = hot_rows(acc_ref.shape[0], index)
        acc_ref[...] = acc_ref[...] + jnp.dot(hit, rows, preferred_element_type=F32)
        return carry

    lax.fori_loop(0, turns, add, 0)


STEPS = 4


def half_spec(second):
    count = DEVS // 2 // STEPS
    return pl.BlockSpec((count, ROUND, LANES), lambda i: (i + second * STEPS, 0, 0))


def whole(shape, at=None):
    place = at if at is not None else (0,) * len(shape)
    return pl.BlockSpec(shape, lambda i: place)


STATE_SPEC = whole((DEVS, 32, LANES), (0, ROUND // 32, 0))


def line_of(state_ref):
    high = state_ref[:, 24:25, :].astype(F32).reshape(DEVS, LANES)
    low = state_ref[:, 25:26, :].astype(F32).reshape(DEVS, LANES)
    return high * 32.0 + low - 1.0


def adam(core, state_ref, acc_ref, new_ref, sums_ref, spots_ref):
    def step(i, carry):
        at = pl.multiple_of(i * LANES, LANES)
        part = pl.ds(i * 16, 16)
        total = acc_ref[pl.ds(at, LANES), :]
        shape = (16, 8, LANES)
        grad = total[:, :LANES].reshape(shape)
        touched = (total[:, LANES:] > 0.5).reshape(shape)
        state = state_ref[part].astype(F32)
        still = state[:, 0:8, :] + state[:, 8:16, :]
        moment = state[:, 16:24, :]
        source = iota(shape, 0)
        within = iota(shape, 1)
        lane = iota(shape, 2)
        parity = (core + i * 8 + (source >> 1)) & 1
        own = (source & 1) * 16 + within * 2 + parity
        high = jnp.broadcast_to(state[:, 24:25, :], shape)
        extra = high + jnp.broadcast_to(state[:, 25:26, :], shape)
        var = jnp.sum(jnp.where(lane == ROUND + own, extra, 0.0), axis=2, keepdims=True)
        spot = jnp.sum(jnp.where(lane == ROUND + 32 + own, extra, 0.0), axis=2, keepdims=True)
        mean = jnp.sum(grad * grad, axis=2, keepdims=True) * (1.0 / LANES)
        new_var = beta_two * var + (1.0 - beta_two) * mean
        scale = 1.0 / (jnp.sqrt(new_var) + epsilon)
        change = scale - 1.0 / (jnp.sqrt(beta_two * var) + epsilon)
        step_of = beta_one * moment * change + (1.0 - beta_one) * grad * scale
        new_table = still - learn_rate * step_of
        new_ref[pl.ds(at, LANES), :] = new_table.reshape(LANES, LANES).astype(BF16)
        sums_ref[part] = jnp.where(touched, grad, UNTOUCHED)
        spot = jnp.where(lane == source * 8 + within, jnp.where(touched, spot, 4096.0), 0.0)
        spot = jnp.sum(jnp.sum(spot, axis=0), axis=0, keepdims=True)
        spots_ref[pl.ds(i, 1), :] = spot.astype(I32)
        return carry

    lax.fori_loop(0, 8, step, 0)


def update_kernel(
    core_ref,
    state_ref,
    left_ref,
    right_ref,
    new_ref,
    sums_ref,
    spots_ref,
    acc_ref,
    line_ref,
    rounds_ref,
    index_ref,
):
    @pl.when(pl.program_id(0) == 0)
    def _():
        line = line_of(state_ref)
        line_ref[...] = line
        index_ref[...] = pair_up(line, True)
        rounds = state_ref[:, 26:27, :].astype(F32).reshape(DEVS, LANES)
        rounds_ref[0] = jnp.max(rounds).astype(I32)
        acc_ref[...] = jnp.zeros(acc_ref.shape, F32)

    add_rows(index_ref, left_ref, right_ref, acc_ref, True)

    @pl.when(pl.program_id(0) == STEPS - 1)
    def _():
        adam(core_ref[0], state_ref, acc_ref, new_ref, sums_ref, spots_ref)


def updated_shapes(rows):
    return (
        jax.ShapeDtypeStruct((rows, LANES), BF16),
        jax.ShapeDtypeStruct((DEVS, 8, LANES), F32),
        jax.ShapeDtypeStruct((8, LANES), I32),
    )


def updated_specs(rows):
    return [whole((rows, LANES)), whole((DEVS, 8, LANES)), whole((8, LANES))]


def update(core, received, rows):
    return pl.pallas_call(
        update_kernel,
        grid=(STEPS,),
        in_specs=[
            pl.BlockSpec(memory_space=pltpu.SMEM),
            STATE_SPEC,
            half_spec(0),
            half_spec(1),
        ],
        out_specs=updated_specs(rows)
        + [
            whole((rows, 2 * LANES)),
            whole((DEVS, LANES)),
            pl.BlockSpec(memory_space=pltpu.SMEM),
        ],
        out_shape=updated_shapes(rows)
        + (
            jax.ShapeDtypeStruct((rows, 2 * LANES), F32),
            jax.ShapeDtypeStruct((DEVS, LANES), F32),
            jax.ShapeDtypeStruct((1,), I32),
        ),
        scratch_shapes=[pltpu.VMEM((DEVS // 2, LANES), I32)],
        name="update",
    )(core, received, received, received)


def adam_kernel(core_ref, state_ref, acc_ref, new_ref, sums_ref, spots_ref):
    adam(core_ref[0], state_ref, acc_ref, new_ref, sums_ref, spots_ref)


def adam_again(core, received, acc):
    rows = acc.shape[0]
    return pl.pallas_call(
        adam_kernel,
        grid=(1,),
        in_specs=[pl.BlockSpec(memory_space=pltpu.SMEM), STATE_SPEC, whole(acc.shape)],
        out_specs=updated_specs(rows),
        out_shape=updated_shapes(rows),
        name="adam",
    )(core, received, acc)


def more_kernel(line_ref, left_ref, right_ref, start_ref, out_ref, index_ref, *, low, with_count):
    @pl.when(pl.program_id(0) == 0)
    def _():
        index_ref[...] = pair_up(line_ref[...], low)
        out_ref[...] = start_ref[...]

    add_rows(index_ref, left_ref, right_ref, out_ref, with_count)


def more_rows(line, rows, start, low, with_count):
    return pl.pallas_call(
        functools.partial(more_kernel, low=low, with_count=with_count),
        grid=(STEPS,),
        in_specs=[whole(line.shape), half_spec(0), half_spec(1), whole(start.shape)],
        out_specs=whole(start.shape),
        out_shape=jax.ShapeDtypeStruct(start.shape, F32),
        scratch_shapes=[pltpu.VMEM((DEVS // 2, LANES), I32)],
        name="more_rows",
    )(line, rows, rows, start)


def reply_kernel(line_ref, new_ref, out_ref, turned_ref, table_ref):
    turned_ref[...] = line_ref[...].T
    part = new_ref.shape[0] // 4
    table_ref[...] = jnp.concatenate(
        [new_ref[k * part : (k + 1) * part, :] for k in range(4)], axis=1
    )

    def look(i, carry):
        turned = pltpu.roll(turned_ref[0:ROUND, :], LANES - i * 16, 1).astype(I32)
        within = turned & (part - 1)
        hit = jnp.concatenate(
            [one_hot(iota((ROUND, part), 1) == within[:, u : u + 1]) for u in range(16)], axis=0
        )
        found = jnp.dot(hit, table_ref[...], preferred_element_type=F32)
        for u in range(16):
            piece = found[u * ROUND : (u + 1) * ROUND]
            row = jnp.broadcast_to(turned[:, u : u + 1], (ROUND, LANES))
            low = jnp.where(row < part, piece[:, :LANES], piece[:, LANES : 2 * LANES])
            high = jnp.where(
                row < 3 * part, piece[:, 2 * LANES : 3 * LANES], piece[:, 3 * LANES :]
            )
            out_ref[i * 16 + u] = jnp.where(row < 2 * part, low, high).astype(BF16)
        return carry

    lax.fori_loop(0, DEVS // 16, look, 0)


def reply(line, new_rows):
    return pl.pallas_call(
        reply_kernel,
        in_specs=[pl.BlockSpec(memory_space=pltpu.VMEM)] * 2,
        out_specs=pl.BlockSpec(memory_space=pltpu.VMEM),
        out_shape=jax.ShapeDtypeStruct((DEVS, ROUND, LANES), BF16),
        scratch_shapes=[
            pltpu.VMEM((DEVS, LANES), F32),
            pltpu.VMEM((new_rows.shape[0] // 4, 4 * LANES), BF16),
        ],
        name="reply",
    )(line, new_rows)


def score_kernel(
    keys_ref,
    left_ref,
    right_ref,
    start_ref,
    first_ref,
    second_ref,
    score_ref,
    out_ref,
    index_ref,
    acc_ref,
):
    @pl.when(pl.program_id(0) == 0)
    def _():
        index_ref[...] = pair_up(keys_ref[...], False)
        acc_ref[...] = start_ref[...]

    add_rows(index_ref, left_ref, right_ref, acc_ref, False)

    @pl.when(pl.program_id(0) == STEPS - 1)
    def _():
        samples = out_ref.shape[1]
        pooled = jnp.concatenate(
            [acc_ref[f * samples : (f + 1) * samples, :] for f in range(4)], axis=1
        ).astype(BF16)
        hidden = jnp.dot(pooled, first_ref[...], preferred_element_type=F32)
        hidden = jnp.maximum(hidden, 0.0).astype(BF16)
        hidden = jnp.dot(hidden, second_ref[...], preferred_element_type=F32)
        hidden = jnp.maximum(hidden, 0.0).astype(BF16)
        weights = jnp.broadcast_to(score_ref[...], (16, score_ref.shape[1]))
        scores = lax.dot_general(
            weights, hidden, (((1,), (1,)), ((), ())), preferred_element_type=F32
        )
        out_ref[...] = scores[0:1, :]


def score(keys, rows, start, w_first, w_second, w_score):
    samples = start.shape[0] // 4
    return pl.pallas_call(
        score_kernel,
        grid=(STEPS,),
        in_specs=[whole(keys.shape), half_spec(0), half_spec(1), whole(start.shape)]
        + [whole(w.shape) for w in (w_first, w_second, w_score)],
        out_specs=whole((1, samples)),
        out_shape=jax.ShapeDtypeStruct((1, samples), F32),
        scratch_shapes=[
            pltpu.VMEM((DEVS // 2, LANES), I32),
            pltpu.VMEM(start.shape, F32),
        ],
        name="score",
    )(keys, rows, rows, start, w_first, w_second, w_score)


def exchange(value):
    return lax.all_to_all(value, ALL, 0, 0, tiled=True)


def place_kernel(old_ref, own_ref, other_ref, own_at_ref, other_at_ref, out_ref):
    block = 512

    def place(i, carry):
        at = pl.ds(pl.multiple_of(i * block, block), block)
        total = jnp.zeros((block, 2 * LANES), F32)
        for at_ref, rows_ref in ((own_at_ref, own_ref), (other_at_ref, other_ref)):
            spots = at_ref[...] - i * block
            spots = jnp.where((spots >= 0) & (spots < block), spots, -1)
            spots = jnp.concatenate([spots[u : u + 1] for u in range(8)], axis=1)
            rows = rows_ref[...]
            rows = jnp.concatenate([rows, jnp.ones_like(rows)], axis=1)
            total = total + jnp.dot(hot_rows(block, spots), rows, preferred_element_type=F32)
        fresh = total[:, :LANES].astype(BF16).astype(F32)
        old = old_ref[at, :].astype(F32)
        out_ref[at, :] = jnp.where(total[:, LANES:] > 0.5, fresh, old).astype(BF16)
        return carry

    lax.fori_loop(0, old_ref.shape[0] // block, place, 0)


def place_rows(old, own, other, own_at, other_at):
    return pl.pallas_call(
        place_kernel,
        in_specs=[pl.BlockSpec(memory_space=pltpu.VMEM)] * 5,
        out_specs=pl.BlockSpec(memory_space=pltpu.VMEM),
        out_shape=jax.ShapeDtypeStruct(old.shape, BF16),
        name="place",
    )(old, own, other, own_at, other_at)


def per_device(
    touched_ids,
    bag_lengths,
    train_map,
    serve_map,
    slot_grads,
    table,
    moment,
    row_var,
    serving_old,
    w_first,
    w_second,
    w_score,
):
    owners = lax.axis_size("shard")
    owner = lax.axis_index("shard")
    rep = lax.axis_index("rep")
    tab_rows, row_width = table.shape
    samples, bag = touched_ids.shape
    swap = [(0, 1), (1, 0)]
    odd = owner % 2 == 1
    rows_here = tab_rows // 2

    ids = jnp.concatenate([touched_ids, bag_lengths], axis=1).T
    map_rows = train_map.reshape(-1, LANES)
    grads = slot_grads.reshape(samples * bag, row_width)

    def outgoing(value):
        half = lax.dynamic_slice_in_dim(value, rep * rows_here, rows_here, 0)
        half = half.reshape(8, 2, owners, row_width)
        half = jnp.where(odd, half[:, ::-1], half)
        return half.transpose(2, 1, 0, 3).reshape(DEVS, 8, row_width)

    spots = (serve_map % tab_rows).astype(F32).reshape(tab_rows // owners, owners).T
    spread = jnp.concatenate([row_var.reshape(tab_rows // owners, owners).T, spots], axis=1)
    spread = jnp.broadcast_to(spread[:, None, :], (owners, 2, 2 * tab_rows // owners))
    extra = jnp.concatenate([jnp.zeros((DEVS, ROUND), F32), spread.reshape(DEVS, -1)], axis=1)

    scale = learn_rate * beta_one / (jnp.sqrt(beta_two * row_var) + epsilon)
    table_out, moment_out = outgoing(table - moment * scale[:, None]), outgoing(moment)
    slots, keys, head = route(jnp.zeros((1,), I32), ids, map_rows, extra)
    received = exchange(pack(slots, grads, table_out, moment_out, head))
    core = rep.reshape(1).astype(I32)
    new_rows, sums, places, acc, line, rounds = update(core, received, rows_here)
    rounds = rounds[0]
    one = jnp.ones((), I32)

    def more_sums(carry):
        k, acc = carry[0], carry[1]
        slots, _, head = route(k.reshape(1), ids, map_rows, extra)
        got = exchange(pack(slots, grads, table_out, moment_out, head))
        line = got[:, ROUND + 24].astype(F32) * 32.0 + got[:, ROUND + 25].astype(F32) - 1.0
        acc = more_rows(line, got, acc, True, True)
        return (k + 1, acc) + tuple(adam_again(core, received, acc))

    _, _, new_rows, sums, places = lax.while_loop(
        lambda c: c[0] < rounds, more_sums, (one, acc, new_rows, sums, places)
    )

    back = exchange(sums)
    answer = exchange(reply(line, new_rows))

    other_rows = lax.ppermute(new_rows, "rep", swap)
    other_places = lax.ppermute(places, "rep", swap)
    serving_table = place_rows(serving_old, new_rows, other_rows, places, other_places)

    back = back.reshape(owners, 2, 8, row_width)
    back = jnp.where(odd, back[:, ::-1], back)
    half = back.transpose(2, 1, 0, 3).reshape(rows_here, row_width)
    other = lax.ppermute(half, "rep", swap)
    grad_sum = jnp.where(
        rep == 0, jnp.concatenate([half, other]), jnp.concatenate([other, half])
    )
    touched = grad_sum[:, :1] < 0.5 * UNTOUCHED
    new_moment = jnp.where(touched, beta_one * moment + (1.0 - beta_one) * grad_sum, moment)
    mean = jnp.mean(jnp.where(touched, grad_sum * grad_sum, 0.0), axis=1)
    new_var = jnp.where(touched[:, 0], beta_two * row_var + (1.0 - beta_two) * mean, row_var)
    new_table = jnp.where(
        touched, table - learn_rate * new_moment / (jnp.sqrt(new_var)[:, None] + epsilon), table
    )

    def more_pooled(carry):
        k, acc = carry
        _, keys, head = route(k.reshape(1), ids, map_rows, extra)
        got = exchange(head)
        line = got[:, 0] * 32.0 + got[:, 1] - 1.0
        return (k + 1, more_rows(keys, exchange(reply(line, new_rows)), acc, False, False))

    rounds, _ = lax.optimization_barrier((rounds, answer[0, 0, 0]))
    _, pooled = lax.while_loop(
        lambda c: c[0] < rounds,
        more_pooled,
        (one, jnp.zeros((4 * samples, row_width), F32)),
    )
    scores = score(keys, answer, pooled, w_first, w_second, w_score.reshape(1, -1))
    return (new_table, new_moment, new_var, serving_table, scores.reshape(samples))


def solution(mesh):
    in_specs = (
        P(("shard", "rep"), None),
        P(("shard", "rep"), None),
        P(),
        P("shard"),
        P(("shard", "rep"), None, None),
        P("shard", None),
        P("shard", None),
        P("shard"),
        P("shard", None),
        P(),
        P(),
        P(),
    )
    out_specs = (
        P("shard", None),
        P("shard", None),
        P("shard"),
        P("shard", None),
        P(("shard", "rep")),
    )
    return jax.shard_map(
        per_device, mesh=mesh, in_specs=in_specs, out_specs=out_specs, check_vma=False
    )
```

```python
import functools

import jax
import jax.numpy as jnp
from jax import lax
from jax.experimental import pallas as pl
from jax.experimental.pallas import tpu as pltpu
from jax.sharding import PartitionSpec as P

beta_one = 0.9
beta_two = 0.999
learn_rate = 0.1
epsilon = 1e-06

ROUND = 64
DEVS = 128
LANES = 128
UNTOUCHED = 1e30
F32 = jnp.float32
BF16 = jnp.bfloat16
I32 = jnp.int32
ALL = ("shard", "rep")
SENT = ROUND + 32


def iota(shape, dim):
    return lax.broadcasted_iota(I32, shape, dim)


def one_hot(mask):
    return jnp.where(mask, 1.0, 0.0).astype(BF16)


def hot_rows(count, index):
    index = index.astype(jnp.int16)
    place = iota((count, index.shape[1]), 0).astype(jnp.int16)
    return jnp.where(place == index, jnp.bfloat16(1), jnp.bfloat16(0))


def route_kernel(round_ref, ids_ref, map_ref, extra_ref, slots_ref, keys_ref, row_ref):
    bag, samples = ids_ref.shape[0] - 4, ids_ref.shape[1]
    step = 4
    wide = step * samples
    first = round_ref[0] * ROUND
    table = map_ref[...]
    high = (table >> 9).astype(F32).T
    low = ((table & 511) - 256).astype(F32).T
    parts = jnp.concatenate([high, low], axis=0).astype(BF16)
    upto = one_hot(iota((wide, wide), 0) <= iota((wide, wide), 1))
    ends = []
    total = jnp.zeros((1, samples), I32)
    for f in range(3):
        total = total + ids_ref[bag + f : bag + f + 1, :]
        ends.append(total)
    sample = iota((1, samples), 1)
    seen = jnp.zeros((DEVS, 1), F32)
    layout = jnp.zeros((DEVS, 4 * ROUND), F32)
    for t in range(0, bag, step):
        ids = jnp.concatenate([ids_ref[t + u : t + u + 1, :] for u in range(step)], axis=1)
        keys = []
        for u in range(step):
            field = sum((jnp.where(e <= t + u, 1, 0) for e in ends), jnp.zeros((1, samples), I32))
            keys.append(field * samples + sample)
        key = jnp.concatenate(keys, axis=1) + 1
        hit = hot_rows(table.shape[0], ids >> 7)
        both = jnp.dot(parts, hit, preferred_element_type=F32)
        value = both[:LANES] * 512.0 + both[LANES:] + 256.0
        value = jnp.where(iota((LANES, wide), 0) == (ids & 127), value, 0.0)
        position = jnp.sum(value, axis=0, keepdims=True).astype(I32)
        owner = position >> 11
        stride = (position >> 6) & 31
        dest = (position & 63) * 2 + ((stride + owner) & 1)
        local = owner * 16 + (stride >> 1) + 1
        mine = iota((DEVS, wide), 0) == dest
        hot = one_hot(mine)
        running = jnp.dot(hot, upto, preferred_element_type=F32)
        rank = jnp.sum(jnp.where(mine, running + seen, 0.0), axis=0, keepdims=True)
        seen = seen + running[:, wide - 1 : wide]
        rank = rank.astype(I32) - 1 - first
        here = iota((ROUND, wide), 0) == rank
        columns = jnp.concatenate(
            [
                jnp.where(here, v.astype(F32), 0.0)
                for v in (local >> 5, key >> 5, local & 31, key & 31)
            ],
            axis=0,
        ).astype(BF16)
        layout = layout + lax.dot_general(
            hot, columns, (((1,), (1,)), ((), ())), preferred_element_type=F32
        )
        fits = (rank >= 0) & (rank < ROUND)
        slot = jnp.where(fits, dest * ROUND + rank, DEVS * ROUND)
        for u in range(step):
            slots_ref[t + u : t + u + 1, :] = slot[:, u * samples : (u + 1) * samples]
    keys_ref[...] = layout[:, :LANES] * 32.0 + layout[:, LANES:] - 1.0
    most = jnp.max(seen, axis=0, keepdims=True).astype(I32)
    rounds = ((most + ROUND - 1) // ROUND).astype(F32)
    extra = extra_ref[...]
    coarse = extra.astype(BF16).astype(F32)
    index = iota((DEVS, LANES), 1) < ROUND
    high = jnp.where(index, layout[:, :LANES], coarse)
    low = jnp.where(index, layout[:, LANES:], extra - coarse)
    row_ref[:, 0:1, :] = high.reshape(DEVS, 1, LANES)
    row_ref[:, 1:2, :] = low.reshape(DEVS, 1, LANES)
    row_ref[:, 2:8, :] = jnp.broadcast_to(rounds.reshape(1, 1, 1), (DEVS, 6, LANES))


def route(round_index, ids, train_map, extra):
    bag = ids.shape[0] - 4
    return pl.pallas_call(
        route_kernel,
        in_specs=[pl.BlockSpec(memory_space=pltpu.SMEM)]
        + [pl.BlockSpec(memory_space=pltpu.VMEM)] * 3,
        out_specs=[pl.BlockSpec(memory_space=pltpu.VMEM)] * 3,
        out_shape=(
            jax.ShapeDtypeStruct((bag, ids.shape[1]), I32),
            jax.ShapeDtypeStruct((DEVS, LANES), F32),
            jax.ShapeDtypeStruct((DEVS, 8, LANES), F32),
        ),
        name="route",
    )(round_index, ids, train_map, extra)


def pack_kernel(
    slots_ref, place_ref, grads_ref, table_ref, moment_ref, head_ref, out_ref, from_ref, to_ref
):
    count = slots_ref.shape[0]
    bag = 32
    samples = count // bag
    block = 512

    def widen(i, carry):
        at = pl.multiple_of(i * block, block)
        from_ref[pl.ds(at, block), :] = grads_ref[pl.ds(at, block), :].astype(F32)
        to_ref[pl.ds(at * 2, block), :] = jnp.zeros((block, LANES), F32)
        to_ref[pl.ds(at * 2 + block, block), :] = jnp.zeros((block, LANES), F32)
        return carry

    def move(i, carry):
        first = (i & 3) * (bag * bag) + (i >> 2)
        for u in range(bag):
            slot = slots_ref[i * bag + u]
            to_ref[pl.ds(slot, 1), :] = from_ref[pl.ds(first + u * bag, 1), :]
        return carry

    half, odd = place_ref[0], place_ref[1]

    def rows_of(ref, i):
        base = half * (ref.shape[0] // 2) + i * 4
        starts = [base + ((u + odd) & 1) * (LANES // 2) + u // 2 for u in range(8)]
        rows = [ref[pl.ds(start, 8, stride=LANES), :] for start in starts]
        return jnp.concatenate([r.reshape(1, 8, LANES) for r in rows], axis=0)

    def narrow(i, carry):
        at = pl.multiple_of(i * 8, 8)
        rows = to_ref[pl.ds(pl.multiple_of(i * block, block), block), :].astype(BF16)
        table = rows_of(table_ref, i)
        coarse = table.astype(BF16).astype(F32)
        state = jnp.concatenate([coarse, table - coarse], axis=1).astype(BF16)
        more = jnp.concatenate([rows_of(moment_ref, i), head_ref[pl.ds(at, 8)]], axis=1)
        out_ref[pl.ds(at, 8), 0:ROUND, :] = rows.reshape(8, ROUND, LANES)
        out_ref[pl.ds(at, 8), ROUND : ROUND + 16, :] = state
        out_ref[pl.ds(at, 8), ROUND + 16 : ROUND + 32, :] = more.astype(BF16)
        return carry

    lax.fori_loop(0, bag * samples // block, widen, 0)
    lax.fori_loop(0, count // bag, move, 0)
    lax.fori_loop(0, DEVS // 8, narrow, 0)


def pack(slots, place, grads, table, moment, head):
    return pl.pallas_call(
        pack_kernel,
        in_specs=[pl.BlockSpec(memory_space=pltpu.SMEM)] * 2
        + [pl.BlockSpec(memory_space=pltpu.VMEM)] * 4,
        out_specs=pl.BlockSpec(memory_space=pltpu.VMEM),
        out_shape=jax.ShapeDtypeStruct((DEVS, SENT, LANES), BF16),
        scratch_shapes=[
            pltpu.VMEM(grads.shape, F32),
            pltpu.VMEM((DEVS * ROUND + 8, LANES), F32),
        ],
        name="pack",
    )(slots.reshape(-1), place, grads, table, moment, head)


def pair_up(line, low):
    other = pltpu.roll(line, ROUND, 1)
    half = DEVS // 2
    left = (line if low else other)[:half]
    right = (other if low else line)[half:]
    return jnp.where(iota((half, LANES), 1) < ROUND, left, right).astype(I32)


def add_rows(index_ref, left_ref, right_ref, acc_ref, with_count):
    step = pl.program_id(0)
    turns = left_ref.shape[0] // PAIRS

    def add(i, carry):
        at = pl.ds(pl.multiple_of(i * PAIRS, PAIRS), PAIRS)
        pieces = pl.ds(pl.multiple_of((step * turns + i) * PAIRS, PAIRS), PAIRS)
        index = index_ref[pieces, :]
        index = jnp.concatenate([index[u : u + 1] for u in range(PAIRS)], axis=1)
        left, right = left_ref[at], right_ref[at]
        rows = jnp.concatenate([p[u] for u in range(PAIRS) for p in (left, right)], axis=0)
        if with_count:
            rows = jnp.concatenate([rows, jnp.ones_like(rows)], axis=1)
        hit = hot_rows(acc_ref.shape[0], index)
        acc_ref[...] = acc_ref[...] + jnp.dot(hit, rows, preferred_element_type=F32)
        return carry

    lax.fori_loop(0, turns, add, 0)


PAIRS = 16
STEPS = 4


def half_spec(second):
    count = DEVS // 2 // STEPS
    return pl.BlockSpec((count, ROUND, LANES), lambda i: (i + second * STEPS, 0, 0))


def whole(shape, at=None):
    place = at if at is not None else (0,) * len(shape)
    return pl.BlockSpec(shape, lambda i: place)


STATE_SPEC = whole((DEVS, 32, LANES), (0, ROUND // 32, 0))


def line_of(state_ref):
    high = state_ref[:, 24:25, :].astype(F32).reshape(DEVS, LANES)
    low = state_ref[:, 25:26, :].astype(F32).reshape(DEVS, LANES)
    return high * 32.0 + low - 1.0


def adam(core, state_ref, acc_ref, new_ref, sums_ref, spots_ref):
    def step(i, carry):
        at = pl.multiple_of(i * LANES, LANES)
        part = pl.ds(i * 16, 16)
        total = acc_ref[pl.ds(at, LANES), :]
        shape = (16, 8, LANES)
        grad = total[:, :LANES].reshape(shape)
        touched = (total[:, LANES:] > 0.5).reshape(shape)
        state = state_ref[part].astype(F32)
        table = state[:, 0:8, :] + state[:, 8:16, :]
        moment = state[:, 16:24, :]
        source = iota(shape, 0)
        within = iota(shape, 1)
        lane = iota(shape, 2)
        parity = (core + i * 8 + (source >> 1)) & 1
        own = (source & 1) * 16 + within * 2 + parity
        high = jnp.broadcast_to(state[:, 24:25, :], shape)
        extra = high + jnp.broadcast_to(state[:, 25:26, :], shape)
        var = jnp.sum(jnp.where(lane == ROUND + own, extra, 0.0), axis=2, keepdims=True)
        spot = jnp.sum(jnp.where(lane == ROUND + 32 + own, extra, 0.0), axis=2, keepdims=True)
        mean = jnp.sum(grad * grad, axis=2, keepdims=True) * (1.0 / LANES)
        new_var = beta_two * var + (1.0 - beta_two) * mean
        new_moment = beta_one * moment + (1.0 - beta_one) * grad
        new_table = table - learn_rate * new_moment / (jnp.sqrt(new_var) + epsilon)
        new_ref[pl.ds(at, LANES), :] = new_table.reshape(LANES, LANES).astype(BF16)
        sums_ref[part] = jnp.where(touched, grad, UNTOUCHED)
        spot = jnp.where(lane == source * 8 + within, jnp.where(touched, spot, 4096.0), 0.0)
        spot = jnp.sum(jnp.sum(spot, axis=0), axis=0, keepdims=True)
        spots_ref[pl.ds(i, 1), :] = spot.astype(I32)
        return carry

    lax.fori_loop(0, 8, step, 0)


def update_kernel(
    core_ref,
    state_ref,
    left_ref,
    right_ref,
    new_ref,
    sums_ref,
    spots_ref,
    acc_ref,
    line_ref,
    rounds_ref,
    index_ref,
):
    @pl.when(pl.program_id(0) == 0)
    def _():
        line = line_of(state_ref)
        line_ref[...] = line
        index_ref[...] = pair_up(line, True)
        rounds = state_ref[:, 26:27, :].astype(F32).reshape(DEVS, LANES)
        rounds_ref[0] = jnp.max(rounds).astype(I32)
        acc_ref[...] = jnp.zeros(acc_ref.shape, F32)

    add_rows(index_ref, left_ref, right_ref, acc_ref, True)

    @pl.when(pl.program_id(0) == STEPS - 1)
    def _():
        adam(core_ref[0], state_ref, acc_ref, new_ref, sums_ref, spots_ref)


def updated_shapes(rows):
    return (
        jax.ShapeDtypeStruct((rows, LANES), BF16),
        jax.ShapeDtypeStruct((DEVS, 8, LANES), F32),
        jax.ShapeDtypeStruct((8, LANES), I32),
    )


def updated_specs(rows):
    return [whole((rows, LANES)), whole((DEVS, 8, LANES)), whole((8, LANES))]


def update(core, received, rows):
    return pl.pallas_call(
        update_kernel,
        grid=(STEPS,),
        in_specs=[
            pl.BlockSpec(memory_space=pltpu.SMEM),
            STATE_SPEC,
            half_spec(0),
            half_spec(1),
        ],
        out_specs=updated_specs(rows)
        + [
            whole((rows, 2 * LANES)),
            whole((DEVS, LANES)),
            pl.BlockSpec(memory_space=pltpu.SMEM),
        ],
        out_shape=updated_shapes(rows)
        + (
            jax.ShapeDtypeStruct((rows, 2 * LANES), F32),
            jax.ShapeDtypeStruct((DEVS, LANES), F32),
            jax.ShapeDtypeStruct((1,), I32),
        ),
        scratch_shapes=[pltpu.VMEM((DEVS // 2, LANES), I32)],
        name="update",
    )(core, received, received, received)


def adam_kernel(core_ref, state_ref, acc_ref, new_ref, sums_ref, spots_ref):
    adam(core_ref[0], state_ref, acc_ref, new_ref, sums_ref, spots_ref)


def adam_again(core, received, acc):
    rows = acc.shape[0]
    return pl.pallas_call(
        adam_kernel,
        grid=(1,),
        in_specs=[pl.BlockSpec(memory_space=pltpu.SMEM), STATE_SPEC, whole(acc.shape)],
        out_specs=updated_specs(rows),
        out_shape=updated_shapes(rows),
        name="adam",
    )(core, received, acc)


def more_kernel(line_ref, left_ref, right_ref, start_ref, out_ref, index_ref, *, low, with_count):
    @pl.when(pl.program_id(0) == 0)
    def _():
        index_ref[...] = pair_up(line_ref[...], low)
        out_ref[...] = start_ref[...]

    add_rows(index_ref, left_ref, right_ref, out_ref, with_count)


def more_rows(line, rows, start, low, with_count):
    return pl.pallas_call(
        functools.partial(more_kernel, low=low, with_count=with_count),
        grid=(STEPS,),
        in_specs=[whole(line.shape), half_spec(0), half_spec(1), whole(start.shape)],
        out_specs=whole(start.shape),
        out_shape=jax.ShapeDtypeStruct(start.shape, F32),
        scratch_shapes=[pltpu.VMEM((DEVS // 2, LANES), I32)],
        name="more_rows",
    )(line, rows, rows, start)


def reply_kernel(line_ref, new_ref, out_ref, turned_ref, table_ref):
    turned_ref[...] = line_ref[...].T
    part = new_ref.shape[0] // 4
    table_ref[...] = jnp.concatenate(
        [new_ref[k * part : (k + 1) * part, :] for k in range(4)], axis=1
    )

    def look(i, carry):
        turned = pltpu.roll(turned_ref[0:ROUND, :], LANES - i * 32, 1).astype(I32)
        within = turned & (part - 1)
        hit = jnp.concatenate(
            [one_hot(iota((ROUND, part), 1) == within[:, u : u + 1]) for u in range(32)], axis=0
        )
        found = jnp.dot(hit, table_ref[...], preferred_element_type=F32)
        for u in range(32):
            piece = found[u * ROUND : (u + 1) * ROUND]
            row = jnp.broadcast_to(turned[:, u : u + 1], (ROUND, LANES))
            low = jnp.where(row < part, piece[:, :LANES], piece[:, LANES : 2 * LANES])
            high = jnp.where(
                row < 3 * part, piece[:, 2 * LANES : 3 * LANES], piece[:, 3 * LANES :]
            )
            out_ref[i * 32 + u] = jnp.where(row < 2 * part, low, high).astype(BF16)
        return carry

    lax.fori_loop(0, DEVS // 32, look, 0)


def reply(line, new_rows):
    return pl.pallas_call(
        reply_kernel,
        in_specs=[pl.BlockSpec(memory_space=pltpu.VMEM)] * 2,
        out_specs=pl.BlockSpec(memory_space=pltpu.VMEM),
        out_shape=jax.ShapeDtypeStruct((DEVS, ROUND, LANES), BF16),
        scratch_shapes=[
            pltpu.VMEM((DEVS, LANES), F32),
            pltpu.VMEM((new_rows.shape[0] // 4, 4 * LANES), BF16),
        ],
        name="reply",
    )(line, new_rows)


def score_kernel(
    keys_ref,
    left_ref,
    right_ref,
    start_ref,
    first_ref,
    second_ref,
    score_ref,
    out_ref,
    index_ref,
    acc_ref,
):
    @pl.when(pl.program_id(0) == 0)
    def _():
        index_ref[...] = pair_up(keys_ref[...], False)
        acc_ref[...] = start_ref[...]

    add_rows(index_ref, left_ref, right_ref, acc_ref, False)

    @pl.when(pl.program_id(0) == STEPS - 1)
    def _():
        samples = out_ref.shape[1]
        pooled = jnp.concatenate(
            [acc_ref[f * samples : (f + 1) * samples, :] for f in range(4)], axis=1
        ).astype(BF16)
        hidden = jnp.dot(pooled, first_ref[...], preferred_element_type=F32)
        hidden = jnp.maximum(hidden, 0.0).astype(BF16)
        hidden = jnp.dot(hidden, second_ref[...], preferred_element_type=F32)
        hidden = jnp.maximum(hidden, 0.0).astype(BF16)
        weights = jnp.broadcast_to(score_ref[...], (16, score_ref.shape[1]))
        scores = lax.dot_general(
            weights, hidden, (((1,), (1,)), ((), ())), preferred_element_type=F32
        )
        out_ref[...] = scores[0:1, :]


def score(keys, rows, start, w_first, w_second, w_score):
    samples = start.shape[0] // 4
    return pl.pallas_call(
        score_kernel,
        grid=(STEPS,),
        in_specs=[whole(keys.shape), half_spec(0), half_spec(1), whole(start.shape)]
        + [whole(w.shape) for w in (w_first, w_second, w_score)],
        out_specs=whole((1, samples)),
        out_shape=jax.ShapeDtypeStruct((1, samples), F32),
        scratch_shapes=[
            pltpu.VMEM((DEVS // 2, LANES), I32),
            pltpu.VMEM(start.shape, F32),
        ],
        name="score",
    )(keys, rows, rows, start, w_first, w_second, w_score)


def exchange(value):
    return lax.all_to_all(value, ALL, 0, 0, tiled=True)


def place_kernel(old_ref, own_ref, other_ref, own_at_ref, other_at_ref, out_ref):
    block = 512

    def place(i, carry):
        at = pl.ds(pl.multiple_of(i * block, block), block)
        total = jnp.zeros((block, 2 * LANES), F32)
        for at_ref, rows_ref in ((own_at_ref, own_ref), (other_at_ref, other_ref)):
            spots = at_ref[...] - i * block
            spots = jnp.where((spots >= 0) & (spots < block), spots, -1)
            spots = jnp.concatenate([spots[u : u + 1] for u in range(8)], axis=1)
            rows = rows_ref[...]
            rows = jnp.concatenate([rows, jnp.ones_like(rows)], axis=1)
            total = total + jnp.dot(hot_rows(block, spots), rows, preferred_element_type=F32)
        fresh = total[:, :LANES].astype(BF16).astype(F32)
        old = old_ref[at, :].astype(F32)
        out_ref[at, :] = jnp.where(total[:, LANES:] > 0.5, fresh, old).astype(BF16)
        return carry

    lax.fori_loop(0, old_ref.shape[0] // block, place, 0)


def place_rows(old, own, other, own_at, other_at):
    return pl.pallas_call(
        place_kernel,
        in_specs=[pl.BlockSpec(memory_space=pltpu.VMEM)] * 5,
        out_specs=pl.BlockSpec(memory_space=pltpu.VMEM),
        out_shape=jax.ShapeDtypeStruct(old.shape, BF16),
        name="place",
    )(old, own, other, own_at, other_at)


def per_device(
    touched_ids,
    bag_lengths,
    train_map,
    serve_map,
    slot_grads,
    table,
    moment,
    row_var,
    serving_old,
    w_first,
    w_second,
    w_score,
):
    owners = lax.axis_size("shard")
    owner = lax.axis_index("shard")
    rep = lax.axis_index("rep")
    tab_rows, row_width = table.shape
    samples, bag = touched_ids.shape
    swap = [(0, 1), (1, 0)]
    odd = owner % 2 == 1
    rows_here = tab_rows // 2

    ids = jnp.concatenate([touched_ids, bag_lengths], axis=1).T
    map_rows = train_map.reshape(-1, LANES)
    grads = slot_grads.reshape(samples * bag, row_width)

    spots = (serve_map % tab_rows).astype(F32).reshape(tab_rows // owners, owners).T
    spread = jnp.concatenate([row_var.reshape(tab_rows // owners, owners).T, spots], axis=1)
    spread = jnp.broadcast_to(spread[:, None, :], (owners, 2, 2 * tab_rows // owners))
    extra = jnp.concatenate([jnp.zeros((DEVS, ROUND), F32), spread.reshape(DEVS, -1)], axis=1)

    place = jnp.stack([rep, owner % 2]).astype(I32)
    slots, keys, head = route(jnp.zeros((1,), I32), ids, map_rows, extra)
    received = exchange(pack(slots, place, grads, table, moment, head))
    core = rep.reshape(1).astype(I32)
    new_rows, sums, places, acc, line, rounds = update(core, received, rows_here)
    rounds = rounds[0]
    one = jnp.ones((), I32)

    def more_sums(carry):
        k, acc = carry[0], carry[1]
        slots, _, head = route(k.reshape(1), ids, map_rows, extra)
        got = exchange(pack(slots, place, grads, table, moment, head))
        line = got[:, ROUND + 24].astype(F32) * 32.0 + got[:, ROUND + 25].astype(F32) - 1.0
        acc = more_rows(line, got, acc, True, True)
        return (k + 1, acc) + tuple(adam_again(core, received, acc))

    _, _, new_rows, sums, places = lax.while_loop(
        lambda c: c[0] < rounds, more_sums, (one, acc, new_rows, sums, places)
    )

    back = exchange(sums)
    answer = exchange(reply(line, new_rows))

    other_rows = lax.ppermute(new_rows, "rep", swap)
    other_places = lax.ppermute(places, "rep", swap)
    serving_table = place_rows(serving_old, new_rows, other_rows, places, other_places)

    back = back.reshape(owners, 2, 8, row_width)
    back = jnp.where(odd, back[:, ::-1], back)
    half = back.transpose(2, 1, 0, 3).reshape(rows_here, row_width)
    other = lax.ppermute(half, "rep", swap)
    grad_sum = jnp.where(
        rep == 0, jnp.concatenate([half, other]), jnp.concatenate([other, half])
    )
    touched = grad_sum[:, :1] < 0.5 * UNTOUCHED
    new_moment = jnp.where(touched, beta_one * moment + (1.0 - beta_one) * grad_sum, moment)
    mean = jnp.mean(jnp.where(touched, grad_sum * grad_sum, 0.0), axis=1)
    new_var = jnp.where(touched[:, 0], beta_two * row_var + (1.0 - beta_two) * mean, row_var)
    new_table = jnp.where(
        touched, table - learn_rate * new_moment / (jnp.sqrt(new_var)[:, None] + epsilon), table
    )

    def more_pooled(carry):
        k, acc = carry
        _, keys, head = route(k.reshape(1), ids, map_rows, extra)
        got = exchange(head)
        line = got[:, 0] * 32.0 + got[:, 1] - 1.0
        return (k + 1, more_rows(keys, exchange(reply(line, new_rows)), acc, False, False))

    rounds, _ = lax.optimization_barrier((rounds, answer[0, 0, 0]))
    _, pooled = lax.while_loop(
        lambda c: c[0] < rounds,
        more_pooled,
        (one, jnp.zeros((4 * samples, row_width), F32)),
    )
    scores = score(keys, answer, pooled, w_first, w_second, w_score.reshape(1, -1))
    return (new_table, new_moment, new_var, serving_table, scores.reshape(samples))


def solution(mesh):
    in_specs = (
        P(("shard", "rep"), None),
        P(("shard", "rep"), None),
        P(),
        P("shard"),
        P(("shard", "rep"), None, None),
        P("shard", None),
        P("shard", None),
        P("shard"),
        P("shard", None),
        P(),
        P(),
        P(),
    )
    out_specs = (
        P("shard", None),
        P("shard", None),
        P("shard"),
        P("shard", None),
        P(("shard", "rep")),
    )
    return jax.shard_map(
        per_device, mesh=mesh, in_specs=in_specs, out_specs=out_specs, check_vma=False
    )
```

```python
import functools

import jax
import jax.numpy as jnp
from jax import lax
from jax.experimental import pallas as pl
from jax.experimental.pallas import tpu as pltpu
from jax.sharding import PartitionSpec as P

beta_one = 0.9
beta_two = 0.999
learn_rate = 0.1
epsilon = 1e-06

ROUND = 64
DEVS = 128
LANES = 128
UNTOUCHED = 1e30
F32 = jnp.float32
BF16 = jnp.bfloat16
I32 = jnp.int32
ALL = ("shard", "rep")
SENT = ROUND + 32


def iota(shape, dim):
    return lax.broadcasted_iota(I32, shape, dim)


def one_hot(mask):
    return jnp.where(mask, 1.0, 0.0).astype(BF16)


def hot_rows(count, index):
    index = index.astype(jnp.int16)
    place = iota((count, index.shape[1]), 0).astype(jnp.int16)
    return jnp.where(place == index, jnp.bfloat16(1), jnp.bfloat16(0))


def route_kernel(round_ref, ids_ref, map_ref, extra_ref, slots_ref, keys_ref, row_ref):
    bag, samples = ids_ref.shape[0] - 4, ids_ref.shape[1]
    step = 4
    wide = step * samples
    first = round_ref[0] * ROUND
    table = map_ref[...]
    high = (table >> 9).astype(F32).T
    low = ((table & 511) - 256).astype(F32).T
    parts = jnp.concatenate([high, low], axis=0).astype(BF16)
    upto = one_hot(iota((wide, wide), 0) <= iota((wide, wide), 1))
    ends = []
    total = jnp.zeros((1, samples), I32)
    for f in range(3):
        total = total + ids_ref[bag + f : bag + f + 1, :]
        ends.append(total)
    sample = iota((1, samples), 1)
    seen = jnp.zeros((DEVS, 1), F32)
    layout = jnp.zeros((DEVS, 4 * ROUND), F32)
    for t in range(0, bag, step):
        ids = jnp.concatenate([ids_ref[t + u : t + u + 1, :] for u in range(step)], axis=1)
        keys = []
        for u in range(step):
            field = sum((jnp.where(e <= t + u, 1, 0) for e in ends), jnp.zeros((1, samples), I32))
            keys.append(field * samples + sample)
        key = jnp.concatenate(keys, axis=1) + 1
        hit = hot_rows(table.shape[0], ids >> 7)
        both = jnp.dot(parts, hit, preferred_element_type=F32)
        value = both[:LANES] * 512.0 + both[LANES:] + 256.0
        value = jnp.where(iota((LANES, wide), 0) == (ids & 127), value, 0.0)
        position = jnp.sum(value, axis=0, keepdims=True).astype(I32)
        owner = position >> 11
        stride = (position >> 6) & 31
        dest = (position & 63) * 2 + ((stride + owner) & 1)
        local = owner * 16 + (stride >> 1) + 1
        mine = iota((DEVS, wide), 0) == dest
        hot = one_hot(mine)
        running = jnp.dot(hot, upto, preferred_element_type=F32)
        rank = jnp.sum(jnp.where(mine, running + seen, 0.0), axis=0, keepdims=True)
        seen = seen + running[:, wide - 1 : wide]
        rank = rank.astype(I32) - 1 - first
        here = iota((ROUND, wide), 0) == rank
        columns = jnp.concatenate(
            [
                jnp.where(here, v.astype(F32), 0.0)
                for v in (local >> 5, key >> 5, local & 31, key & 31)
            ],
            axis=0,
        ).astype(BF16)
        layout = layout + lax.dot_general(
            hot, columns, (((1,), (1,)), ((), ())), preferred_element_type=F32
        )
        fits = (rank >= 0) & (rank < ROUND)
        slot = jnp.where(fits, dest * ROUND + rank, DEVS * ROUND)
        for u in range(step):
            slots_ref[t + u : t + u + 1, :] = slot[:, u * samples : (u + 1) * samples]
    keys_ref[...] = layout[:, :LANES] * 32.0 + layout[:, LANES:] - 1.0
    most = jnp.max(seen, axis=0, keepdims=True).astype(I32)
    rounds = ((most + ROUND - 1) // ROUND).astype(F32)
    extra = extra_ref[...]
    coarse = extra.astype(BF16).astype(F32)
    index = iota((DEVS, LANES), 1) < ROUND
    high = jnp.where(index, layout[:, :LANES], coarse)
    low = jnp.where(index, layout[:, LANES:], extra - coarse)
    row_ref[:, 0:1, :] = high.reshape(DEVS, 1, LANES)
    row_ref[:, 1:2, :] = low.reshape(DEVS, 1, LANES)
    row_ref[:, 2:8, :] = jnp.broadcast_to(rounds.reshape(1, 1, 1), (DEVS, 6, LANES))


def route(round_index, ids, train_map, extra):
    bag = ids.shape[0] - 4
    return pl.pallas_call(
        route_kernel,
        in_specs=[pl.BlockSpec(memory_space=pltpu.SMEM)]
        + [pl.BlockSpec(memory_space=pltpu.VMEM)] * 3,
        out_specs=[pl.BlockSpec(memory_space=pltpu.VMEM)] * 3,
        out_shape=(
            jax.ShapeDtypeStruct((bag, ids.shape[1]), I32),
            jax.ShapeDtypeStruct((DEVS, LANES), F32),
            jax.ShapeDtypeStruct((DEVS, 8, LANES), F32),
        ),
        name="route",
    )(round_index, ids, train_map, extra)


def pack_kernel(
    slots_ref, place_ref, grads_ref, table_ref, moment_ref, head_ref, out_ref, from_ref, to_ref
):
    count = slots_ref.shape[0]
    bag = 32
    samples = count // bag
    block = 512

    def widen(i, carry):
        at = pl.multiple_of(i * block, block)
        from_ref[pl.ds(at, block), :] = grads_ref[pl.ds(at, block), :].astype(F32)
        to_ref[pl.ds(at * 2, block), :] = jnp.zeros((block, LANES), F32)
        to_ref[pl.ds(at * 2 + block, block), :] = jnp.zeros((block, LANES), F32)
        return carry

    def move(i, carry):
        first = (i & 3) * (bag * bag) + (i >> 2)
        for u in range(bag):
            slot = slots_ref[i * bag + u]
            to_ref[pl.ds(slot, 1), :] = from_ref[pl.ds(first + u * bag, 1), :]
        return carry

    half, odd = place_ref[0], place_ref[1]

    def rows_of(ref, i):
        base = half * (ref.shape[0] // 2) + i * 4
        starts = [base + ((u + odd) & 1) * (LANES // 2) + u // 2 for u in range(8)]
        rows = [ref[pl.ds(start, 8, stride=LANES), :] for start in starts]
        return jnp.concatenate([r.reshape(1, 8, LANES) for r in rows], axis=0)

    def narrow(i, carry):
        at = pl.multiple_of(i * 8, 8)
        rows = to_ref[pl.ds(pl.multiple_of(i * block, block), block), :].astype(BF16)
        table = rows_of(table_ref, i)
        coarse = table.astype(BF16).astype(F32)
        state = jnp.concatenate([coarse, table - coarse], axis=1).astype(BF16)
        more = jnp.concatenate([rows_of(moment_ref, i), head_ref[pl.ds(at, 8)]], axis=1)
        out_ref[pl.ds(at, 8), 0:ROUND, :] = rows.reshape(8, ROUND, LANES)
        out_ref[pl.ds(at, 8), ROUND : ROUND + 16, :] = state
        out_ref[pl.ds(at, 8), ROUND + 16 : ROUND + 32, :] = more.astype(BF16)
        return carry

    lax.fori_loop(0, bag * samples // block, widen, 0)
    lax.fori_loop(0, count // bag, move, 0)
    lax.fori_loop(0, DEVS // 8, narrow, 0)


def pack(slots, place, grads, table, moment, head):
    return pl.pallas_call(
        pack_kernel,
        in_specs=[pl.BlockSpec(memory_space=pltpu.SMEM)] * 2
        + [pl.BlockSpec(memory_space=pltpu.VMEM)] * 4,
        out_specs=pl.BlockSpec(memory_space=pltpu.VMEM),
        out_shape=jax.ShapeDtypeStruct((DEVS, SENT, LANES), BF16),
        scratch_shapes=[
            pltpu.VMEM(grads.shape, F32),
            pltpu.VMEM((DEVS * ROUND + 8, LANES), F32),
        ],
        name="pack",
    )(slots.reshape(-1), place, grads, table, moment, head)


def pair_up(line, low):
    other = pltpu.roll(line, ROUND, 1)
    half = DEVS // 2
    left = (line if low else other)[:half]
    right = (other if low else line)[half:]
    return jnp.where(iota((half, LANES), 1) < ROUND, left, right).astype(I32)


def add_rows(index_ref, left_ref, right_ref, acc_ref, with_count):
    step = pl.program_id(0)
    turns = left_ref.shape[0] // PAIRS

    def add(i, carry):
        at = pl.ds(pl.multiple_of(i * PAIRS, PAIRS), PAIRS)
        pieces = pl.ds(pl.multiple_of((step * turns + i) * PAIRS, PAIRS), PAIRS)
        index = index_ref[pieces, :]
        index = jnp.concatenate([index[u : u + 1] for u in range(PAIRS)], axis=1)
        left, right = left_ref[at], right_ref[at]
        rows = jnp.concatenate([p[u] for u in range(PAIRS) for p in (left, right)], axis=0)
        if with_count:
            rows = jnp.concatenate([rows, jnp.ones_like(rows)], axis=1)
        hit = hot_rows(acc_ref.shape[0], index)
        acc_ref[...] = acc_ref[...] + jnp.dot(hit, rows, preferred_element_type=F32)
        return carry

    lax.fori_loop(0, turns, add, 0)


PAIRS = 16
STEPS = 4


def half_spec(second):
    count = DEVS // 2 // STEPS
    return pl.BlockSpec((count, ROUND, LANES), lambda i: (i + second * STEPS, 0, 0))


def whole(shape, at=None):
    place = at if at is not None else (0,) * len(shape)
    return pl.BlockSpec(shape, lambda i: place)


STATE_SPEC = whole((DEVS, 32, LANES), (0, ROUND // 32, 0))


def line_of(state_ref):
    high = state_ref[:, 24:25, :].astype(F32).reshape(DEVS, LANES)
    low = state_ref[:, 25:26, :].astype(F32).reshape(DEVS, LANES)
    return high * 32.0 + low - 1.0


def adam(core, state_ref, acc_ref, new_ref, sums_ref, spots_ref):
    def step(i, carry):
        at = pl.multiple_of(i * LANES, LANES)
        part = pl.ds(i * 16, 16)
        total = acc_ref[pl.ds(at, LANES), :]
        shape = (16, 8, LANES)
        grad = total[:, :LANES].reshape(shape)
        touched = (total[:, LANES:] > 0.5).reshape(shape)
        state = state_ref[part].astype(F32)
        table = state[:, 0:8, :] + state[:, 8:16, :]
        moment = state[:, 16:24, :]
        source = iota(shape, 0)
        within = iota(shape, 1)
        lane = iota(shape, 2)
        parity = (core + i * 8 + (source >> 1)) & 1
        own = (source & 1) * 16 + within * 2 + parity
        high = jnp.broadcast_to(state[:, 24:25, :], shape)
        extra = high + jnp.broadcast_to(state[:, 25:26, :], shape)
        var = jnp.sum(jnp.where(lane == ROUND + own, extra, 0.0), axis=2, keepdims=True)
        spot = jnp.sum(jnp.where(lane == ROUND + 32 + own, extra, 0.0), axis=2, keepdims=True)
        mean = jnp.sum(grad * grad, axis=2, keepdims=True) * (1.0 / LANES)
        new_var = beta_two * var + (1.0 - beta_two) * mean
        new_moment = beta_one * moment + (1.0 - beta_one) * grad
        new_table = table - learn_rate * new_moment / (jnp.sqrt(new_var) + epsilon)
        new_ref[pl.ds(at, LANES), :] = new_table.reshape(LANES, LANES).astype(BF16)
        sums_ref[part] = jnp.where(touched, grad, UNTOUCHED)
        spot = jnp.where(lane == source * 8 + within, jnp.where(touched, spot, 4096.0), 0.0)
        spot = jnp.sum(jnp.sum(spot, axis=0), axis=0, keepdims=True)
        spots_ref[pl.ds(i, 1), :] = spot.astype(I32)
        return carry

    lax.fori_loop(0, 8, step, 0)


def update_kernel(
    core_ref,
    state_ref,
    left_ref,
    right_ref,
    new_ref,
    sums_ref,
    spots_ref,
    acc_ref,
    line_ref,
    rounds_ref,
    index_ref,
):
    @pl.when(pl.program_id(0) == 0)
    def _():
        line = line_of(state_ref)
        line_ref[...] = line
        index_ref[...] = pair_up(line, True)
        rounds = state_ref[:, 26:27, :].astype(F32).reshape(DEVS, LANES)
        rounds_ref[0] = jnp.max(rounds).astype(I32)
        acc_ref[...] = jnp.zeros(acc_ref.shape, F32)

    add_rows(index_ref, left_ref, right_ref, acc_ref, True)

    @pl.when(pl.program_id(0) == STEPS - 1)
    def _():
        adam(core_ref[0], state_ref, acc_ref, new_ref, sums_ref, spots_ref)


def updated_shapes(rows):
    return (
        jax.ShapeDtypeStruct((rows, LANES), BF16),
        jax.ShapeDtypeStruct((DEVS, 8, LANES), F32),
        jax.ShapeDtypeStruct((8, LANES), I32),
    )


def updated_specs(rows):
    return [whole((rows, LANES)), whole((DEVS, 8, LANES)), whole((8, LANES))]


def update(core, received, rows):
    return pl.pallas_call(
        update_kernel,
        grid=(STEPS,),
        in_specs=[
            pl.BlockSpec(memory_space=pltpu.SMEM),
            STATE_SPEC,
            half_spec(0),
            half_spec(1),
        ],
        out_specs=updated_specs(rows)
        + [
            whole((rows, 2 * LANES)),
            whole((DEVS, LANES)),
            pl.BlockSpec(memory_space=pltpu.SMEM),
        ],
        out_shape=updated_shapes(rows)
        + (
            jax.ShapeDtypeStruct((rows, 2 * LANES), F32),
            jax.ShapeDtypeStruct((DEVS, LANES), F32),
            jax.ShapeDtypeStruct((1,), I32),
        ),
        scratch_shapes=[pltpu.VMEM((DEVS // 2, LANES), I32)],
        name="update",
    )(core, received, received, received)


def adam_kernel(core_ref, state_ref, acc_ref, new_ref, sums_ref, spots_ref):
    adam(core_ref[0], state_ref, acc_ref, new_ref, sums_ref, spots_ref)


def adam_again(core, received, acc):
    rows = acc.shape[0]
    return pl.pallas_call(
        adam_kernel,
        grid=(1,),
        in_specs=[pl.BlockSpec(memory_space=pltpu.SMEM), STATE_SPEC, whole(acc.shape)],
        out_specs=updated_specs(rows),
        out_shape=updated_shapes(rows),
        name="adam",
    )(core, received, acc)


def more_kernel(line_ref, left_ref, right_ref, start_ref, out_ref, index_ref, *, low, with_count):
    @pl.when(pl.program_id(0) == 0)
    def _():
        index_ref[...] = pair_up(line_ref[...], low)
        out_ref[...] = start_ref[...]

    add_rows(index_ref, left_ref, right_ref, out_ref, with_count)


def more_rows(line, rows, start, low, with_count):
    return pl.pallas_call(
        functools.partial(more_kernel, low=low, with_count=with_count),
        grid=(STEPS,),
        in_specs=[whole(line.shape), half_spec(0), half_spec(1), whole(start.shape)],
        out_specs=whole(start.shape),
        out_shape=jax.ShapeDtypeStruct(start.shape, F32),
        scratch_shapes=[pltpu.VMEM((DEVS // 2, LANES), I32)],
        name="more_rows",
    )(line, rows, rows, start)


def reply_kernel(line_ref, new_ref, out_ref, turned_ref, table_ref):
    turned_ref[...] = line_ref[...].T
    part = new_ref.shape[0] // 4
    table_ref[...] = jnp.concatenate(
        [new_ref[k * part : (k + 1) * part, :] for k in range(4)], axis=1
    )

    def look(i, carry):
        turned = pltpu.roll(turned_ref[0:ROUND, :], LANES - i * 32, 1).astype(I32)
        within = turned & (part - 1)
        hit = jnp.concatenate(
            [one_hot(iota((ROUND, part), 1) == within[:, u : u + 1]) for u in range(32)], axis=0
        )
        found = jnp.dot(hit, table_ref[...], preferred_element_type=F32)
        for u in range(32):
            piece = found[u * ROUND : (u + 1) * ROUND]
            row = jnp.broadcast_to(turned[:, u : u + 1], (ROUND, LANES))
            low = jnp.where(row < part, piece[:, :LANES], piece[:, LANES : 2 * LANES])
            high = jnp.where(
                row < 3 * part, piece[:, 2 * LANES : 3 * LANES], piece[:, 3 * LANES :]
            )
            out_ref[i * 32 + u] = jnp.where(row < 2 * part, low, high).astype(BF16)
        return carry

    lax.fori_loop(0, DEVS // 32, look, 0)


def reply(line, new_rows):
    return pl.pallas_call(
        reply_kernel,
        in_specs=[pl.BlockSpec(memory_space=pltpu.VMEM)] * 2,
        out_specs=pl.BlockSpec(memory_space=pltpu.VMEM),
        out_shape=jax.ShapeDtypeStruct((DEVS, ROUND, LANES), BF16),
        scratch_shapes=[
            pltpu.VMEM((DEVS, LANES), F32),
            pltpu.VMEM((new_rows.shape[0] // 4, 4 * LANES), BF16),
        ],
        name="reply",
    )(line, new_rows)


def score_kernel(
    keys_ref,
    left_ref,
    right_ref,
    start_ref,
    first_ref,
    second_ref,
    score_ref,
    out_ref,
    index_ref,
    acc_ref,
):
    @pl.when(pl.program_id(0) == 0)
    def _():
        index_ref[...] = pair_up(keys_ref[...], False)
        acc_ref[...] = start_ref[...]

    add_rows(index_ref, left_ref, right_ref, acc_ref, False)

    @pl.when(pl.program_id(0) == STEPS - 1)
    def _():
        samples = out_ref.shape[1]
        pooled = jnp.concatenate(
            [acc_ref[f * samples : (f + 1) * samples, :] for f in range(4)], axis=1
        ).astype(BF16)
        hidden = jnp.dot(pooled, first_ref[...], preferred_element_type=F32)
        hidden = jnp.maximum(hidden, 0.0).astype(BF16)
        hidden = jnp.dot(hidden, second_ref[...], preferred_element_type=F32)
        hidden = jnp.maximum(hidden, 0.0).astype(BF16)
        weights = jnp.broadcast_to(score_ref[...], (16, score_ref.shape[1]))
        scores = lax.dot_general(
            weights, hidden, (((1,), (1,)), ((), ())), preferred_element_type=F32
        )
        out_ref[...] = scores[0:1, :]


def score(keys, rows, start, w_first, w_second, w_score):
    samples = start.shape[0] // 4
    return pl.pallas_call(
        score_kernel,
        grid=(STEPS,),
        in_specs=[whole(keys.shape), half_spec(0), half_spec(1), whole(start.shape)]
        + [whole(w.shape) for w in (w_first, w_second, w_score)],
        out_specs=whole((1, samples)),
        out_shape=jax.ShapeDtypeStruct((1, samples), F32),
        scratch_shapes=[
            pltpu.VMEM((DEVS // 2, LANES), I32),
            pltpu.VMEM(start.shape, F32),
        ],
        name="score",
    )(keys, rows, rows, start, w_first, w_second, w_score)


def exchange(value):
    return lax.all_to_all(value, ALL, 0, 0, tiled=True)


def place_kernel(old_ref, own_ref, other_ref, own_at_ref, other_at_ref, out_ref):
    block = 512

    def place(i, carry):
        at = pl.ds(pl.multiple_of(i * block, block), block)
        total = jnp.zeros((block, 2 * LANES), F32)
        for at_ref, rows_ref in ((own_at_ref, own_ref), (other_at_ref, other_ref)):
            spots = at_ref[...] - i * block
            spots = jnp.where((spots >= 0) & (spots < block), spots, -1)
            spots = jnp.concatenate([spots[u : u + 1] for u in range(8)], axis=1)
            rows = rows_ref[...]
            rows = jnp.concatenate([rows, jnp.ones_like(rows)], axis=1)
            total = total + jnp.dot(hot_rows(block, spots), rows, preferred_element_type=F32)
        fresh = total[:, :LANES].astype(BF16).astype(F32)
        old = old_ref[at, :].astype(F32)
        out_ref[at, :] = jnp.where(total[:, LANES:] > 0.5, fresh, old).astype(BF16)
        return carry

    lax.fori_loop(0, old_ref.shape[0] // block, place, 0)


def place_rows(old, own, other, own_at, other_at):
    return pl.pallas_call(
        place_kernel,
        in_specs=[pl.BlockSpec(memory_space=pltpu.VMEM)] * 5,
        out_specs=pl.BlockSpec(memory_space=pltpu.VMEM),
        out_shape=jax.ShapeDtypeStruct(old.shape, BF16),
        name="place",
    )(old, own, other, own_at, other_at)


def send_home(value, owner):
    value = value.reshape(4, 4, 4, -1, LANES)
    for axis, unit in enumerate((16, 4, 1)):
        digit = (owner // unit) % 4
        out = value
        for k in range(1, 4):
            piece = lax.dynamic_index_in_dim(value, (digit + k) % 4, axis, keepdims=True)
            pairs = []
            for s in range(64):
                d = (s // unit) % 4
                pairs.append((s, s + ((d + k) % 4 - d) * unit))
            piece = lax.ppermute(piece, "shard", pairs)
            out = lax.dynamic_update_slice_in_dim(out, piece, (digit - k) % 4, axis)
        value = out
    return value.reshape(64, -1, LANES)


def per_device(
    touched_ids,
    bag_lengths,
    train_map,
    serve_map,
    slot_grads,
    table,
    moment,
    row_var,
    serving_old,
    w_first,
    w_second,
    w_score,
):
    owners = lax.axis_size("shard")
    owner = lax.axis_index("shard")
    rep = lax.axis_index("rep")
    tab_rows, row_width = table.shape
    samples, bag = touched_ids.shape
    swap = [(0, 1), (1, 0)]
    rows_here = tab_rows // 2

    ids = jnp.concatenate([touched_ids, bag_lengths], axis=1).T
    map_rows = train_map.reshape(-1, LANES)
    grads = slot_grads.reshape(samples * bag, row_width)

    spots = (serve_map % tab_rows).astype(F32).reshape(tab_rows // owners, owners).T
    spread = jnp.concatenate([row_var.reshape(tab_rows // owners, owners).T, spots], axis=1)
    spread = jnp.broadcast_to(spread[:, None, :], (owners, 2, 2 * tab_rows // owners))
    extra = jnp.concatenate([jnp.zeros((DEVS, ROUND), F32), spread.reshape(DEVS, -1)], axis=1)

    place = jnp.stack([rep, owner % 2]).astype(I32)
    slots, keys, head = route(jnp.zeros((1,), I32), ids, map_rows, extra)
    received = exchange(pack(slots, place, grads, table, moment, head))
    core = rep.reshape(1).astype(I32)
    new_rows, sums, places, acc, line, rounds = update(core, received, rows_here)
    rounds = rounds[0]
    one = jnp.ones((), I32)

    def more_sums(carry):
        k, acc = carry[0], carry[1]
        slots, _, head = route(k.reshape(1), ids, map_rows, extra)
        got = exchange(pack(slots, place, grads, table, moment, head))
        line = got[:, ROUND + 24].astype(F32) * 32.0 + got[:, ROUND + 25].astype(F32) - 1.0
        acc = more_rows(line, got, acc, True, True)
        return (k + 1, acc) + tuple(adam_again(core, received, acc))

    _, _, new_rows, sums, places = lax.while_loop(
        lambda c: c[0] < rounds, more_sums, (one, acc, new_rows, sums, places)
    )

    found = reply(line, new_rows)
    answer = exchange(found)

    other_rows = lax.ppermute(new_rows, "rep", swap)
    other_places = lax.ppermute(places, "rep", swap)
    serving_table = place_rows(serving_old, new_rows, other_rows, places, other_places)

    half = send_home(sums, owner).transpose(1, 0, 2)
    other = lax.ppermute(half, "rep", swap)
    even = (rep + owner) % 2 == 0
    grad_sum = jnp.stack([jnp.where(even, half, other), jnp.where(even, other, half)], axis=1)
    grad_sum = grad_sum.reshape(tab_rows, row_width)
    touched = grad_sum[:, :1] < 0.5 * UNTOUCHED
    new_moment = jnp.where(touched, beta_one * moment + (1.0 - beta_one) * grad_sum, moment)
    mean = jnp.mean(jnp.where(touched, grad_sum * grad_sum, 0.0), axis=1)
    new_var = jnp.where(touched[:, 0], beta_two * row_var + (1.0 - beta_two) * mean, row_var)
    new_table = jnp.where(
        touched, table - learn_rate * new_moment / (jnp.sqrt(new_var)[:, None] + epsilon), table
    )

    def more_pooled(carry):
        k, acc = carry
        _, keys, head = route(k.reshape(1), ids, map_rows, extra)
        got = exchange(head)
        line = got[:, 0] * 32.0 + got[:, 1] - 1.0
        return (k + 1, more_rows(keys, exchange(reply(line, new_rows)), acc, False, False))

    rounds, _ = lax.optimization_barrier((rounds, answer[0, 0, 0]))
    _, pooled = lax.while_loop(
        lambda c: c[0] < rounds,
        more_pooled,
        (one, jnp.zeros((4 * samples, row_width), F32)),
    )
    scores = score(keys, answer, pooled, w_first, w_second, w_score.reshape(1, -1))
    return (new_table, new_moment, new_var, serving_table, scores.reshape(samples))


def solution(mesh):
    in_specs = (
        P(("shard", "rep"), None),
        P(("shard", "rep"), None),
        P(),
        P("shard"),
        P(("shard", "rep"), None, None),
        P("shard", None),
        P("shard", None),
        P("shard"),
        P("shard", None),
        P(),
        P(),
        P(),
    )
    out_specs = (
        P("shard", None),
        P("shard", None),
        P("shard"),
        P("shard", None),
        P(("shard", "rep")),
    )
    return jax.shard_map(
        per_device, mesh=mesh, in_specs=in_specs, out_specs=out_specs, check_vma=False
    )
```

```python
import functools

import jax
import jax.numpy as jnp
from jax import lax
from jax.experimental import pallas as pl
from jax.experimental.pallas import tpu as pltpu
from jax.sharding import PartitionSpec as P

beta_one = 0.9
beta_two = 0.999
learn_rate = 0.1
epsilon = 1e-06

ROUND = 64
DEVS = 128
LANES = 128
UNTOUCHED = 1e30
F32 = jnp.float32
BF16 = jnp.bfloat16
I32 = jnp.int32
ALL = ("shard", "rep")
SENT = ROUND + 32


def iota(shape, dim):
    return lax.broadcasted_iota(I32, shape, dim)


def one_hot(mask):
    return jnp.where(mask, 1.0, 0.0).astype(BF16)


def hot_rows(count, index):
    index = index.astype(jnp.int16)
    place = iota((count, index.shape[1]), 0).astype(jnp.int16)
    return jnp.where(place == index, jnp.bfloat16(1), jnp.bfloat16(0))


def route_kernel(
    round_ref, ids_ref, lengths_ref, map_ref, var_ref, serve_ref, slots_ref, keys_ref, row_ref
):
    bag, samples = ids_ref.shape
    step = 4
    wide = step * samples
    first = round_ref[0] * ROUND
    table = map_ref[...]
    high = (table >> 9).astype(F32).T
    low = ((table & 511) - 256).astype(F32).T
    parts = jnp.concatenate([high, low], axis=0).astype(BF16)
    upto = one_hot(iota((wide, wide), 0) <= iota((wide, wide), 1))
    ends = []
    total = jnp.zeros((1, samples), I32)
    for f in range(3):
        total = total + lengths_ref[f : f + 1, :]
        ends.append(total)
    sample = iota((1, samples), 1)
    seen = jnp.zeros((DEVS, 1), F32)
    layout = jnp.zeros((DEVS, 4 * ROUND), F32)
    for t in range(0, bag, step):
        ids = jnp.concatenate([ids_ref[t + u : t + u + 1, :] for u in range(step)], axis=1)
        keys = []
        for u in range(step):
            field = sum((jnp.where(e <= t + u, 1, 0) for e in ends), jnp.zeros((1, samples), I32))
            keys.append(field * samples + sample)
        key = jnp.concatenate(keys, axis=1) + 1
        hit = hot_rows(table.shape[0], ids >> 7)
        both = jnp.dot(parts, hit, preferred_element_type=F32)
        value = both[:LANES] * 512.0 + both[LANES:] + 256.0
        value = jnp.where(iota((LANES, wide), 0) == (ids & 127), value, 0.0)
        position = jnp.sum(value, axis=0, keepdims=True).astype(I32)
        owner = position >> 11
        stride = (position >> 6) & 31
        dest = (position & 63) * 2 + ((stride + owner) & 1)
        local = owner * 16 + (stride >> 1) + 1
        mine = iota((DEVS, wide), 0) == dest
        hot = one_hot(mine)
        running = jnp.dot(hot, upto, preferred_element_type=F32)
        rank = jnp.sum(jnp.where(mine, running + seen, 0.0), axis=0, keepdims=True)
        seen = seen + running[:, wide - 1 : wide]
        rank = rank.astype(I32) - 1 - first
        here = iota((ROUND, wide), 0) == rank
        columns = jnp.concatenate(
            [
                jnp.where(here, v.astype(F32), 0.0)
                for v in (local >> 5, key >> 5, local & 31, key & 31)
            ],
            axis=0,
        ).astype(BF16)
        layout = layout + lax.dot_general(
            hot, columns, (((1,), (1,)), ((), ())), preferred_element_type=F32
        )
        fits = (rank >= 0) & (rank < ROUND)
        slot = jnp.where(fits, dest * ROUND + rank, DEVS * ROUND)
        for u in range(step):
            slots_ref[t + u : t + u + 1, :] = slot[:, u * samples : (u + 1) * samples]
    keys_ref[...] = layout[:, :LANES] * 32.0 + layout[:, LANES:] - 1.0
    most = jnp.max(seen, axis=0, keepdims=True).astype(I32)
    rounds = ((most + ROUND - 1) // ROUND).astype(F32)
    var = var_ref[...]
    spot = (serve_ref[...] & (var.shape[0] * LANES - 1)).astype(F32)
    blank = jnp.zeros((ROUND, LANES), F32)
    sides = [var, pltpu.roll(var, ROUND, 1), spot, pltpu.roll(spot, ROUND, 1)]
    extra = jnp.concatenate([blank] + sides, axis=0).T
    coarse = extra.astype(BF16)
    fine = (extra - coarse.astype(F32)).astype(BF16)
    twice = one_hot((iota((DEVS, DEVS), 0) >> 1) == iota((DEVS, DEVS), 1))
    coarse = jnp.dot(twice, coarse, preferred_element_type=F32)
    fine = jnp.dot(twice, fine, preferred_element_type=F32)
    index = iota((DEVS, LANES), 1) < ROUND
    high = jnp.where(index, layout[:, :LANES], coarse)
    low = jnp.where(index, layout[:, LANES:], fine)
    row_ref[:, 0:1, :] = high.reshape(DEVS, 1, LANES)
    row_ref[:, 1:2, :] = low.reshape(DEVS, 1, LANES)
    row_ref[:, 2:8, :] = jnp.broadcast_to(rounds.reshape(1, 1, 1), (DEVS, 6, LANES))


def route(round_index, ids, lengths, train_map, var, serve):
    return pl.pallas_call(
        route_kernel,
        in_specs=[pl.BlockSpec(memory_space=pltpu.SMEM)]
        + [pl.BlockSpec(memory_space=pltpu.VMEM)] * 5,
        out_specs=[pl.BlockSpec(memory_space=pltpu.VMEM)] * 3,
        out_shape=(
            jax.ShapeDtypeStruct(ids.shape, I32),
            jax.ShapeDtypeStruct((DEVS, LANES), F32),
            jax.ShapeDtypeStruct((DEVS, 8, LANES), F32),
        ),
        name="route",
    )(round_index, ids, lengths, train_map, var, serve)


def pack_kernel(
    slots_ref,
    place_ref,
    grads_ref,
    table_from_ref,
    moment_from_ref,
    head_ref,
    out_ref,
    from_ref,
    to_ref,
    table_ref,
    moment_ref,
    sems,
):
    half, odd = place_ref[0], place_ref[1]
    mine = pl.ds(pl.multiple_of(half * table_ref.shape[0], 8), table_ref.shape[0])
    copies = [
        pltpu.make_async_copy(table_from_ref.at[mine], table_ref, sems.at[0]),
        pltpu.make_async_copy(moment_from_ref.at[mine], moment_ref, sems.at[1]),
    ]
    for copy in copies:
        copy.start()
    count = slots_ref.shape[0]
    bag = 32
    samples = count // bag
    block = 512

    def widen(i, carry):
        at = pl.multiple_of(i * block, block)
        from_ref[pl.ds(at, block), :] = grads_ref[pl.ds(at, block), :].astype(F32)
        to_ref[pl.ds(at * 2, block), :] = jnp.zeros((block, LANES), F32)
        to_ref[pl.ds(at * 2 + block, block), :] = jnp.zeros((block, LANES), F32)
        return carry

    def move(i, carry):
        first = (i & 3) * (bag * bag) + (i >> 2)
        for u in range(bag):
            slot = slots_ref[i * bag + u]
            to_ref[pl.ds(slot, 1), :] = from_ref[pl.ds(first + u * bag, 1), :]
        return carry

    def rows_of(ref, i):
        starts = [i * 4 + ((u + odd) & 1) * (LANES // 2) + u // 2 for u in range(8)]
        rows = [ref[pl.ds(start, 8, stride=LANES), :] for start in starts]
        return jnp.concatenate([r.reshape(1, 8, LANES) for r in rows], axis=0)

    def narrow(i, carry):
        at = pl.multiple_of(i * 8, 8)
        rows = to_ref[pl.ds(pl.multiple_of(i * block, block), block), :].astype(BF16)
        table = rows_of(table_ref, i)
        coarse = table.astype(BF16).astype(F32)
        state = jnp.concatenate([coarse, table - coarse], axis=1).astype(BF16)
        more = jnp.concatenate([rows_of(moment_ref, i), head_ref[pl.ds(at, 8)]], axis=1)
        out_ref[pl.ds(at, 8), 0:ROUND, :] = rows.reshape(8, ROUND, LANES)
        out_ref[pl.ds(at, 8), ROUND : ROUND + 16, :] = state
        out_ref[pl.ds(at, 8), ROUND + 16 : ROUND + 32, :] = more.astype(BF16)
        return carry

    lax.fori_loop(0, bag * samples // block, widen, 0)
    lax.fori_loop(0, count // bag, move, 0)
    for copy in copies:
        copy.wait()
    lax.fori_loop(0, DEVS // 8, narrow, 0)


def pack(slots, place, grads, table, moment, head):
    return pl.pallas_call(
        pack_kernel,
        in_specs=[pl.BlockSpec(memory_space=pltpu.SMEM)] * 2
        + [pl.BlockSpec(memory_space=pltpu.VMEM)]
        + [pl.BlockSpec(memory_space=pl.ANY)] * 2
        + [pl.BlockSpec(memory_space=pltpu.VMEM)],
        out_specs=pl.BlockSpec(memory_space=pltpu.VMEM),
        out_shape=jax.ShapeDtypeStruct((DEVS, SENT, LANES), BF16),
        scratch_shapes=[
            pltpu.VMEM(grads.shape, F32),
            pltpu.VMEM((DEVS * ROUND + 8, LANES), F32),
            pltpu.VMEM((table.shape[0] // 2, LANES), F32),
            pltpu.VMEM((table.shape[0] // 2, LANES), F32),
            pltpu.SemaphoreType.DMA((2,)),
        ],
        name="pack",
    )(slots.reshape(-1), place, grads, table, moment, head)


def pair_up(line, low):
    other = pltpu.roll(line, ROUND, 1)
    half = DEVS // 2
    left = (line if low else other)[:half]
    right = (other if low else line)[half:]
    return jnp.where(iota((half, LANES), 1) < ROUND, left, right).astype(I32)


def add_rows(index_ref, left_ref, right_ref, acc_ref, with_count):
    step = pl.program_id(0)
    turns = left_ref.shape[0] // PAIRS

    def add(i, carry):
        at = pl.ds(pl.multiple_of(i * PAIRS, PAIRS), PAIRS)
        pieces = pl.ds(pl.multiple_of((step * turns + i) * PAIRS, PAIRS), PAIRS)
        index = index_ref[pieces, :]
        index = jnp.concatenate([index[u : u + 1] for u in range(PAIRS)], axis=1)
        left, right = left_ref[at], right_ref[at]
        rows = jnp.concatenate([p[u] for u in range(PAIRS) for p in (left, right)], axis=0)
        if with_count:
            rows = jnp.concatenate([rows, jnp.ones_like(rows)], axis=1)
        hit = hot_rows(acc_ref.shape[0], index)
        acc_ref[...] = acc_ref[...] + jnp.dot(hit, rows, preferred_element_type=F32)
        return carry

    lax.fori_loop(0, turns, add, 0)


PAIRS = 16
STEPS = 4


def half_spec(second):
    count = DEVS // 2 // STEPS
    return pl.BlockSpec((count, ROUND, LANES), lambda i: (i + second * STEPS, 0, 0))


def whole(shape, at=None):
    place = at if at is not None else (0,) * len(shape)
    return pl.BlockSpec(shape, lambda i: place)


STATE_SPEC = whole((DEVS, 32, LANES), (0, ROUND // 32, 0))


def line_of(state_ref):
    high = state_ref[:, 24:25, :].astype(F32).reshape(DEVS, LANES)
    low = state_ref[:, 25:26, :].astype(F32).reshape(DEVS, LANES)
    return high * 32.0 + low - 1.0


def adam(core, state_ref, acc_ref, new_ref, sums_ref, spots_ref):
    def step(i, carry):
        at = pl.multiple_of(i * LANES, LANES)
        part = pl.ds(i * 16, 16)
        total = acc_ref[pl.ds(at, LANES), :]
        shape = (16, 8, LANES)
        grad = total[:, :LANES].reshape(shape)
        touched = (total[:, LANES:] > 0.5).reshape(shape)
        state = state_ref[part].astype(F32)
        table = state[:, 0:8, :] + state[:, 8:16, :]
        moment = state[:, 16:24, :]
        source = iota(shape, 0)
        within = iota(shape, 1)
        lane = iota(shape, 2)
        parity = (core + i * 8 + (source >> 1)) & 1
        own = parity * 16 + (source & 1) * 8 + within
        high = jnp.broadcast_to(state[:, 24:25, :], shape)
        extra = high + jnp.broadcast_to(state[:, 25:26, :], shape)
        var = jnp.sum(jnp.where(lane == ROUND + own, extra, 0.0), axis=2, keepdims=True)
        spot = jnp.sum(jnp.where(lane == ROUND + 32 + own, extra, 0.0), axis=2, keepdims=True)
        mean = jnp.sum(grad * grad, axis=2, keepdims=True) * (1.0 / LANES)
        new_var = beta_two * var + (1.0 - beta_two) * mean
        new_moment = beta_one * moment + (1.0 - beta_one) * grad
        new_table = table - learn_rate * new_moment / (jnp.sqrt(new_var) + epsilon)
        new_ref[pl.ds(at, LANES), :] = new_table.reshape(LANES, LANES).astype(BF16)
        sums_ref[part] = jnp.where(touched, grad, UNTOUCHED)
        spot = jnp.where(lane == source * 8 + within, jnp.where(touched, spot, 4096.0), 0.0)
        spot = jnp.sum(jnp.sum(spot, axis=0), axis=0, keepdims=True)
        spots_ref[pl.ds(i, 1), :] = spot.astype(I32)
        return carry

    lax.fori_loop(0, 8, step, 0)


def update_kernel(
    core_ref,
    state_ref,
    left_ref,
    right_ref,
    new_ref,
    sums_ref,
    spots_ref,
    acc_ref,
    line_ref,
    rounds_ref,
    index_ref,
):
    @pl.when(pl.program_id(0) == 0)
    def _():
        line = line_of(state_ref)
        line_ref[...] = line
        index_ref[...] = pair_up(line, True)
        rounds = state_ref[:, 26:27, :].astype(F32).reshape(DEVS, LANES)
        rounds_ref[0] = jnp.max(rounds).astype(I32)
        acc_ref[...] = jnp.zeros(acc_ref.shape, F32)

    add_rows(index_ref, left_ref, right_ref, acc_ref, True)

    @pl.when(pl.program_id(0) == STEPS - 1)
    def _():
        adam(core_ref[0], state_ref, acc_ref, new_ref, sums_ref, spots_ref)


def updated_shapes(rows):
    return (
        jax.ShapeDtypeStruct((rows, LANES), BF16),
        jax.ShapeDtypeStruct((DEVS, 8, LANES), F32),
        jax.ShapeDtypeStruct((8, LANES), I32),
    )


def updated_specs(rows):
    return [whole((rows, LANES)), whole((DEVS, 8, LANES)), whole((8, LANES))]


def update(core, received, rows):
    return pl.pallas_call(
        update_kernel,
        grid=(STEPS,),
        in_specs=[
            pl.BlockSpec(memory_space=pltpu.SMEM),
            STATE_SPEC,
            half_spec(0),
            half_spec(1),
        ],
        out_specs=updated_specs(rows)
        + [
            whole((rows, 2 * LANES)),
            whole((DEVS, LANES)),
            pl.BlockSpec(memory_space=pltpu.SMEM),
        ],
        out_shape=updated_shapes(rows)
        + (
            jax.ShapeDtypeStruct((rows, 2 * LANES), F32),
            jax.ShapeDtypeStruct((DEVS, LANES), F32),
            jax.ShapeDtypeStruct((1,), I32),
        ),
        scratch_shapes=[pltpu.VMEM((DEVS // 2, LANES), I32)],
        name="update",
    )(core, received, received, received)


def adam_kernel(core_ref, state_ref, acc_ref, new_ref, sums_ref, spots_ref):
    adam(core_ref[0], state_ref, acc_ref, new_ref, sums_ref, spots_ref)


def adam_again(core, received, acc):
    rows = acc.shape[0]
    return pl.pallas_call(
        adam_kernel,
        grid=(1,),
        in_specs=[pl.BlockSpec(memory_space=pltpu.SMEM), STATE_SPEC, whole(acc.shape)],
        out_specs=updated_specs(rows),
        out_shape=updated_shapes(rows),
        name="adam",
    )(core, received, acc)


def more_kernel(line_ref, left_ref, right_ref, start_ref, out_ref, index_ref, *, low, with_count):
    @pl.when(pl.program_id(0) == 0)
    def _():
        index_ref[...] = pair_up(line_ref[...], low)
        out_ref[...] = start_ref[...]

    add_rows(index_ref, left_ref, right_ref, out_ref, with_count)


def more_rows(line, rows, start, low, with_count):
    return pl.pallas_call(
        functools.partial(more_kernel, low=low, with_count=with_count),
        grid=(STEPS,),
        in_specs=[whole(line.shape), half_spec(0), half_spec(1), whole(start.shape)],
        out_specs=whole(start.shape),
        out_shape=jax.ShapeDtypeStruct(start.shape, F32),
        scratch_shapes=[pltpu.VMEM((DEVS // 2, LANES), I32)],
        name="more_rows",
    )(line, rows, rows, start)


def reply_kernel(line_ref, new_ref, out_ref, turned_ref, table_ref):
    turned_ref[...] = line_ref[...].T
    part = new_ref.shape[0] // 4
    table_ref[...] = jnp.concatenate(
        [new_ref[k * part : (k + 1) * part, :] for k in range(4)], axis=1
    )

    def look(i, carry):
        turned = pltpu.roll(turned_ref[0:ROUND, :], LANES - i * 32, 1).astype(I32)
        within = turned & (part - 1)
        hit = jnp.concatenate(
            [one_hot(iota((ROUND, part), 1) == within[:, u : u + 1]) for u in range(32)], axis=0
        )
        found = jnp.dot(hit, table_ref[...], preferred_element_type=F32)
        for u in range(32):
            piece = found[u * ROUND : (u + 1) * ROUND]
            row = jnp.broadcast_to(turned[:, u : u + 1], (ROUND, LANES))
            low = jnp.where(row < part, piece[:, :LANES], piece[:, LANES : 2 * LANES])
            high = jnp.where(
                row < 3 * part, piece[:, 2 * LANES : 3 * LANES], piece[:, 3 * LANES :]
            )
            out_ref[i * 32 + u] = jnp.where(row < 2 * part, low, high).astype(BF16)
        return carry

    lax.fori_loop(0, DEVS // 32, look, 0)


def reply(line, new_rows):
    return pl.pallas_call(
        reply_kernel,
        in_specs=[pl.BlockSpec(memory_space=pltpu.VMEM)] * 2,
        out_specs=pl.BlockSpec(memory_space=pltpu.VMEM),
        out_shape=jax.ShapeDtypeStruct((DEVS, ROUND, LANES), BF16),
        scratch_shapes=[
            pltpu.VMEM((DEVS, LANES), F32),
            pltpu.VMEM((new_rows.shape[0] // 4, 4 * LANES), BF16),
        ],
        name="reply",
    )(line, new_rows)


def score_kernel(
    keys_ref,
    left_ref,
    right_ref,
    start_ref,
    first_ref,
    second_ref,
    score_ref,
    out_ref,
    index_ref,
    acc_ref,
):
    @pl.when(pl.program_id(0) == 0)
    def _():
        index_ref[...] = pair_up(keys_ref[...], False)
        acc_ref[...] = start_ref[...]

    add_rows(index_ref, left_ref, right_ref, acc_ref, False)

    @pl.when(pl.program_id(0) == STEPS - 1)
    def _():
        samples = out_ref.shape[1]
        pooled = jnp.concatenate(
            [acc_ref[f * samples : (f + 1) * samples, :] for f in range(4)], axis=1
        ).astype(BF16)
        hidden = jnp.dot(pooled, first_ref[...], preferred_element_type=F32)
        hidden = jnp.maximum(hidden, 0.0).astype(BF16)
        hidden = jnp.dot(hidden, second_ref[...], preferred_element_type=F32)
        hidden = jnp.maximum(hidden, 0.0).astype(BF16)
        weights = jnp.broadcast_to(score_ref[...], (16, score_ref.shape[1]))
        scores = lax.dot_general(
            weights, hidden, (((1,), (1,)), ((), ())), preferred_element_type=F32
        )
        out_ref[...] = scores[0:1, :]


def score(keys, rows, start, w_first, w_second, w_score):
    samples = start.shape[0] // 4
    return pl.pallas_call(
        score_kernel,
        grid=(STEPS,),
        in_specs=[whole(keys.shape), half_spec(0), half_spec(1), whole(start.shape)]
        + [whole(w.shape) for w in (w_first, w_second, w_score)],
        out_specs=whole((1, samples)),
        out_shape=jax.ShapeDtypeStruct((1, samples), F32),
        scratch_shapes=[
            pltpu.VMEM((DEVS // 2, LANES), I32),
            pltpu.VMEM(start.shape, F32),
        ],
        name="score",
    )(keys, rows, rows, start, w_first, w_second, w_score)


def exchange(value):
    return lax.all_to_all(value, ALL, 0, 0, tiled=True)


def place_kernel(old_ref, own_ref, other_ref, own_at_ref, other_at_ref, out_ref):
    block = 512

    def place(i, carry):
        at = pl.ds(pl.multiple_of(i * block, block), block)
        total = jnp.zeros((block, 2 * LANES), F32)
        for at_ref, rows_ref in ((own_at_ref, own_ref), (other_at_ref, other_ref)):
            spots = at_ref[...] - i * block
            spots = jnp.where((spots >= 0) & (spots < block), spots, -1)
            spots = jnp.concatenate([spots[u : u + 1] for u in range(8)], axis=1)
            rows = rows_ref[...]
            rows = jnp.concatenate([rows, jnp.ones_like(rows)], axis=1)
            total = total + jnp.dot(hot_rows(block, spots), rows, preferred_element_type=F32)
        fresh = total[:, :LANES].astype(BF16).astype(F32)
        old = old_ref[at, :].astype(F32)
        out_ref[at, :] = jnp.where(total[:, LANES:] > 0.5, fresh, old).astype(BF16)
        return carry

    lax.fori_loop(0, old_ref.shape[0] // block, place, 0)


def place_rows(old, own, other, own_at, other_at):
    return pl.pallas_call(
        place_kernel,
        in_specs=[pl.BlockSpec(memory_space=pltpu.VMEM)] * 5,
        out_specs=pl.BlockSpec(memory_space=pltpu.VMEM),
        out_shape=jax.ShapeDtypeStruct(old.shape, BF16),
        name="place",
    )(old, own, other, own_at, other_at)


def per_device(
    touched_ids,
    bag_lengths,
    train_map,
    serve_map,
    slot_grads,
    table,
    moment,
    row_var,
    serving_old,
    w_first,
    w_second,
    w_score,
):
    owners = lax.axis_size("shard")
    owner = lax.axis_index("shard")
    rep = lax.axis_index("rep")
    tab_rows, row_width = table.shape
    samples, bag = touched_ids.shape
    swap = [(0, 1), (1, 0)]
    odd = owner % 2 == 1
    rows_here = tab_rows // 2

    front = (
        touched_ids.T,
        bag_lengths.T,
        train_map.reshape(-1, LANES),
        row_var.reshape(-1, LANES),
        serve_map.reshape(-1, LANES),
    )
    grads = slot_grads.reshape(samples * bag, row_width)

    place = jnp.stack([rep, owner % 2]).astype(I32)
    slots, keys, head = route(jnp.zeros((1,), I32), *front)
    received = exchange(pack(slots, place, grads, table, moment, head))
    core = rep.reshape(1).astype(I32)
    new_rows, sums, places, acc, line, rounds = update(core, received, rows_here)
    rounds = rounds[0]
    one = jnp.ones((), I32)

    def more_sums(carry):
        k, acc = carry[0], carry[1]
        slots, _, head = route(k.reshape(1), *front)
        got = exchange(pack(slots, place, grads, table, moment, head))
        line = got[:, ROUND + 24].astype(F32) * 32.0 + got[:, ROUND + 25].astype(F32) - 1.0
        acc = more_rows(line, got, acc, True, True)
        return (k + 1, acc) + tuple(adam_again(core, received, acc))

    _, _, new_rows, sums, places = lax.while_loop(
        lambda c: c[0] < rounds, more_sums, (one, acc, new_rows, sums, places)
    )

    back = exchange(sums)
    answer = exchange(reply(line, new_rows))

    other_rows = lax.ppermute(new_rows, "rep", swap)
    other_places = lax.ppermute(places, "rep", swap)
    serving_table = place_rows(serving_old, new_rows, other_rows, places, other_places)

    back = back.reshape(owners, 2, 8, row_width)
    back = jnp.where(odd, back[:, ::-1], back)
    half = back.transpose(2, 1, 0, 3).reshape(rows_here, row_width)
    other = lax.ppermute(half, "rep", swap)
    grad_sum = jnp.where(
        rep == 0, jnp.concatenate([half, other]), jnp.concatenate([other, half])
    )
    touched = grad_sum[:, :1] < 0.5 * UNTOUCHED
    new_moment = jnp.where(touched, beta_one * moment + (1.0 - beta_one) * grad_sum, moment)
    mean = jnp.mean(jnp.where(touched, grad_sum * grad_sum, 0.0), axis=1)
    new_var = jnp.where(touched[:, 0], beta_two * row_var + (1.0 - beta_two) * mean, row_var)
    new_table = jnp.where(
        touched, table - learn_rate * new_moment / (jnp.sqrt(new_var)[:, None] + epsilon), table
    )

    def more_pooled(carry):
        k, acc = carry
        _, keys, head = route(k.reshape(1), *front)
        got = exchange(head)
        line = got[:, 0] * 32.0 + got[:, 1] - 1.0
        return (k + 1, more_rows(keys, exchange(reply(line, new_rows)), acc, False, False))

    rounds, _ = lax.optimization_barrier((rounds, answer[0, 0, 0]))
    _, pooled = lax.while_loop(
        lambda c: c[0] < rounds,
        more_pooled,
        (one, jnp.zeros((4 * samples, row_width), F32)),
    )
    scores = score(keys, answer, pooled, w_first, w_second, w_score.reshape(1, -1))
    return (new_table, new_moment, new_var, serving_table, scores.reshape(samples))


def solution(mesh):
    in_specs = (
        P(("shard", "rep"), None),
        P(("shard", "rep"), None),
        P(),
        P("shard"),
        P(("shard", "rep"), None, None),
        P("shard", None),
        P("shard", None),
        P("shard"),
        P("shard", None),
        P(),
        P(),
        P(),
    )
    out_specs = (
        P("shard", None),
        P("shard", None),
        P("shard"),
        P("shard", None),
        P(("shard", "rep")),
    )
    return jax.shard_map(
        per_device, mesh=mesh, in_specs=in_specs, out_specs=out_specs, check_vma=False
    )
```

```python
import functools

import jax
import jax.numpy as jnp
from jax import lax
from jax.experimental import pallas as pl
from jax.experimental.pallas import tpu as pltpu
from jax.sharding import PartitionSpec as P

beta_one = 0.9
beta_two = 0.999
learn_rate = 0.1
epsilon = 1e-06

ROUND = 64
DEVS = 128
LANES = 128
UNTOUCHED = 1e30
F32 = jnp.float32
BF16 = jnp.bfloat16
I32 = jnp.int32
ALL = ("shard", "rep")
SENT = ROUND + 32


def iota(shape, dim):
    return lax.broadcasted_iota(I32, shape, dim)


def one_hot(mask):
    return jnp.where(mask, 1.0, 0.0).astype(BF16)


def hot_rows(count, index):
    index = index.astype(jnp.int16)
    place = iota((count, index.shape[1]), 0).astype(jnp.int16)
    return jnp.where(place == index, jnp.bfloat16(1), jnp.bfloat16(0))


def route_kernel(
    round_ref, ids_ref, lengths_ref, map_ref, var_ref, serve_ref, slots_ref, keys_ref, row_ref
):
    bag, samples = ids_ref.shape
    step = 4
    wide = step * samples
    first = round_ref[0] * ROUND
    table = map_ref[...]
    high = (table >> 9).astype(F32).T
    low = ((table & 511) - 256).astype(F32).T
    parts = jnp.concatenate([high, low], axis=0).astype(BF16)
    upto = one_hot(iota((wide, wide), 0) <= iota((wide, wide), 1))
    ends = []
    total = jnp.zeros((1, samples), I32)
    for f in range(3):
        total = total + lengths_ref[f : f + 1, :]
        ends.append(total)
    sample = iota((1, samples), 1)
    seen = jnp.zeros((DEVS, 1), F32)
    layout = jnp.zeros((DEVS, 4 * ROUND), F32)
    for t in range(0, bag, step):
        ids = jnp.concatenate([ids_ref[t + u : t + u + 1, :] for u in range(step)], axis=1)
        keys = []
        for u in range(step):
            field = sum((jnp.where(e <= t + u, 1, 0) for e in ends), jnp.zeros((1, samples), I32))
            keys.append(field * samples + sample)
        key = jnp.concatenate(keys, axis=1) + 1
        hit = hot_rows(table.shape[0], ids >> 7)
        both = jnp.dot(parts, hit, preferred_element_type=F32)
        value = both[:LANES] * 512.0 + both[LANES:] + 256.0
        value = jnp.where(iota((LANES, wide), 0) == (ids & 127), value, 0.0)
        position = jnp.sum(value, axis=0, keepdims=True).astype(I32)
        owner = position >> 11
        stride = (position >> 6) & 31
        dest = (position & 63) * 2 + ((stride + owner) & 1)
        local = owner * 16 + (stride >> 1) + 1
        mine = iota((DEVS, wide), 0) == dest
        hot = one_hot(mine)
        running = jnp.dot(hot, upto, preferred_element_type=F32)
        rank = jnp.sum(jnp.where(mine, running + seen, 0.0), axis=0, keepdims=True)
        seen = seen + running[:, wide - 1 : wide]
        rank = rank.astype(I32) - 1 - first
        here = iota((ROUND, wide), 0) == rank
        columns = jnp.concatenate(
            [
                jnp.where(here, v.astype(F32), 0.0)
                for v in (local >> 5, key >> 5, local & 31, key & 31)
            ],
            axis=0,
        ).astype(BF16)
        layout = layout + lax.dot_general(
            hot, columns, (((1,), (1,)), ((), ())), preferred_element_type=F32
        )
        fits = (rank >= 0) & (rank < ROUND)
        slot = jnp.where(fits, dest * ROUND + rank, DEVS * ROUND)
        for u in range(step):
            slots_ref[t + u : t + u + 1, :] = slot[:, u * samples : (u + 1) * samples]
    keys_ref[...] = layout[:, :LANES] * 32.0 + layout[:, LANES:] - 1.0
    most = jnp.max(seen, axis=0, keepdims=True).astype(I32)
    rounds = ((most + ROUND - 1) // ROUND).astype(F32)
    var = var_ref[...]
    spot = (serve_ref[...] & (var.shape[0] * LANES - 1)).astype(F32)
    blank = jnp.zeros((ROUND, LANES), F32)
    sides = [var, pltpu.roll(var, ROUND, 1), spot, pltpu.roll(spot, ROUND, 1)]
    extra = jnp.concatenate([blank] + sides, axis=0).T
    coarse = extra.astype(BF16)
    fine = (extra - coarse.astype(F32)).astype(BF16)
    twice = one_hot((iota((DEVS, DEVS), 0) >> 1) == iota((DEVS, DEVS), 1))
    coarse = jnp.dot(twice, coarse, preferred_element_type=F32)
    fine = jnp.dot(twice, fine, preferred_element_type=F32)
    index = iota((DEVS, LANES), 1) < ROUND
    high = jnp.where(index, layout[:, :LANES], coarse)
    low = jnp.where(index, layout[:, LANES:], fine)
    row_ref[:, 0:1, :] = high.reshape(DEVS, 1, LANES)
    row_ref[:, 1:2, :] = low.reshape(DEVS, 1, LANES)
    row_ref[:, 2:8, :] = jnp.broadcast_to(rounds.reshape(1, 1, 1), (DEVS, 6, LANES))


def route(round_index, ids, lengths, train_map, var, serve):
    return pl.pallas_call(
        route_kernel,
        in_specs=[pl.BlockSpec(memory_space=pltpu.SMEM)]
        + [pl.BlockSpec(memory_space=pltpu.VMEM)] * 5,
        out_specs=[pl.BlockSpec(memory_space=pltpu.VMEM)] * 3,
        out_shape=(
            jax.ShapeDtypeStruct(ids.shape, I32),
            jax.ShapeDtypeStruct((DEVS, LANES), F32),
            jax.ShapeDtypeStruct((DEVS, 8, LANES), F32),
        ),
        name="route",
    )(round_index, ids, lengths, train_map, var, serve)


def pack_kernel(
    slots_ref,
    place_ref,
    grads_ref,
    table_from_ref,
    moment_from_ref,
    head_ref,
    out_ref,
    from_ref,
    to_ref,
    table_ref,
    moment_ref,
    sems,
):
    half, odd = place_ref[0], place_ref[1]
    mine = pl.ds(pl.multiple_of(half * table_ref.shape[0], 8), table_ref.shape[0])
    copies = [
        pltpu.make_async_copy(table_from_ref.at[mine], table_ref, sems.at[0]),
        pltpu.make_async_copy(moment_from_ref.at[mine], moment_ref, sems.at[1]),
    ]
    for copy in copies:
        copy.start()
    count = slots_ref.shape[0]
    bag = 32
    samples = count // bag
    block = 512

    def widen(i, carry):
        at = pl.multiple_of(i * block, block)
        from_ref[pl.ds(at, block), :] = grads_ref[pl.ds(at, block), :].astype(F32)
        to_ref[pl.ds(at * 2, block), :] = jnp.zeros((block, LANES), F32)
        to_ref[pl.ds(at * 2 + block, block), :] = jnp.zeros((block, LANES), F32)
        return carry

    def move(i, carry):
        first = (i & 3) * (bag * bag) + (i >> 2)
        for u in range(bag):
            slot = slots_ref[i * bag + u]
            to_ref[pl.ds(slot, 1), :] = from_ref[pl.ds(first + u * bag, 1), :]
        return carry

    def rows_of(ref, i):
        starts = [i * 4 + ((u + odd) & 1) * (LANES // 2) + u // 2 for u in range(8)]
        rows = [ref[pl.ds(start, 8, stride=LANES), :] for start in starts]
        return jnp.concatenate([r.reshape(1, 8, LANES) for r in rows], axis=0)

    def narrow(i, carry):
        at = pl.multiple_of(i * 8, 8)
        rows = to_ref[pl.ds(pl.multiple_of(i * block, block), block), :].astype(BF16)
        table = rows_of(table_ref, i)
        coarse = table.astype(BF16).astype(F32)
        state = jnp.concatenate([coarse, table - coarse], axis=1).astype(BF16)
        more = jnp.concatenate([rows_of(moment_ref, i), head_ref[pl.ds(at, 8)]], axis=1)
        out_ref[pl.ds(at, 8), 0:ROUND, :] = rows.reshape(8, ROUND, LANES)
        out_ref[pl.ds(at, 8), ROUND : ROUND + 16, :] = state
        out_ref[pl.ds(at, 8), ROUND + 16 : ROUND + 32, :] = more.astype(BF16)
        return carry

    lax.fori_loop(0, bag * samples // block, widen, 0)
    lax.fori_loop(0, count // bag, move, 0)
    for copy in copies:
        copy.wait()
    lax.fori_loop(0, DEVS // 8, narrow, 0)


def pack(slots, place, grads, table, moment, head):
    return pl.pallas_call(
        pack_kernel,
        in_specs=[pl.BlockSpec(memory_space=pltpu.SMEM)] * 2
        + [pl.BlockSpec(memory_space=pltpu.VMEM)]
        + [pl.BlockSpec(memory_space=pl.ANY)] * 2
        + [pl.BlockSpec(memory_space=pltpu.VMEM)],
        out_specs=pl.BlockSpec(memory_space=pltpu.VMEM),
        out_shape=jax.ShapeDtypeStruct((DEVS, SENT, LANES), BF16),
        scratch_shapes=[
            pltpu.VMEM(grads.shape, F32),
            pltpu.VMEM((DEVS * ROUND + 8, LANES), F32),
            pltpu.VMEM((table.shape[0] // 2, LANES), F32),
            pltpu.VMEM((table.shape[0] // 2, LANES), F32),
            pltpu.SemaphoreType.DMA((2,)),
        ],
        name="pack",
    )(slots.reshape(-1), place, grads, table, moment, head)


def pair_up(line, low):
    other = pltpu.roll(line, ROUND, 1)
    half = DEVS // 2
    left = (line if low else other)[:half]
    right = (other if low else line)[half:]
    return jnp.where(iota((half, LANES), 1) < ROUND, left, right).astype(I32)


def add_rows(index_ref, left_ref, right_ref, acc_ref, with_count):
    step = pl.program_id(0)
    turns = left_ref.shape[0] // PAIRS

    def add(i, carry):
        at = pl.ds(pl.multiple_of(i * PAIRS, PAIRS), PAIRS)
        pieces = pl.ds(pl.multiple_of((step * turns + i) * PAIRS, PAIRS), PAIRS)
        index = index_ref[pieces, :]
        index = jnp.concatenate([index[u : u + 1] for u in range(PAIRS)], axis=1)
        left, right = left_ref[at], right_ref[at]
        rows = jnp.concatenate([p[u] for u in range(PAIRS) for p in (left, right)], axis=0)
        if with_count:
            rows = jnp.concatenate([rows, jnp.ones_like(rows)], axis=1)
        hit = hot_rows(acc_ref.shape[0], index)
        acc_ref[...] = acc_ref[...] + jnp.dot(hit, rows, preferred_element_type=F32)
        return carry

    lax.fori_loop(0, turns, add, 0)


PAIRS = 16
STEPS = 4


def half_spec(second):
    count = DEVS // 2 // STEPS
    return pl.BlockSpec((count, ROUND, LANES), lambda i: (i + second * STEPS, 0, 0))


def whole(shape, at=None):
    place = at if at is not None else (0,) * len(shape)
    return pl.BlockSpec(shape, lambda i: place)


STATE_SPEC = whole((DEVS, 32, LANES), (0, ROUND // 32, 0))


def line_of(state_ref):
    high = state_ref[:, 24:25, :].astype(F32).reshape(DEVS, LANES)
    low = state_ref[:, 25:26, :].astype(F32).reshape(DEVS, LANES)
    return high * 32.0 + low - 1.0


def adam(core, state_ref, acc_ref, new_ref, sums_ref, spots_ref):
    def step(i, carry):
        at = pl.multiple_of(i * LANES, LANES)
        part = pl.ds(i * 16, 16)
        total = acc_ref[pl.ds(at, LANES), :]
        shape = (16, 8, LANES)
        grad = total[:, :LANES].reshape(shape)
        touched = (total[:, LANES:] > 0.5).reshape(shape)
        state = state_ref[part].astype(F32)
        table = state[:, 0:8, :] + state[:, 8:16, :]
        moment = state[:, 16:24, :]
        source = iota(shape, 0)
        within = iota(shape, 1)
        lane = iota(shape, 2)
        parity = (core + i * 8 + (source >> 1)) & 1
        own = parity * 16 + (source & 1) * 8 + within
        high = jnp.broadcast_to(state[:, 24:25, :], shape)
        extra = high + jnp.broadcast_to(state[:, 25:26, :], shape)
        var = jnp.sum(jnp.where(lane == ROUND + own, extra, 0.0), axis=2, keepdims=True)
        spot = jnp.sum(jnp.where(lane == ROUND + 32 + own, extra, 0.0), axis=2, keepdims=True)
        mean = jnp.sum(grad * grad, axis=2, keepdims=True) * (1.0 / LANES)
        new_var = beta_two * var + (1.0 - beta_two) * mean
        new_moment = beta_one * moment + (1.0 - beta_one) * grad
        new_table = table - learn_rate * new_moment / (jnp.sqrt(new_var) + epsilon)
        new_ref[pl.ds(at, LANES), :] = new_table.reshape(LANES, LANES).astype(BF16)
        sums_ref[part] = jnp.where(touched, grad, UNTOUCHED)
        spot = jnp.where(lane == source * 8 + within, jnp.where(touched, spot, 4096.0), 0.0)
        spot = jnp.sum(jnp.sum(spot, axis=0), axis=0, keepdims=True)
        spots_ref[pl.ds(i, 1), :] = spot.astype(I32)
        return carry

    lax.fori_loop(0, 8, step, 0)


def update_kernel(
    core_ref,
    state_ref,
    left_ref,
    right_ref,
    new_ref,
    sums_ref,
    spots_ref,
    acc_ref,
    line_ref,
    rounds_ref,
    index_ref,
):
    @pl.when(pl.program_id(0) == 0)
    def _():
        line = line_of(state_ref)
        line_ref[...] = line
        index_ref[...] = pair_up(line, True)
        rounds = state_ref[:, 26:27, :].astype(F32).reshape(DEVS, LANES)
        rounds_ref[0] = jnp.max(rounds).astype(I32)
        acc_ref[...] = jnp.zeros(acc_ref.shape, F32)

    add_rows(index_ref, left_ref, right_ref, acc_ref, True)

    @pl.when(pl.program_id(0) == STEPS - 1)
    def _():
        adam(core_ref[0], state_ref, acc_ref, new_ref, sums_ref, spots_ref)


def updated_shapes(rows):
    return (
        jax.ShapeDtypeStruct((rows, LANES), BF16),
        jax.ShapeDtypeStruct((DEVS, 8, LANES), F32),
        jax.ShapeDtypeStruct((8, LANES), I32),
    )


def updated_specs(rows):
    return [whole((rows, LANES)), whole((DEVS, 8, LANES)), whole((8, LANES))]


def update(core, received, rows):
    return pl.pallas_call(
        update_kernel,
        grid=(STEPS,),
        in_specs=[
            pl.BlockSpec(memory_space=pltpu.SMEM),
            STATE_SPEC,
            half_spec(0),
            half_spec(1),
        ],
        out_specs=updated_specs(rows)
        + [
            whole((rows, 2 * LANES)),
            whole((DEVS, LANES)),
            pl.BlockSpec(memory_space=pltpu.SMEM),
        ],
        out_shape=updated_shapes(rows)
        + (
            jax.ShapeDtypeStruct((rows, 2 * LANES), F32),
            jax.ShapeDtypeStruct((DEVS, LANES), F32),
            jax.ShapeDtypeStruct((1,), I32),
        ),
        scratch_shapes=[pltpu.VMEM((DEVS // 2, LANES), I32)],
        name="update",
    )(core, received, received, received)


def adam_kernel(core_ref, state_ref, acc_ref, new_ref, sums_ref, spots_ref):
    adam(core_ref[0], state_ref, acc_ref, new_ref, sums_ref, spots_ref)


def adam_again(core, received, acc):
    rows = acc.shape[0]
    return pl.pallas_call(
        adam_kernel,
        grid=(1,),
        in_specs=[pl.BlockSpec(memory_space=pltpu.SMEM), STATE_SPEC, whole(acc.shape)],
        out_specs=updated_specs(rows),
        out_shape=updated_shapes(rows),
        name="adam",
    )(core, received, acc)


def more_kernel(line_ref, left_ref, right_ref, start_ref, out_ref, index_ref, *, low, with_count):
    @pl.when(pl.program_id(0) == 0)
    def _():
        index_ref[...] = pair_up(line_ref[...], low)
        out_ref[...] = start_ref[...]

    add_rows(index_ref, left_ref, right_ref, out_ref, with_count)


def more_rows(line, rows, start, low, with_count):
    return pl.pallas_call(
        functools.partial(more_kernel, low=low, with_count=with_count),
        grid=(STEPS,),
        in_specs=[whole(line.shape), half_spec(0), half_spec(1), whole(start.shape)],
        out_specs=whole(start.shape),
        out_shape=jax.ShapeDtypeStruct(start.shape, F32),
        scratch_shapes=[pltpu.VMEM((DEVS // 2, LANES), I32)],
        name="more_rows",
    )(line, rows, rows, start)


def reply_kernel(line_ref, new_ref, sums_ref, out_ref, turned_ref, table_ref):
    turned_ref[...] = line_ref[...].T
    part = new_ref.shape[0] // 4
    table_ref[...] = jnp.concatenate(
        [new_ref[k * part : (k + 1) * part, :] for k in range(4)], axis=1
    )

    def look(i, carry):
        turned = pltpu.roll(turned_ref[0:ROUND, :], LANES - i * 32, 1).astype(I32)
        within = turned & (part - 1)
        hit = jnp.concatenate(
            [one_hot(iota((ROUND, part), 1) == within[:, u : u + 1]) for u in range(32)], axis=0
        )
        found = jnp.dot(hit, table_ref[...], preferred_element_type=F32)
        for u in range(32):
            piece = found[u * ROUND : (u + 1) * ROUND]
            row = jnp.broadcast_to(turned[:, u : u + 1], (ROUND, LANES))
            low = jnp.where(row < part, piece[:, :LANES], piece[:, LANES : 2 * LANES])
            high = jnp.where(
                row < 3 * part, piece[:, 2 * LANES : 3 * LANES], piece[:, 3 * LANES :]
            )
            out_ref[i * 32 + u, 0:ROUND, :] = jnp.where(row < 2 * part, low, high).astype(BF16)
        return carry

    out_ref[:, ROUND : ROUND + 8, :] = sums_ref[...].astype(BF16)
    lax.fori_loop(0, DEVS // 32, look, 0)


def reply(line, new_rows, sums):
    return pl.pallas_call(
        reply_kernel,
        in_specs=[pl.BlockSpec(memory_space=pltpu.VMEM)] * 3,
        out_specs=pl.BlockSpec(memory_space=pltpu.VMEM),
        out_shape=jax.ShapeDtypeStruct((DEVS, ROUND + 8, LANES), BF16),
        scratch_shapes=[
            pltpu.VMEM((DEVS, LANES), F32),
            pltpu.VMEM((new_rows.shape[0] // 4, 4 * LANES), BF16),
        ],
        name="reply",
    )(line, new_rows, sums)


def score_kernel(
    keys_ref,
    left_ref,
    right_ref,
    start_ref,
    first_ref,
    second_ref,
    score_ref,
    out_ref,
    index_ref,
    acc_ref,
):
    @pl.when(pl.program_id(0) == 0)
    def _():
        index_ref[...] = pair_up(keys_ref[...], False)
        acc_ref[...] = start_ref[...]

    add_rows(index_ref, left_ref, right_ref, acc_ref, False)

    @pl.when(pl.program_id(0) == STEPS - 1)
    def _():
        samples = out_ref.shape[1]
        pooled = jnp.concatenate(
            [acc_ref[f * samples : (f + 1) * samples, :] for f in range(4)], axis=1
        ).astype(BF16)
        hidden = jnp.dot(pooled, first_ref[...], preferred_element_type=F32)
        hidden = jnp.maximum(hidden, 0.0).astype(BF16)
        hidden = jnp.dot(hidden, second_ref[...], preferred_element_type=F32)
        hidden = jnp.maximum(hidden, 0.0).astype(BF16)
        weights = jnp.broadcast_to(score_ref[...], (16, score_ref.shape[1]))
        scores = lax.dot_general(
            weights, hidden, (((1,), (1,)), ((), ())), preferred_element_type=F32
        )
        out_ref[...] = scores[0:1, :]


def score(keys, rows, start, w_first, w_second, w_score):
    samples = start.shape[0] // 4
    return pl.pallas_call(
        score_kernel,
        grid=(STEPS,),
        in_specs=[whole(keys.shape), half_spec(0), half_spec(1), whole(start.shape)]
        + [whole(w.shape) for w in (w_first, w_second, w_score)],
        out_specs=whole((1, samples)),
        out_shape=jax.ShapeDtypeStruct((1, samples), F32),
        scratch_shapes=[
            pltpu.VMEM((DEVS // 2, LANES), I32),
            pltpu.VMEM(start.shape, F32),
        ],
        name="score",
    )(keys, rows, rows, start, w_first, w_second, w_score)


def finish_kernel(
    place_ref,
    own_ref,
    other_ref,
    table_ref,
    moment_ref,
    var_ref,
    new_table_ref,
    new_moment_ref,
    new_var_ref,
    sums_ref,
):
    half, odd = place_ref[0], place_ref[1]
    step = pl.program_id(0)

    @pl.when(step == 0)
    def _():
        sums_ref[half] = own_ref[...].astype(F32).reshape(sums_ref.shape[1:])
        sums_ref[1 - half] = other_ref[...].astype(F32).reshape(sums_ref.shape[1:])

    eye = iota((LANES, LANES), 0) == iota((LANES, LANES), 1)
    for u in range(4):
        block = step * 4 + u
        at = pl.ds(u * LANES, LANES)
        sides = []
        for parity in range(2):
            first = ((parity + odd) & 1) * 8 + (block & 7)
            sides.append(sums_ref[block >> 3, pl.ds(first, LANES // 2, stride=16), :])
        grad = jnp.concatenate(sides, axis=0)
        touched = grad < 0.5 * UNTOUCHED
        var = jnp.broadcast_to(var_ref[pl.ds(block, 1), :], (LANES, LANES))
        var = jnp.sum(jnp.where(eye, var, 0.0), axis=1, keepdims=True)
        known = jnp.where(touched, grad, 0.0)
        mean = jnp.sum(known * known, axis=1, keepdims=True) * (1.0 / LANES)
        new_var = jnp.where(touched, beta_two * var + (1.0 - beta_two) * mean, var)
        table, moment = table_ref[at, :], moment_ref[at, :]
        new_moment = jnp.where(touched, beta_one * moment + (1.0 - beta_one) * grad, moment)
        new_table = table - learn_rate * new_moment / (jnp.sqrt(new_var) + epsilon)
        new_moment_ref[at, :] = new_moment
        new_table_ref[at, :] = jnp.where(touched, new_table, table)
        line = jnp.sum(jnp.where(eye, new_var, 0.0), axis=0, keepdims=True)
        new_var_ref[pl.ds(block, 1), :] = line


def finish(place, answer, other, table, moment, var):
    rows = pl.BlockSpec((4 * LANES, LANES), lambda i: (i, 0))
    return pl.pallas_call(
        finish_kernel,
        grid=(table.shape[0] // (4 * LANES),),
        in_specs=[
            pl.BlockSpec(memory_space=pltpu.SMEM),
            whole((DEVS, 8, LANES), (0, ROUND // 8, 0)),
            whole(other.shape),
            rows,
            rows,
            whole(var.shape),
        ],
        out_specs=[rows, rows, whole(var.shape)],
        out_shape=tuple(jax.ShapeDtypeStruct(a.shape, F32) for a in (table, moment, var)),
        scratch_shapes=[pltpu.VMEM((2, table.shape[0] // 2, LANES), F32)],
        name="finish",
    )(place, answer, other, table, moment, var)


def exchange(value):
    return lax.all_to_all(value, ALL, 0, 0, tiled=True)


def place_kernel(old_ref, own_ref, other_ref, own_at_ref, other_at_ref, out_ref):
    block = 512

    def place(i, carry):
        at = pl.ds(pl.multiple_of(i * block, block), block)
        total = jnp.zeros((block, 2 * LANES), F32)
        for at_ref, rows_ref in ((own_at_ref, own_ref), (other_at_ref, other_ref)):
            spots = at_ref[...] - i * block
            spots = jnp.where((spots >= 0) & (spots < block), spots, -1)
            spots = jnp.concatenate([spots[u : u + 1] for u in range(8)], axis=1)
            rows = rows_ref[...]
            rows = jnp.concatenate([rows, jnp.ones_like(rows)], axis=1)
            total = total + jnp.dot(hot_rows(block, spots), rows, preferred_element_type=F32)
        fresh = total[:, :LANES].astype(BF16).astype(F32)
        old = old_ref[at, :].astype(F32)
        out_ref[at, :] = jnp.where(total[:, LANES:] > 0.5, fresh, old).astype(BF16)
        return carry

    lax.fori_loop(0, old_ref.shape[0] // block, place, 0)


def place_rows(old, own, other, own_at, other_at):
    return pl.pallas_call(
        place_kernel,
        in_specs=[pl.BlockSpec(memory_space=pltpu.VMEM)] * 5,
        out_specs=pl.BlockSpec(memory_space=pltpu.VMEM),
        out_shape=jax.ShapeDtypeStruct(old.shape, BF16),
        name="place",
    )(old, own, other, own_at, other_at)


def per_device(
    touched_ids,
    bag_lengths,
    train_map,
    serve_map,
    slot_grads,
    table,
    moment,
    row_var,
    serving_old,
    w_first,
    w_second,
    w_score,
):
    owners = lax.axis_size("shard")
    owner = lax.axis_index("shard")
    rep = lax.axis_index("rep")
    tab_rows, row_width = table.shape
    samples, bag = touched_ids.shape
    swap = [(0, 1), (1, 0)]
    rows_here = tab_rows // 2

    front = (
        touched_ids.T,
        bag_lengths.T,
        train_map.reshape(-1, LANES),
        row_var.reshape(-1, LANES),
        serve_map.reshape(-1, LANES),
    )
    grads = slot_grads.reshape(samples * bag, row_width)

    place = jnp.stack([rep, owner % 2]).astype(I32)
    slots, keys, head = route(jnp.zeros((1,), I32), *front)
    received = exchange(pack(slots, place, grads, table, moment, head))
    core = rep.reshape(1).astype(I32)
    new_rows, sums, places, acc, line, rounds = update(core, received, rows_here)
    rounds = rounds[0]
    one = jnp.ones((), I32)

    def more_sums(carry):
        k, acc = carry[0], carry[1]
        slots, _, head = route(k.reshape(1), *front)
        got = exchange(pack(slots, place, grads, table, moment, head))
        line = got[:, ROUND + 24].astype(F32) * 32.0 + got[:, ROUND + 25].astype(F32) - 1.0
        acc = more_rows(line, got, acc, True, True)
        return (k + 1, acc) + tuple(adam_again(core, received, acc))

    _, _, new_rows, sums, places = lax.while_loop(
        lambda c: c[0] < rounds, more_sums, (one, acc, new_rows, sums, places)
    )

    answer = exchange(reply(line, new_rows, sums))

    other_rows = lax.ppermute(new_rows, "rep", swap)
    other_places = lax.ppermute(places, "rep", swap)
    serving_table = place_rows(serving_old, new_rows, other_rows, places, other_places)

    def more_pooled(carry):
        k, acc = carry
        _, keys, head = route(k.reshape(1), *front)
        got = exchange(head)
        line = got[:, 0] * 32.0 + got[:, 1] - 1.0
        return (k + 1, more_rows(keys, exchange(reply(line, new_rows, sums)), acc, False, False))

    rounds, _ = lax.optimization_barrier((rounds, answer[0, 0, 0]))
    _, pooled = lax.while_loop(
        lambda c: c[0] < rounds,
        more_pooled,
        (one, jnp.zeros((4 * samples, row_width), F32)),
    )
    other = lax.ppermute(answer[:, ROUND:], "rep", swap)
    scores = score(keys, answer, pooled, w_first, w_second, w_score.reshape(1, -1))
    new_table, new_moment, new_var = finish(
        place, answer, other, table, moment, row_var.reshape(-1, LANES)
    )
    return (new_table, new_moment, new_var.reshape(-1), serving_table, scores.reshape(samples))


def solution(mesh):
    in_specs = (
        P(("shard", "rep"), None),
        P(("shard", "rep"), None),
        P(),
        P("shard"),
        P(("shard", "rep"), None, None),
        P("shard", None),
        P("shard", None),
        P("shard"),
        P("shard", None),
        P(),
        P(),
        P(),
    )
    out_specs = (
        P("shard", None),
        P("shard", None),
        P("shard"),
        P("shard", None),
        P(("shard", "rep")),
    )
    return jax.shard_map(
        per_device, mesh=mesh, in_specs=in_specs, out_specs=out_specs, check_vma=False
    )
```

```python
import functools

import jax
import jax.numpy as jnp
from jax import lax
from jax.experimental import pallas as pl
from jax.experimental.pallas import tpu as pltpu
from jax.sharding import PartitionSpec as P

beta_one = 0.9
beta_two = 0.999
learn_rate = 0.1
epsilon = 1e-06

ROUND = 64
DEVS = 128
LANES = 128
UNTOUCHED = 1e30
F32 = jnp.float32
BF16 = jnp.bfloat16
I32 = jnp.int32
ALL = ("shard", "rep")
SENT = ROUND + 32


def iota(shape, dim):
    return lax.broadcasted_iota(I32, shape, dim)


def one_hot(mask):
    return jnp.where(mask, 1.0, 0.0).astype(BF16)


def hot_rows(count, index):
    index = index.astype(jnp.int16)
    place = iota((count, index.shape[1]), 0).astype(jnp.int16)
    return jnp.where(place == index, jnp.bfloat16(1), jnp.bfloat16(0))


def route_kernel(
    round_ref, ids_ref, lengths_ref, map_ref, var_ref, serve_ref, slots_ref, keys_ref, row_ref
):
    bag, samples = ids_ref.shape
    step = 4
    wide = step * samples
    first = round_ref[0] * ROUND
    table = map_ref[...]
    high = (table >> 9).astype(F32).T
    low = ((table & 511) - 256).astype(F32).T
    parts = jnp.concatenate([high, low], axis=0).astype(BF16)
    upto = one_hot(iota((wide, wide), 0) <= iota((wide, wide), 1))
    ends = []
    total = jnp.zeros((1, samples), I32)
    for f in range(3):
        total = total + lengths_ref[f : f + 1, :]
        ends.append(total)
    sample = iota((1, samples), 1)
    seen = jnp.zeros((DEVS, 1), F32)
    layout = jnp.zeros((DEVS, 4 * ROUND), F32)
    for t in range(0, bag, step):
        ids = jnp.concatenate([ids_ref[t + u : t + u + 1, :] for u in range(step)], axis=1)
        keys = []
        for u in range(step):
            field = sum((jnp.where(e <= t + u, 1, 0) for e in ends), jnp.zeros((1, samples), I32))
            keys.append(field * samples + sample)
        key = jnp.concatenate(keys, axis=1) + 1
        hit = hot_rows(table.shape[0], ids >> 7)
        both = jnp.dot(parts, hit, preferred_element_type=F32)
        value = both[:LANES] * 512.0 + both[LANES:] + 256.0
        value = jnp.where(iota((LANES, wide), 0) == (ids & 127), value, 0.0)
        position = jnp.sum(value, axis=0, keepdims=True).astype(I32)
        owner = position >> 11
        stride = (position >> 6) & 31
        dest = (position & 63) * 2 + ((stride + owner) & 1)
        local = owner * 16 + (stride >> 1) + 1
        mine = iota((DEVS, wide), 0) == dest
        hot = one_hot(mine)
        running = jnp.dot(hot, upto, preferred_element_type=F32)
        rank = jnp.sum(jnp.where(mine, running + seen, 0.0), axis=0, keepdims=True)
        seen = seen + running[:, wide - 1 : wide]
        rank = rank.astype(I32) - 1 - first
        here = iota((ROUND, wide), 0) == rank
        columns = jnp.concatenate(
            [
                jnp.where(here, v.astype(F32), 0.0)
                for v in (local >> 5, key >> 5, local & 31, key & 31)
            ],
            axis=0,
        ).astype(BF16)
        layout = layout + lax.dot_general(
            hot, columns, (((1,), (1,)), ((), ())), preferred_element_type=F32
        )
        fits = (rank >= 0) & (rank < ROUND)
        slot = jnp.where(fits, dest * ROUND + rank, DEVS * ROUND)
        for u in range(step):
            slots_ref[t + u : t + u + 1, :] = slot[:, u * samples : (u + 1) * samples]
    keys_ref[...] = layout[:, :LANES] * 32.0 + layout[:, LANES:] - 1.0
    most = jnp.max(seen, axis=0, keepdims=True).astype(I32)
    rounds = ((most + ROUND - 1) // ROUND).astype(F32)
    var = var_ref[...]
    spot = (serve_ref[...] & (var.shape[0] * LANES - 1)).astype(F32)
    blank = jnp.zeros((ROUND, LANES), F32)
    sides = [var, pltpu.roll(var, ROUND, 1), spot, pltpu.roll(spot, ROUND, 1)]
    extra = jnp.concatenate([blank] + sides, axis=0).T
    coarse = extra.astype(BF16)
    fine = (extra - coarse.astype(F32)).astype(BF16)
    twice = one_hot((iota((DEVS, DEVS), 0) >> 1) == iota((DEVS, DEVS), 1))
    coarse = jnp.dot(twice, coarse, preferred_element_type=F32)
    fine = jnp.dot(twice, fine, preferred_element_type=F32)
    index = iota((DEVS, LANES), 1) < ROUND
    high = jnp.where(index, layout[:, :LANES], coarse)
    low = jnp.where(index, layout[:, LANES:], fine)
    row_ref[:, 0:1, :] = high.reshape(DEVS, 1, LANES)
    row_ref[:, 1:2, :] = low.reshape(DEVS, 1, LANES)
    row_ref[:, 2:8, :] = jnp.broadcast_to(rounds.reshape(1, 1, 1), (DEVS, 6, LANES))


def route(round_index, ids, lengths, train_map, var, serve):
    return pl.pallas_call(
        route_kernel,
        in_specs=[pl.BlockSpec(memory_space=pltpu.SMEM)]
        + [pl.BlockSpec(memory_space=pltpu.VMEM)] * 5,
        out_specs=[pl.BlockSpec(memory_space=pltpu.VMEM)] * 3,
        out_shape=(
            jax.ShapeDtypeStruct(ids.shape, I32),
            jax.ShapeDtypeStruct((DEVS, LANES), F32),
            jax.ShapeDtypeStruct((DEVS, 8, LANES), F32),
        ),
        name="route",
    )(round_index, ids, lengths, train_map, var, serve)


def pack_kernel(
    slots_ref,
    place_ref,
    grads_ref,
    table_from_ref,
    moment_from_ref,
    head_ref,
    out_ref,
    from_ref,
    to_ref,
    table_ref,
    moment_ref,
    sems,
):
    half, odd = place_ref[0], place_ref[1]
    mine = pl.ds(pl.multiple_of(half * table_ref.shape[0], 8), table_ref.shape[0])
    copies = [
        pltpu.make_async_copy(table_from_ref.at[mine], table_ref, sems.at[0]),
        pltpu.make_async_copy(moment_from_ref.at[mine], moment_ref, sems.at[1]),
    ]
    for copy in copies:
        copy.start()
    count = slots_ref.shape[0]
    bag = 32
    samples = count // bag
    block = 512

    def widen(i, carry):
        at = pl.multiple_of(i * block, block)
        from_ref[pl.ds(at, block), :] = grads_ref[pl.ds(at, block), :].astype(F32)
        to_ref[pl.ds(at * 2, block), :] = jnp.zeros((block, LANES), F32)
        to_ref[pl.ds(at * 2 + block, block), :] = jnp.zeros((block, LANES), F32)
        return carry

    def move(i, carry):
        first = (i & 3) * (bag * bag) + (i >> 2)
        for u in range(bag):
            slot = slots_ref[i * bag + u]
            to_ref[pl.ds(slot, 1), :] = from_ref[pl.ds(first + u * bag, 1), :]
        return carry

    def rows_of(ref, i):
        starts = [i * 4 + ((u + odd) & 1) * (LANES // 2) + u // 2 for u in range(8)]
        rows = [ref[pl.ds(start, 8, stride=LANES), :] for start in starts]
        return jnp.concatenate([r.reshape(1, 8, LANES) for r in rows], axis=0)

    def narrow(i, carry):
        at = pl.multiple_of(i * 8, 8)
        rows = to_ref[pl.ds(pl.multiple_of(i * block, block), block), :].astype(BF16)
        table = rows_of(table_ref, i)
        coarse = table.astype(BF16).astype(F32)
        state = jnp.concatenate([coarse, table - coarse], axis=1).astype(BF16)
        more = jnp.concatenate([rows_of(moment_ref, i), head_ref[pl.ds(at, 8)]], axis=1)
        out_ref[pl.ds(at, 8), 0:ROUND, :] = rows.reshape(8, ROUND, LANES)
        out_ref[pl.ds(at, 8), ROUND : ROUND + 16, :] = state
        out_ref[pl.ds(at, 8), ROUND + 16 : ROUND + 32, :] = more.astype(BF16)
        return carry

    lax.fori_loop(0, bag * samples // block, widen, 0)
    lax.fori_loop(0, count // bag, move, 0)
    for copy in copies:
        copy.wait()
    lax.fori_loop(0, DEVS // 8, narrow, 0)


def pack(slots, place, grads, table, moment, head):
    return pl.pallas_call(
        pack_kernel,
        in_specs=[pl.BlockSpec(memory_space=pltpu.SMEM)] * 2
        + [pl.BlockSpec(memory_space=pltpu.VMEM)]
        + [pl.BlockSpec(memory_space=pl.ANY)] * 2
        + [pl.BlockSpec(memory_space=pltpu.VMEM)],
        out_specs=pl.BlockSpec(memory_space=pltpu.VMEM),
        out_shape=jax.ShapeDtypeStruct((DEVS, SENT, LANES), BF16),
        scratch_shapes=[
            pltpu.VMEM(grads.shape, F32),
            pltpu.VMEM((DEVS * ROUND + 8, LANES), F32),
            pltpu.VMEM((table.shape[0] // 2, LANES), F32),
            pltpu.VMEM((table.shape[0] // 2, LANES), F32),
            pltpu.SemaphoreType.DMA((2,)),
        ],
        name="pack",
    )(slots.reshape(-1), place, grads, table, moment, head)


def pair_up(line, low):
    other = pltpu.roll(line, ROUND, 1)
    half = DEVS // 2
    left = (line if low else other)[:half]
    right = (other if low else line)[half:]
    return jnp.where(iota((half, LANES), 1) < ROUND, left, right).astype(I32)


def add_rows(index_ref, left_ref, right_ref, acc_ref, with_count):
    step = pl.program_id(0)
    turns = left_ref.shape[0] // PAIRS

    def add(i, carry):
        at = pl.ds(pl.multiple_of(i * PAIRS, PAIRS), PAIRS)
        pieces = pl.ds(pl.multiple_of((step * turns + i) * PAIRS, PAIRS), PAIRS)
        index = index_ref[pieces, :]
        index = jnp.concatenate([index[u : u + 1] for u in range(PAIRS)], axis=1)
        left, right = left_ref[at], right_ref[at]
        rows = jnp.concatenate([p[u] for u in range(PAIRS) for p in (left, right)], axis=0)
        if with_count:
            rows = jnp.concatenate([rows, jnp.ones_like(rows)], axis=1)
        hit = hot_rows(acc_ref.shape[0], index)
        acc_ref[...] = acc_ref[...] + jnp.dot(hit, rows, preferred_element_type=F32)
        return carry

    lax.fori_loop(0, turns, add, 0)


PAIRS = 32
STEPS = 2


def half_spec(second):
    count = DEVS // 2 // STEPS
    return pl.BlockSpec((count, ROUND, LANES), lambda i: (i + second * STEPS, 0, 0))


def whole(shape, at=None):
    place = at if at is not None else (0,) * len(shape)
    return pl.BlockSpec(shape, lambda i: place)


STATE_SPEC = whole((DEVS, 32, LANES), (0, ROUND // 32, 0))


def line_of(state_ref):
    high = state_ref[:, 24:25, :].astype(F32).reshape(DEVS, LANES)
    low = state_ref[:, 25:26, :].astype(F32).reshape(DEVS, LANES)
    return high * 32.0 + low - 1.0


def adam(core, state_ref, acc_ref, new_ref, sums_ref, spots_ref):
    def step(i, carry):
        at = pl.multiple_of(i * LANES, LANES)
        part = pl.ds(i * 16, 16)
        total = acc_ref[pl.ds(at, LANES), :]
        shape = (16, 8, LANES)
        grad = total[:, :LANES].reshape(shape)
        touched = (total[:, LANES:] > 0.5).reshape(shape)
        state = state_ref[part].astype(F32)
        table = state[:, 0:8, :] + state[:, 8:16, :]
        moment = state[:, 16:24, :]
        source = iota(shape, 0)
        within = iota(shape, 1)
        lane = iota(shape, 2)
        parity = (core + i * 8 + (source >> 1)) & 1
        own = parity * 16 + (source & 1) * 8 + within
        high = jnp.broadcast_to(state[:, 24:25, :], shape)
        extra = high + jnp.broadcast_to(state[:, 25:26, :], shape)
        var = jnp.sum(jnp.where(lane == ROUND + own, extra, 0.0), axis=2, keepdims=True)
        spot = jnp.sum(jnp.where(lane == ROUND + 32 + own, extra, 0.0), axis=2, keepdims=True)
        mean = jnp.sum(grad * grad, axis=2, keepdims=True) * (1.0 / LANES)
        new_var = beta_two * var + (1.0 - beta_two) * mean
        new_moment = beta_one * moment + (1.0 - beta_one) * grad
        new_table = table - learn_rate * new_moment / (jnp.sqrt(new_var) + epsilon)
        new_ref[pl.ds(at, LANES), :] = new_table.reshape(LANES, LANES).astype(BF16)
        sums_ref[part] = jnp.where(touched, grad, UNTOUCHED)
        spot = jnp.where(lane == source * 8 + within, jnp.where(touched, spot, 4096.0), 0.0)
        spot = jnp.sum(jnp.sum(spot, axis=0), axis=0, keepdims=True)
        spots_ref[pl.ds(i, 1), :] = spot.astype(I32)
        return carry

    lax.fori_loop(0, 8, step, 0)


def update_kernel(
    core_ref,
    state_ref,
    left_ref,
    right_ref,
    new_ref,
    sums_ref,
    spots_ref,
    acc_ref,
    line_ref,
    rounds_ref,
    index_ref,
):
    @pl.when(pl.program_id(0) == 0)
    def _():
        line = line_of(state_ref)
        line_ref[...] = line
        index_ref[...] = pair_up(line, True)
        rounds = state_ref[:, 26:27, :].astype(F32).reshape(DEVS, LANES)
        rounds_ref[0] = jnp.max(rounds).astype(I32)
        acc_ref[...] = jnp.zeros(acc_ref.shape, F32)

    add_rows(index_ref, left_ref, right_ref, acc_ref, True)

    @pl.when(pl.program_id(0) == STEPS - 1)
    def _():
        adam(core_ref[0], state_ref, acc_ref, new_ref, sums_ref, spots_ref)


def updated_shapes(rows):
    return (
        jax.ShapeDtypeStruct((rows, LANES), BF16),
        jax.ShapeDtypeStruct((DEVS, 8, LANES), F32),
        jax.ShapeDtypeStruct((8, LANES), I32),
    )


def updated_specs(rows):
    return [whole((rows, LANES)), whole((DEVS, 8, LANES)), whole((8, LANES))]


def update(core, received, rows):
    return pl.pallas_call(
        update_kernel,
        grid=(STEPS,),
        in_specs=[
            pl.BlockSpec(memory_space=pltpu.SMEM),
            STATE_SPEC,
            half_spec(0),
            half_spec(1),
        ],
        out_specs=updated_specs(rows)
        + [
            whole((rows, 2 * LANES)),
            whole((DEVS, LANES)),
            pl.BlockSpec(memory_space=pltpu.SMEM),
        ],
        out_shape=updated_shapes(rows)
        + (
            jax.ShapeDtypeStruct((rows, 2 * LANES), F32),
            jax.ShapeDtypeStruct((DEVS, LANES), F32),
            jax.ShapeDtypeStruct((1,), I32),
        ),
        scratch_shapes=[pltpu.VMEM((DEVS // 2, LANES), I32)],
        name="update",
    )(core, received, received, received)


def adam_kernel(core_ref, state_ref, acc_ref, new_ref, sums_ref, spots_ref):
    adam(core_ref[0], state_ref, acc_ref, new_ref, sums_ref, spots_ref)


def adam_again(core, received, acc):
    rows = acc.shape[0]
    return pl.pallas_call(
        adam_kernel,
        grid=(1,),
        in_specs=[pl.BlockSpec(memory_space=pltpu.SMEM), STATE_SPEC, whole(acc.shape)],
        out_specs=updated_specs(rows),
        out_shape=updated_shapes(rows),
        name="adam",
    )(core, received, acc)


def more_kernel(line_ref, left_ref, right_ref, start_ref, out_ref, index_ref, *, low, with_count):
    @pl.when(pl.program_id(0) == 0)
    def _():
        index_ref[...] = pair_up(line_ref[...], low)
        out_ref[...] = start_ref[...]

    add_rows(index_ref, left_ref, right_ref, out_ref, with_count)


def more_rows(line, rows, start, low, with_count):
    return pl.pallas_call(
        functools.partial(more_kernel, low=low, with_count=with_count),
        grid=(STEPS,),
        in_specs=[whole(line.shape), half_spec(0), half_spec(1), whole(start.shape)],
        out_specs=whole(start.shape),
        out_shape=jax.ShapeDtypeStruct(start.shape, F32),
        scratch_shapes=[pltpu.VMEM((DEVS // 2, LANES), I32)],
        name="more_rows",
    )(line, rows, rows, start)


def reply_kernel(line_ref, new_ref, sums_ref, out_ref, turned_ref, table_ref):
    turned_ref[...] = line_ref[...].T
    part = new_ref.shape[0] // 4
    table_ref[...] = jnp.concatenate(
        [new_ref[k * part : (k + 1) * part, :] for k in range(4)], axis=1
    )

    def look(i, carry):
        turned = pltpu.roll(turned_ref[0:ROUND, :], LANES - i * 32, 1).astype(I32)
        within = turned & (part - 1)
        hit = jnp.concatenate(
            [one_hot(iota((ROUND, part), 1) == within[:, u : u + 1]) for u in range(32)], axis=0
        )
        found = jnp.dot(hit, table_ref[...], preferred_element_type=F32)
        for u in range(32):
            piece = found[u * ROUND : (u + 1) * ROUND]
            row = jnp.broadcast_to(turned[:, u : u + 1], (ROUND, LANES))
            low = jnp.where(row < part, piece[:, :LANES], piece[:, LANES : 2 * LANES])
            high = jnp.where(
                row < 3 * part, piece[:, 2 * LANES : 3 * LANES], piece[:, 3 * LANES :]
            )
            out_ref[i * 32 + u, 0:ROUND, :] = jnp.where(row < 2 * part, low, high).astype(BF16)
        return carry

    out_ref[:, ROUND : ROUND + 8, :] = sums_ref[...].astype(BF16)
    lax.fori_loop(0, DEVS // 32, look, 0)


def reply(line, new_rows, sums):
    return pl.pallas_call(
        reply_kernel,
        in_specs=[pl.BlockSpec(memory_space=pltpu.VMEM)] * 3,
        out_specs=pl.BlockSpec(memory_space=pltpu.VMEM),
        out_shape=jax.ShapeDtypeStruct((DEVS, ROUND + 8, LANES), BF16),
        scratch_shapes=[
            pltpu.VMEM((DEVS, LANES), F32),
            pltpu.VMEM((new_rows.shape[0] // 4, 4 * LANES), BF16),
        ],
        name="reply",
    )(line, new_rows, sums)


def score_kernel(
    keys_ref,
    left_ref,
    right_ref,
    start_ref,
    first_ref,
    second_ref,
    score_ref,
    out_ref,
    index_ref,
    acc_ref,
):
    @pl.when(pl.program_id(0) == 0)
    def _():
        index_ref[...] = pair_up(keys_ref[...], False)
        acc_ref[...] = start_ref[...]

    add_rows(index_ref, left_ref, right_ref, acc_ref, False)

    @pl.when(pl.program_id(0) == STEPS - 1)
    def _():
        samples = out_ref.shape[1]
        pooled = jnp.concatenate(
            [acc_ref[f * samples : (f + 1) * samples, :] for f in range(4)], axis=1
        ).astype(BF16)
        hidden = jnp.dot(pooled, first_ref[...], preferred_element_type=F32)
        hidden = jnp.maximum(hidden, 0.0).astype(BF16)
        hidden = jnp.dot(hidden, second_ref[...], preferred_element_type=F32)
        hidden = jnp.maximum(hidden, 0.0).astype(BF16)
        weights = jnp.broadcast_to(score_ref[...], (16, score_ref.shape[1]))
        scores = lax.dot_general(
            weights, hidden, (((1,), (1,)), ((), ())), preferred_element_type=F32
        )
        out_ref[...] = scores[0:1, :]


def score(keys, rows, start, w_first, w_second, w_score):
    samples = start.shape[0] // 4
    return pl.pallas_call(
        score_kernel,
        grid=(STEPS,),
        in_specs=[whole(keys.shape), half_spec(0), half_spec(1), whole(start.shape)]
        + [whole(w.shape) for w in (w_first, w_second, w_score)],
        out_specs=whole((1, samples)),
        out_shape=jax.ShapeDtypeStruct((1, samples), F32),
        scratch_shapes=[
            pltpu.VMEM((DEVS // 2, LANES), I32),
            pltpu.VMEM(start.shape, F32),
        ],
        name="score",
    )(keys, rows, rows, start, w_first, w_second, w_score)


def finish_kernel(
    place_ref,
    own_ref,
    other_ref,
    table_ref,
    moment_ref,
    var_ref,
    new_table_ref,
    new_moment_ref,
    new_var_ref,
    sums_ref,
):
    half, odd = place_ref[0], place_ref[1]
    step = pl.program_id(0)

    @pl.when(step == 0)
    def _():
        sums_ref[half] = own_ref[...].astype(F32).reshape(sums_ref.shape[1:])
        sums_ref[1 - half] = other_ref[...].astype(F32).reshape(sums_ref.shape[1:])

    eye = iota((LANES, LANES), 0) == iota((LANES, LANES), 1)
    for u in range(4):
        block = step * 4 + u
        at = pl.ds(u * LANES, LANES)
        sides = []
        for parity in range(2):
            first = ((parity + odd) & 1) * 8 + (block & 7)
            sides.append(sums_ref[block >> 3, pl.ds(first, LANES // 2, stride=16), :])
        grad = jnp.concatenate(sides, axis=0)
        touched = grad < 0.5 * UNTOUCHED
        var = jnp.broadcast_to(var_ref[pl.ds(block, 1), :], (LANES, LANES))
        var = jnp.sum(jnp.where(eye, var, 0.0), axis=1, keepdims=True)
        known = jnp.where(touched, grad, 0.0)
        mean = jnp.sum(known * known, axis=1, keepdims=True) * (1.0 / LANES)
        new_var = jnp.where(touched, beta_two * var + (1.0 - beta_two) * mean, var)
        table, moment = table_ref[at, :], moment_ref[at, :]
        new_moment = jnp.where(touched, beta_one * moment + (1.0 - beta_one) * grad, moment)
        new_table = table - learn_rate * new_moment / (jnp.sqrt(new_var) + epsilon)
        new_moment_ref[at, :] = new_moment
        new_table_ref[at, :] = jnp.where(touched, new_table, table)
        line = jnp.sum(jnp.where(eye, new_var, 0.0), axis=0, keepdims=True)
        new_var_ref[pl.ds(block, 1), :] = line


def finish(place, answer, other, table, moment, var):
    rows = pl.BlockSpec((4 * LANES, LANES), lambda i: (i, 0))
    return pl.pallas_call(
        finish_kernel,
        grid=(table.shape[0] // (4 * LANES),),
        in_specs=[
            pl.BlockSpec(memory_space=pltpu.SMEM),
            whole((DEVS, 8, LANES), (0, ROUND // 8, 0)),
            whole(other.shape),
            rows,
            rows,
            whole(var.shape),
        ],
        out_specs=[rows, rows, whole(var.shape)],
        out_shape=tuple(jax.ShapeDtypeStruct(a.shape, F32) for a in (table, moment, var)),
        scratch_shapes=[pltpu.VMEM((2, table.shape[0] // 2, LANES), F32)],
        name="finish",
    )(place, answer, other, table, moment, var)


def exchange(value):
    return lax.all_to_all(value, ALL, 0, 0, tiled=True)


def place_kernel(old_ref, own_ref, other_ref, own_at_ref, other_at_ref, out_ref):
    block = 512

    def place(i, carry):
        at = pl.ds(pl.multiple_of(i * block, block), block)
        total = jnp.zeros((block, 2 * LANES), F32)
        for at_ref, rows_ref in ((own_at_ref, own_ref), (other_at_ref, other_ref)):
            spots = at_ref[...] - i * block
            spots = jnp.where((spots >= 0) & (spots < block), spots, -1)
            spots = jnp.concatenate([spots[u : u + 1] for u in range(8)], axis=1)
            rows = rows_ref[...]
            rows = jnp.concatenate([rows, jnp.ones_like(rows)], axis=1)
            total = total + jnp.dot(hot_rows(block, spots), rows, preferred_element_type=F32)
        fresh = total[:, :LANES].astype(BF16).astype(F32)
        old = old_ref[at, :].astype(F32)
        out_ref[at, :] = jnp.where(total[:, LANES:] > 0.5, fresh, old).astype(BF16)
        return carry

    lax.fori_loop(0, old_ref.shape[0] // block, place, 0)


def place_rows(old, own, other, own_at, other_at):
    return pl.pallas_call(
        place_kernel,
        in_specs=[pl.BlockSpec(memory_space=pltpu.VMEM)] * 5,
        out_specs=pl.BlockSpec(memory_space=pltpu.VMEM),
        out_shape=jax.ShapeDtypeStruct(old.shape, BF16),
        name="place",
    )(old, own, other, own_at, other_at)


def per_device(
    touched_ids,
    bag_lengths,
    train_map,
    serve_map,
    slot_grads,
    table,
    moment,
    row_var,
    serving_old,
    w_first,
    w_second,
    w_score,
):
    owners = lax.axis_size("shard")
    owner = lax.axis_index("shard")
    rep = lax.axis_index("rep")
    tab_rows, row_width = table.shape
    samples, bag = touched_ids.shape
    swap = [(0, 1), (1, 0)]
    rows_here = tab_rows // 2

    front = (
        touched_ids.T,
        bag_lengths.T,
        train_map.reshape(-1, LANES),
        row_var.reshape(-1, LANES),
        serve_map.reshape(-1, LANES),
    )
    grads = slot_grads.reshape(samples * bag, row_width)

    place = jnp.stack([rep, owner % 2]).astype(I32)
    slots, keys, head = route(jnp.zeros((1,), I32), *front)
    received = exchange(pack(slots, place, grads, table, moment, head))
    core = rep.reshape(1).astype(I32)
    new_rows, sums, places, acc, line, rounds = update(core, received, rows_here)
    rounds = rounds[0]
    one = jnp.ones((), I32)

    def more_sums(carry):
        k, acc = carry[0], carry[1]
        slots, _, head = route(k.reshape(1), *front)
        got = exchange(pack(slots, place, grads, table, moment, head))
        line = got[:, ROUND + 24].astype(F32) * 32.0 + got[:, ROUND + 25].astype(F32) - 1.0
        acc = more_rows(line, got, acc, True, True)
        return (k + 1, acc) + tuple(adam_again(core, received, acc))

    _, _, new_rows, sums, places = lax.while_loop(
        lambda c: c[0] < rounds, more_sums, (one, acc, new_rows, sums, places)
    )

    answer = exchange(reply(line, new_rows, sums))

    other_rows = lax.ppermute(new_rows, "rep", swap)
    other_places = lax.ppermute(places, "rep", swap)
    serving_table = place_rows(serving_old, new_rows, other_rows, places, other_places)

    def more_pooled(carry):
        k, acc = carry
        _, keys, head = route(k.reshape(1), *front)
        got = exchange(head)
        line = got[:, 0] * 32.0 + got[:, 1] - 1.0
        return (k + 1, more_rows(keys, exchange(reply(line, new_rows, sums)), acc, False, False))

    rounds, _ = lax.optimization_barrier((rounds, answer[0, 0, 0]))
    _, pooled = lax.while_loop(
        lambda c: c[0] < rounds,
        more_pooled,
        (one, jnp.zeros((4 * samples, row_width), F32)),
    )
    other = lax.ppermute(answer[:, ROUND:], "rep", swap)
    scores = score(keys, answer, pooled, w_first, w_second, w_score.reshape(1, -1))
    new_table, new_moment, new_var = finish(
        place, answer, other, table, moment, row_var.reshape(-1, LANES)
    )
    return (new_table, new_moment, new_var.reshape(-1), serving_table, scores.reshape(samples))


def solution(mesh):
    in_specs = (
        P(("shard", "rep"), None),
        P(("shard", "rep"), None),
        P(),
        P("shard"),
        P(("shard", "rep"), None, None),
        P("shard", None),
        P("shard", None),
        P("shard"),
        P("shard", None),
        P(),
        P(),
        P(),
    )
    out_specs = (
        P("shard", None),
        P("shard", None),
        P("shard"),
        P("shard", None),
        P(("shard", "rep")),
    )
    return jax.shard_map(
        per_device, mesh=mesh, in_specs=in_specs, out_specs=out_specs, check_vma=False
    )
```
